256 devices in a mesh: chain: 8 (over y, core), cols: 32 (over x, z).
Axes of the slice: x: 4, y: 4, z: 8, core: 2. Of those that a mesh axis runs over, the one named last changes fastest.
Arguments:
- factor: float32 [4608, 4608], P(('chain', 'cols')), may hold values from -2 to 2, as said below
- right_side: float32 [4608, 16384], P('chain', 'cols'), may hold values from -6 to 6
- occ_order: int32 [64], replicated, may hold values from 0 to 63, each once
- cabs_order: int32 [256], replicated, may hold values from 0 to 255, each once
Outputs:
- fitted: float32 [64, 256, 4608], P('cols', None, 'chain')
The draws below stay inside these ranges and needn't reach their ends.
Inputs may be any that keep to these rules, and one draw needn't show every extreme that they name: factor is lower triangular: zero above the diagonal, its diagonal between 1 and 2.
All inputs are finite; a program needn't handle non-finite values.
Results may differ from the reference program's by a relative error of at most 0.00017.
Values sent between devices are 32-bit elements; how exact they have to be, the bound alone decides.
No kernel may reach another device: no remote copies, remote signals or barrier semaphores. Data moves between devices by JAX's collectives and lax.ppermute only.
A program may use at most 128 MiB of HBM per device.

```python
import math
import jax
import jax.numpy as jnp

NAUX = 4608
CABSW = 256
OCCW = 64
NCOL = 16384


def draw_factor(key, part):
    key_off = jax.random.fold_in(key, 11)
    key_diag = jax.random.fold_in(key, 12)
    off_diag = jnp.clip(jax.random.normal(key_off, (NAUX, NAUX), jnp.float32), -6.0, 6.0)
    off_diag = jnp.tril(off_diag * (2.5 / math.sqrt(NAUX)), -1)
    diag_vals = jax.random.uniform(key_diag, (NAUX,), jnp.float32, 1.0, 2.0)
    return off_diag + jnp.diag(diag_vals)


def block_scale(stream_key, shape, split, low, high):
    level, own = 1.0, jax.random.fold_in(stream_key, 6)
    for position, parts in split:
        steps = jnp.exp(jax.random.uniform(jax.random.fold_in(own, position), (parts,), jnp.float32, low / len(split), high / len(split)))
        level = level * jnp.repeat(steps, shape[position] // parts).reshape([-1 if axis == position else 1 for axis in range(len(shape))])
    return level


def gaussian(own_key, shape, width, bound, cuts=(), kind=jnp.bfloat16):
    drawn = width * jax.random.normal(own_key, shape, jnp.float32)
    if cuts:
        drawn = drawn * block_scale(own_key, shape, cuts, -0.22, 0.18)
    return jnp.clip(drawn, -bound, bound).astype(kind)


def setup_inputs(seed: int = 0) -> dict:
    keys = jax.random.split(jax.random.key(seed), 5)
    factor = draw_factor(jax.random.fold_in(keys[4], 71), 0)
    right_side = gaussian(keys[1], (NAUX, NCOL), 1.0, 6.0, ((0, 8), (1, 32)), jnp.float32)
    occ_order = jax.random.permutation(keys[2], OCCW).astype(jnp.int32)
    cabs_order = jax.random.permutation(keys[3], CABSW).astype(jnp.int32)
    return {"factor": factor, "right_side": right_side, "occ_order": occ_order, "cabs_order": cabs_order}


def reference(factor, right_side, occ_order, cabs_order):
    solution = jax.scipy.linalg.solve_triangular(factor, right_side, lower=True)
    grid = solution.reshape(NAUX, CABSW, OCCW)
    grid = jnp.take(grid, cabs_order.astype(jnp.int32), axis=1)
    grid = jnp.take(grid, occ_order.astype(jnp.int32), axis=2)
    return jnp.transpose(grid, (2, 1, 0))
```

```python
import functools
import jax
import jax.numpy as jnp
from jax import lax
from jax.experimental import pallas as pl
from jax.experimental.pallas import tpu as pltpu
from jax.sharding import Mesh, PartitionSpec as P

HI = lax.Precision.HIGHEST
LANES = 128


def full_dot(left, right):
    return jnp.dot(left, right, precision=HI, preferred_element_type=jnp.float32)


def halves(value):
    high = value.astype(jnp.bfloat16)
    return high, (value - high.astype(jnp.float32)).astype(jnp.bfloat16)


def three_dot(left, right):
    lh, ll = left
    rh, rl = right
    dot = functools.partial(jnp.dot, preferred_element_type=jnp.float32)
    return dot(lh, rh) + (dot(lh, rl) + dot(ll, rh))


def invert_kernel(rows, pieces, pad_rows, tiles, g_ref, o_ref, a_ref):
    per = rows // pieces
    wide = 640
    blocks = wide // LANES
    for tile in range(tiles):
        for row in range(per):
            a_ref[tile, pl.ds(row, pieces, stride=per), :] = g_ref[
                pl.ds(row * tiles + tile, pieces, stride=pad_rows), :
            ]
    extra = wide - rows
    r0 = lax.broadcasted_iota(jnp.int32, (extra, LANES), 0)
    c0 = lax.broadcasted_iota(jnp.int32, (extra, LANES), 1)
    for tile in range(blocks - 1):
        a_ref[tile, rows:wide, :] = jnp.zeros((extra, LANES), jnp.float32)
    a_ref[blocks - 1, rows:wide, :] = jnp.where(c0 == r0 + (LANES - extra), 1.0, 0.0)
    ri = lax.broadcasted_iota(jnp.int32, (LANES, LANES), 0)
    ci = lax.broadcasted_iota(jnp.int32, (LANES, LANES), 1)

    def block(i, j):
        return a_ref[j, i * LANES : (i + 1) * LANES, :]

    inv = [jnp.where(ri == ci, 1.0 / jnp.where(ri == ci, block(i, i), 1.0), 0.0) for i in range(blocks)]
    size = 1
    while size < LANES:
        take = (ri // (2 * size) == ci // (2 * size)) & (ri // size == ci // size + 1)
        mids = [full_dot(jnp.where(take, block(i, i), 0.0), inv[i]) for i in range(blocks)]
        inv = [inv[i] - full_dot(inv[i], mids[i]) for i in range(blocks)]
        size *= 2
    for i in range(blocks):
        for j in range(blocks):
            last = min((i + 1) * LANES, rows)
            if j > i:
                o_ref[i * LANES : last, j * LANES : (j + 1) * LANES] = jnp.zeros((last - i * LANES, LANES), jnp.float32)
    done = [[None] * blocks for _ in range(blocks)]
    for i in range(blocks):
        done[i][i] = inv[i]
        last = min((i + 1) * LANES, rows)
        for j in range(i):
            total = full_dot(block(i, j), done[j][j])
            for k in range(j + 1, i):
                total = total + full_dot(block(i, k), done[k][j])
            done[i][j] = -full_dot(inv[i], total)
        for j in range(i + 1):
            o_ref[i * LANES : last, j * LANES : (j + 1) * LANES] = done[i][j][: last - i * LANES]
    for tile in range(blocks, tiles):
        o_ref[:, tile * LANES : (tile + 1) * LANES] = a_ref[tile, :rows, :]


def stage_kernel(rows, pieces, pad_rows, tiles, updates, core_ref, e_ref, r_ref, *refs):
    per = rows // pieces
    wide = 640
    xs = refs[:updates]
    own = refs[updates : 2 * updates]
    other = refs[2 * updates : 3 * updates]
    r_out, x_out, l_ref, s_ref, u_ref = refs[3 * updates :]
    core = core_ref[0]
    s_ref[0 : 2 * rows, :] = r_ref[...]
    s_ref[2 * rows : 2 * rows + 64, :] = jnp.zeros((64, LANES), jnp.float32)
    for which in range(updates):
        x = halves(xs[which][...])
        for source, base in ((own[which], core * rows), (other[which], (1 - core) * rows)):
            for tile in range(tiles):
                for row in range(per):
                    l_ref[row * pieces : (row + 1) * pieces, tile * LANES : (tile + 1) * LANES] = source[
                        pl.ds(row * tiles + tile, pieces, stride=pad_rows), :
                    ]
            u_ref[...] = three_dot(halves(l_ref[...]), x)
            for row in range(per):
                here = pl.ds(base + row, pieces, stride=per)
                s_ref[here, :] = s_ref[here, :] - u_ref[row * pieces : (row + 1) * pieces, :]
    r_out[...] = s_ref[0 : 2 * rows, :]
    first = three_dot(halves(e_ref[0, :, 0:wide]), halves(s_ref[0:wide, :]))
    x_out[0:rows, :] = first
    first_wide = jnp.concatenate([first, jnp.zeros((wide - rows, LANES), jnp.float32)], axis=0)
    s_ref[rows : 2 * rows, :] = s_ref[rows : 2 * rows, :] - three_dot(
        halves(e_ref[1, :, wide : 2 * wide]), halves(first_wide)
    )
    x_out[rows : 2 * rows, :] = three_dot(halves(e_ref[1, :, 0:wide]), halves(s_ref[rows : rows + wide, :]))


def per_device(factor, right_side, occ_order, cabs_order):
    planes, cores = lax.axis_size("y"), lax.axis_size("core")
    plane, core = lax.axis_index("y"), lax.axis_index("core")
    pieces = lax.axis_size("x") * lax.axis_size("z")
    per, aux = factor.shape
    rows = per * pieces
    span = cores * rows
    occ_total, cabs_total = occ_order.shape[0], cabs_order.shape[0]
    cabs_local = right_side.shape[1] // occ_total
    vmem = pltpu.CompilerParams(vmem_limit_bytes=56 * 1024 * 1024)

    slots = occ_order.reshape(pieces, cores).T.reshape(occ_total)
    pick = (jnp.arange(cabs_local, dtype=jnp.int32)[None, :] * occ_total + slots[:, None]).reshape(-1, 1)
    spread = (pick == jnp.arange(right_side.shape[1], dtype=jnp.int32)[None, :]).astype(jnp.float32)
    sent = lax.dot_general(spread, right_side, (((1,), (1,)), ((), ())), precision=HI, preferred_element_type=jnp.float32)
    sent = sent.reshape(occ_total, cabs_local, rows)
    got = lax.all_to_all(sent, ("core", "x", "z"), 0, 0, tiled=True).reshape(cores, cabs_total, rows)
    place = (jnp.arange(cabs_total, dtype=jnp.int32)[:, None] == cabs_order[None, :]).astype(jnp.float32)
    residual = lax.dot_general(got, place, (((1,), (0,)), ((), ())), precision=HI, preferred_element_type=jnp.float32)
    residual = residual.reshape(span, cabs_total)

    diag = lax.dynamic_slice_in_dim(factor, plane * span, span, 1)
    low, high = diag[:, :rows], diag[:, rows:]
    gap = jnp.zeros((per, 640 - rows), jnp.float32)
    diag = jnp.concatenate([jnp.where(core == 0, low, high), gap, low, gap], axis=1)
    tiles = diag.shape[1] // LANES
    pad_rows = (per * tiles + 7) // 8 * 8
    piece = jnp.pad(diag.reshape(per * tiles, LANES), ((0, pad_rows - per * tiles), (0, 0)))
    zs, xs = lax.axis_size("z"), lax.axis_size("x")
    near = lax.all_to_all(jnp.broadcast_to(piece[None], (zs, pad_rows, LANES)), "z", 0, 0, tiled=True)
    near = near.reshape(1, zs * pad_rows, LANES)
    far = lax.all_to_all(jnp.broadcast_to(near, (xs, zs * pad_rows, LANES)), "x", 0, 0, tiled=True)
    far = far.reshape(pieces * pad_rows, LANES)
    mine = pl.pallas_call(
        functools.partial(invert_kernel, rows, pieces, pad_rows, tiles),
        out_shape=jax.ShapeDtypeStruct((rows, tiles * LANES), jnp.float32),
        scratch_shapes=[pltpu.VMEM((tiles, 640, LANES), jnp.float32)],
        compiler_params=vmem,
        name="invert",
    )(far)
    theirs = lax.ppermute(mine, "core", [(0, 1), (1, 0)])
    pair = jnp.where(core == 0, jnp.stack([mine, theirs]), jnp.stack([theirs, mine]))

    ltiles = span // LANES
    lpad = (per * ltiles + 7) // 8 * 8
    flat = factor.reshape(per, planes, ltiles, LANES).transpose(1, 0, 2, 3).reshape(planes, per * ltiles, LANES)
    flat = jnp.pad(flat, ((0, 0), (0, lpad - per * ltiles), (0, 0)))
    flat = flat.reshape(planes * lpad, LANES)
    whole = lax.all_gather(flat, ("x", "z"), axis=0, tiled=True)
    partner = lax.ppermute(whole, "core", [(0, 1), (1, 0)])
    whole = whole.reshape(pieces, planes, lpad, LANES)
    partner = partner.reshape(pieces, planes, lpad, LANES)
    core_arg = core.reshape(1).astype(jnp.int32)

    def stage(state, arrived):
        updates = len(arrived)
        shape = jax.ShapeDtypeStruct((span, LANES), jnp.float32)

        def at(step):
            return pl.BlockSpec((pieces, 1, lpad, LANES), lambda i: (0, step, 0, 0), pipeline_mode=pl.Buffered(1))

        def body(*refs):
            head = refs[: 3 + updates]
            mats = [ref.reshape(pieces * lpad, LANES) for ref in refs[3 + updates : 3 + 3 * updates]]
            stage_kernel(rows, pieces, lpad, ltiles, updates, *head, *mats, *refs[3 + 3 * updates :])

        specs = [
            pl.BlockSpec(memory_space=pltpu.SMEM),
            pl.BlockSpec((cores, rows, tiles * LANES), lambda i: (0, 0, 0), pipeline_mode=pl.Buffered(1)),
            pl.BlockSpec((span, LANES), lambda i: (0, 0), pipeline_mode=pl.Buffered(1)),
        ]
        specs += [pl.BlockSpec((span, LANES), lambda i: (0, 0), pipeline_mode=pl.Buffered(1))] * updates
        specs += [at(step) for _, step in arrived] * 2
        out_spec = pl.BlockSpec((span, LANES), lambda i: (0, 0), pipeline_mode=pl.Buffered(1))
        return pl.pallas_call(
            body,
            out_shape=(shape, shape),
            grid=(1,),
            in_specs=specs,
            out_specs=(out_spec, out_spec),
            scratch_shapes=[
                pltpu.VMEM((rows, span), jnp.float32),
                pltpu.VMEM((span + 64, LANES), jnp.float32),
                pltpu.VMEM((rows, LANES), jnp.float32),
            ],
            compiler_params=vmem,
            cost_estimate=pl.CostEstimate(flops=10_000_000_000, bytes_accessed=1_000_000, transcendentals=0),
            name=f"stage{updates}",
        )(core_arg, pair, state, *[x for x, _ in arrived], *[whole] * updates, *[partner] * updates)

    def send(value, pairs):
        return lax.ppermute(value, "y", pairs)

    chunks = []
    for start in range(0, cabs_total, LANES):
        state = residual[:, start : start + LANES]
        state, x0 = stage(state, [])
        to1, to3 = send(x0, [(0, 1)]), send(x0, [(0, 3)])
        seen = to1 + to3
        state, x1 = stage(state, [(seen, 0)])
        a2, b2 = send(seen, [(3, 2)]), send(x1, [(1, 2)])
        b3 = send(x1, [(1, 3)])
        state, x2 = stage(state, [(a2, 0), (b2, 1)])
        c3 = send(x2, [(2, 3)])
        state, x3 = stage(state, [(b3, 1), (c3, 2)])
        x = jnp.where(plane == 0, x0, jnp.where(plane == 1, x1, jnp.where(plane == 2, x2, x3)))
        chunks.append(x)
    solved = jnp.concatenate([x.T for x in chunks], axis=0)
    keep = jnp.where(core == 0, solved[:, :rows], solved[:, rows:])
    give = jnp.where(core == 0, solved[:, rows:], solved[:, :rows])
    came = lax.ppermute(give, "core", [(0, 1), (1, 0)])
    return jnp.where(core == 0, jnp.stack([keep, came]), jnp.stack([came, keep]))


def solution(mesh):
    grid = Mesh(mesh.devices.reshape(4, 2, 4, 8), ("y", "core", "x", "z"))
    in_specs = (P(("y", "core", "x", "z"), None), P(("y", "core"), ("x", "z")), P(), P())
    out_specs = P(("x", "z"), None, ("y", "core"))
    return jax.shard_map(per_device, mesh=grid, in_specs=in_specs, out_specs=out_specs, check_vma=False)
```

```python
import functools
import jax
import jax.numpy as jnp
from jax import lax
from jax.experimental import pallas as pl
from jax.experimental.pallas import tpu as pltpu
from jax.sharding import Mesh, PartitionSpec as P

HI = lax.Precision.HIGHEST
LANES = 128


def full_dot(left, right):
    return jnp.dot(left, right, precision=HI, preferred_element_type=jnp.float32)


def halves(value):
    high = value.astype(jnp.bfloat16)
    return high, (value - high.astype(jnp.float32)).astype(jnp.bfloat16)


def three_dot(left, right):
    lh, ll = left
    rh, rl = right
    dot = functools.partial(jnp.dot, preferred_element_type=jnp.float32)
    return dot(lh, rh) + (dot(lh, rl) + dot(ll, rh))


def invert_kernel(rows, pieces, pad_rows, tiles, g_ref, o_ref, a_ref, m_ref):
    per = rows // pieces
    wide = 640
    blocks = wide // LANES
    for tile in range(tiles):
        for row in range(per):
            a_ref[tile, pl.ds(row, pieces, stride=per), :] = g_ref[
                pl.ds(row * tiles + tile, pieces, stride=pad_rows), :
            ]
    extra = wide - rows
    r0 = lax.broadcasted_iota(jnp.int32, (extra, LANES), 0)
    c0 = lax.broadcasted_iota(jnp.int32, (extra, LANES), 1)
    for tile in range(blocks - 1):
        a_ref[tile, rows:wide, :] = jnp.zeros((extra, LANES), jnp.float32)
    a_ref[blocks - 1, rows:wide, :] = jnp.where(c0 == r0 + (LANES - extra), 1.0, 0.0)
    ri = lax.broadcasted_iota(jnp.int32, (LANES, LANES), 0)
    ci = lax.broadcasted_iota(jnp.int32, (LANES, LANES), 1)

    def block(i, j):
        return a_ref[j, i * LANES : (i + 1) * LANES, :]

    for i in range(blocks):
        m_ref[i] = jnp.where(ri == ci, 1.0 / jnp.where(ri == ci, block(i, i), 1.0), 0.0)

    def double(level, carry):
        rb, cb = ri >> level, ci >> level
        take = (rb >> 1 == cb >> 1) & (rb == cb + 1)
        mids = [full_dot(jnp.where(take, block(i, i), 0.0), m_ref[i]) for i in range(blocks)]
        news = [m_ref[i] - full_dot(m_ref[i], mids[i]) for i in range(blocks)]
        for i in range(blocks):
            m_ref[i] = news[i]
        return carry

    lax.fori_loop(0, 7, double, 0)
    inv = [m_ref[i] for i in range(blocks)]
    for i in range(blocks):
        for j in range(blocks):
            last = min((i + 1) * LANES, rows)
            if j > i:
                o_ref[i * LANES : last, j * LANES : (j + 1) * LANES] = jnp.zeros((last - i * LANES, LANES), jnp.float32)
    done = [[None] * blocks for _ in range(blocks)]
    for i in range(blocks):
        done[i][i] = inv[i]
        last = min((i + 1) * LANES, rows)
        for j in range(i):
            total = full_dot(block(i, j), done[j][j])
            for k in range(j + 1, i):
                total = total + full_dot(block(i, k), done[k][j])
            done[i][j] = -full_dot(inv[i], total)
        for j in range(i + 1):
            o_ref[i * LANES : last, j * LANES : (j + 1) * LANES] = done[i][j][: last - i * LANES]
    for tile in range(blocks, tiles):
        o_ref[:, tile * LANES : (tile + 1) * LANES] = a_ref[tile, :rows, :]


def order_kernel(rows, pieces, pad_rows, tiles, core_ref, own_ref, other_ref, o_ref, s_ref):
    per = rows // pieces

    def copy(source, base):
        base = pl.multiple_of(base, rows)
        for tile in range(tiles):

            def move(row, carry):
                s_ref[pl.ds(row, pieces, stride=per), :] = source[
                    pl.ds(row * tiles + tile, pieces, stride=pad_rows), :
                ]
                return carry

            lax.fori_loop(0, per, move, 0, unroll=3)
            high, low = halves(s_ref[...])
            o_ref[0, pl.ds(base, rows), tile * LANES : (tile + 1) * LANES] = high
            o_ref[1, pl.ds(base, rows), tile * LANES : (tile + 1) * LANES] = low

    core = core_ref[0]
    copy(own_ref, core * rows)
    copy(other_ref, (1 - core) * rows)


def pack_kernel(core_ref, own_ref, other_ref, o_ref):
    core = core_ref[0]
    rows = own_ref.shape[0]
    for start in range(0, rows, 192):
        here = slice(start, start + 192)
        high, low = halves(own_ref[here, :])
        o_ref[core, 0, here, :] = high
        o_ref[core, 1, here, :] = low
        high, low = halves(other_ref[here, :])
        o_ref[1 - core, 0, here, :] = high
        o_ref[1 - core, 1, here, :] = low


def subtract(state, l_ref, x_ref, rows):
    x = halves(x_ref[...])
    step = rows // 2

    def part(index, carry):
        here = pl.ds(pl.multiple_of(index * step, step), step)
        state[here, :] = state[here, :] - three_dot((l_ref[0, here, :], l_ref[1, here, :]), x)
        return carry

    lax.fori_loop(0, 4, part, 0)


def solve(state, e_ref, x_ref, rows):
    wide = 640
    step = rows // 3

    def product(which, offset, right, put):
        def part(index, carry):
            here = pl.ds(pl.multiple_of(index * step, step), step)
            left = e_ref[which, 0, here, offset : offset + wide], e_ref[which, 1, here, offset : offset + wide]
            put(index, three_dot(left, right))
            return carry

        lax.fori_loop(0, 3, part, 0)

    def put_first(index, value):
        x_ref[pl.ds(pl.multiple_of(index * step, step), step), :] = value

    def put_second(index, value):
        x_ref[pl.ds(pl.multiple_of(rows + index * step, step), step), :] = value

    def take(index, value):
        here = pl.ds(pl.multiple_of(rows + index * step, step), step)
        state[here, :] = state[here, :] - value

    product(0, 0, halves(state[0:wide, :]), put_first)
    padded = jnp.concatenate([x_ref[0:rows, :], jnp.zeros((wide - rows, LANES), jnp.float32)], axis=0)
    product(1, wide, halves(padded), take)
    product(1, 0, halves(state[rows : rows + wide, :]), put_second)


def load_state(state, r_ref, span):
    state[0:span, :] = r_ref[...]
    state[span:, :] = jnp.zeros((state.shape[0] - span, LANES), jnp.float32)


def stage0_kernel(rows, plane_ref, e_ref, r_ref, x_ref, state):
    @pl.when(plane_ref[0] == 0)
    def _():
        load_state(state, r_ref, 2 * rows)
        solve(state, e_ref, x_ref, rows)

    @pl.when(plane_ref[0] != 0)
    def _():
        x_ref[...] = jnp.zeros_like(x_ref)


def stage1_kernel(rows, plane_ref, e_ref, a_ref, r_ref, seen_ref, r_out, x_ref, state):
    plane = plane_ref[0]
    load_state(state, r_ref, 2 * rows)

    @pl.when((plane == 1) | (plane == 3))
    def _():
        subtract(state, a_ref, seen_ref, rows)

    r_out[...] = state[0 : 2 * rows, :]

    @pl.when(plane == 1)
    def _():
        solve(state, e_ref, x_ref, rows)

    @pl.when(plane != 1)
    def _():
        x_ref[...] = jnp.zeros_like(x_ref)


def stage2_kernel(rows, plane_ref, e_ref, a_ref, b_ref, r_ref, from_ref, near_ref, x_ref, state):
    plane = plane_ref[0]

    @pl.when(plane == 2)
    def _():
        load_state(state, r_ref, 2 * rows)

    @pl.when(plane == 0)
    def _():
        state[...] = jnp.zeros_like(state)

    @pl.when((plane == 2) | (plane == 0))
    def _():
        subtract(state, a_ref, from_ref, rows)

    @pl.when(plane == 2)
    def _():
        subtract(state, b_ref, near_ref, rows)
        solve(state, e_ref, x_ref, rows)

    @pl.when(plane == 0)
    def _():
        x_ref[...] = state[0 : 2 * rows, :]

    @pl.when((plane == 1) | (plane == 3))
    def _():
        x_ref[...] = jnp.zeros_like(x_ref)


def stage3_kernel(rows, plane_ref, e_ref, b_ref, r_ref, part_ref, near_ref, x_ref, state):
    @pl.when(plane_ref[0] == 3)
    def _():
        load_state(state, r_ref, 2 * rows)
        state[0 : 2 * rows, :] = state[0 : 2 * rows, :] + part_ref[...]
        subtract(state, b_ref, near_ref, rows)
        solve(state, e_ref, x_ref, rows)

    @pl.when(plane_ref[0] != 3)
    def _():
        x_ref[...] = jnp.zeros_like(x_ref)


def per_device(factor, right_side, occ_order, cabs_order):
    planes, cores = lax.axis_size("y"), lax.axis_size("core")
    plane, core = lax.axis_index("y"), lax.axis_index("core")
    pieces = lax.axis_size("x") * lax.axis_size("z")
    per, aux = factor.shape
    rows = per * pieces
    span = cores * rows
    occ_total, cabs_total = occ_order.shape[0], cabs_order.shape[0]
    cabs_local = right_side.shape[1] // occ_total
    small = pltpu.CompilerParams(vmem_limit_bytes=8 * 1024 * 1024)

    slots = occ_order.reshape(pieces, cores).T.reshape(occ_total)
    pick = (jnp.arange(cabs_local, dtype=jnp.int32)[None, :] * occ_total + slots[:, None]).reshape(-1, 1)
    spread = (pick == jnp.arange(right_side.shape[1], dtype=jnp.int32)[None, :]).astype(jnp.float32)
    sent = lax.dot_general(spread, right_side, (((1,), (1,)), ((), ())), precision=HI, preferred_element_type=jnp.float32)
    sent = sent.reshape(occ_total, cabs_local, rows)
    got = lax.all_to_all(sent, ("core", "x", "z"), 0, 0, tiled=True).reshape(cores, cabs_total, rows)
    place = (jnp.arange(cabs_total, dtype=jnp.int32)[:, None] == cabs_order[None, :]).astype(jnp.float32)
    residual = lax.dot_general(got, place, (((1,), (0,)), ((), ())), precision=HI, preferred_element_type=jnp.float32)
    residual = residual.reshape(span, cabs_total)

    diag = lax.dynamic_slice_in_dim(factor, plane * span, span, 1)
    low, high = diag[:, :rows], diag[:, rows:]
    gap = jnp.zeros((per, 640 - rows), jnp.float32)
    diag = jnp.concatenate([jnp.where(core == 0, low, high), gap, low, gap], axis=1)
    tiles = diag.shape[1] // LANES
    pad_rows = (per * tiles + 7) // 8 * 8
    piece = jnp.pad(diag.reshape(per * tiles, LANES), ((0, pad_rows - per * tiles), (0, 0)))
    zs, xs = lax.axis_size("z"), lax.axis_size("x")
    near = lax.all_to_all(jnp.broadcast_to(piece[None], (zs, pad_rows, LANES)), "z", 0, 0, tiled=True)
    near = near.reshape(1, zs * pad_rows, LANES)
    far = lax.all_to_all(jnp.broadcast_to(near, (xs, zs * pad_rows, LANES)), "x", 0, 0, tiled=True)
    far = far.reshape(pieces * pad_rows, LANES)
    mine = pl.pallas_call(
        functools.partial(invert_kernel, rows, pieces, pad_rows, tiles),
        out_shape=jax.ShapeDtypeStruct((rows, tiles * LANES), jnp.float32),
        in_specs=[pl.BlockSpec(memory_space=pltpu.VMEM)],
        out_specs=pl.BlockSpec(memory_space=pltpu.VMEM),
        scratch_shapes=[pltpu.VMEM((tiles, 640, LANES), jnp.float32), pltpu.VMEM((5, LANES, LANES), jnp.float32)],
        compiler_params=pltpu.CompilerParams(vmem_limit_bytes=32 * 1024 * 1024),
        name="invert",
    )(far)
    swap = [(0, 1), (1, 0)]
    theirs = lax.ppermute(mine, "core", swap)
    core_arg = core.reshape(1).astype(jnp.int32)
    plane_arg = plane.reshape(1).astype(jnp.int32)
    smem = pl.BlockSpec(memory_space=pltpu.SMEM)
    here = pl.BlockSpec(memory_space=pltpu.VMEM)
    inverse = pl.pallas_call(
        pack_kernel,
        out_shape=jax.ShapeDtypeStruct((cores, 2, rows, tiles * LANES), jnp.bfloat16),
        in_specs=[smem, here, here],
        out_specs=here,
        compiler_params=small,
        name="pack",
    )(core_arg, mine, theirs)

    ltiles = span // LANES
    lpad = (per * ltiles + 7) // 8 * 8

    def gathered(block):
        flat = jnp.pad(block.reshape(per * ltiles, LANES), ((0, lpad - per * ltiles), (0, 0)))
        line = lax.all_gather(flat, "z", axis=0, tiled=True)
        return lax.all_gather(line, "x", axis=0, tiled=True)

    moved = lax.ppermute(factor[:, span : 2 * span], "y", [(3, 0)])
    first = gathered(jnp.where(plane == 0, moved, factor[:, :span]))
    second = gathered(lax.dynamic_slice_in_dim(factor, jnp.maximum(plane - 1, 0) * span, span, 1))

    def ordered(whole, after):
        whole, _ = lax.optimization_barrier((whole, after))
        partner = lax.ppermute(whole, "core", swap)
        return pl.pallas_call(
            functools.partial(order_kernel, rows, pieces, lpad, ltiles),
            out_shape=jax.ShapeDtypeStruct((2, span, span), jnp.bfloat16),
            in_specs=[smem, here, here],
            out_specs=here,
            scratch_shapes=[pltpu.VMEM((rows, LANES), jnp.float32)],
            compiler_params=small,
            name="order",
        )(core_arg, whole, partner)

    block = jax.ShapeDtypeStruct((span, LANES), jnp.float32)

    def call(kernel, outs, args, flops, name):
        return pl.pallas_call(
            functools.partial(kernel, rows),
            out_shape=(block,) * outs,
            in_specs=[smem] + [here] * len(args),
            out_specs=(here,) * outs,
            scratch_shapes=[pltpu.VMEM((span + 64, LANES), jnp.float32)],
            compiler_params=small,
            cost_estimate=pl.CostEstimate(flops=flops, bytes_accessed=4_000_000, transcendentals=0),
            name=name,
        )(plane_arg, *args)

    def send(value, pairs):
        return lax.ppermute(value, "y", pairs)

    starts = range(0, cabs_total, LANES)
    states = [residual[:, start : start + LANES] for start in starts]
    x0s, parts, chunks = [], [], []
    for state in states:
        x0s += call(stage0_kernel, 1, (inverse, state), 1_000_000_000, "stage0")
    a_mat = ordered(first, inverse)
    b_mat = ordered(second, a_mat[0, :8, :128])
    for state, x0 in zip(states, x0s):
        seen = send(x0, [(0, 1)]) + send(x0, [(0, 3)])
        state, x1 = call(stage1_kernel, 2, (inverse, a_mat, state, seen), 2_000_000_000, "stage1")
        far_x = send(seen, [(3, 2)]) + send(x1, [(1, 0)])
        near_x = send(x1, [(1, 2)])
        (x2,) = call(stage2_kernel, 1, (inverse, a_mat, b_mat, state, far_x, near_x), 3_000_000_000, "stage2")
        part = send(x2, [(0, 3)])
        near_x = send(x2, [(2, 3)])
        (x3,) = call(stage3_kernel, 1, (inverse, b_mat, state, part, near_x), 2_000_000_000, "stage3")
        chunks.append(jnp.where(plane == 0, x0, jnp.where(plane == 1, x1, jnp.where(plane == 2, x2, x3))))
    solved = jnp.concatenate([x.T for x in chunks], axis=0)
    keep = jnp.where(core == 0, solved[:, :rows], solved[:, rows:])
    give = jnp.where(core == 0, solved[:, rows:], solved[:, :rows])
    came = lax.ppermute(give, "core", [(0, 1), (1, 0)])
    return jnp.where(core == 0, jnp.stack([keep, came]), jnp.stack([came, keep]))


def solution(mesh):
    grid = Mesh(mesh.devices.reshape(4, 2, 4, 8), ("y", "core", "x", "z"))
    in_specs = (P(("y", "core", "x", "z"), None), P(("y", "core"), ("x", "z")), P(), P())
    out_specs = P(("x", "z"), None, ("y", "core"))
    return jax.shard_map(per_device, mesh=grid, in_specs=in_specs, out_specs=out_specs, check_vma=False)
```

```python
import functools
import jax
import jax.numpy as jnp
from jax import lax
from jax.experimental import pallas as pl
from jax.experimental.pallas import tpu as pltpu
from jax.sharding import Mesh, PartitionSpec as P

HI = lax.Precision.HIGHEST
LANES = 128


def full_dot(left, right):
    return jnp.dot(left, right, precision=HI, preferred_element_type=jnp.float32)


def halves(value):
    high = value.astype(jnp.bfloat16)
    return high, (value - high.astype(jnp.float32)).astype(jnp.bfloat16)


def split_right(value):
    high, low = halves(value)
    return jnp.concatenate([high, low], axis=1), high


def three_dot(left, right):
    lh, ll = left
    both, rh = right
    dot = functools.partial(jnp.dot, preferred_element_type=jnp.float32)
    wide = dot(lh, both)
    return wide[:, :LANES] + (wide[:, LANES:] + dot(ll, rh))


def invert_kernel(rows, groups, pieces, tiles, x_ref, own_ref, left_ref, far0_ref, far1_ref, right_ref, o_ref, a_ref, m_ref):
    per = rows // (groups * pieces)
    wide = 640
    blocks = wide // LANES
    x = x_ref[0]
    half = pieces // 2
    for ref, back, first, count in (
        (own_ref, 0, 0, pieces),
        (left_ref, 1, 0, pieces),
        (far0_ref, 2, 0, half),
        (far1_ref, 2, half, half),
        (right_ref, 3, 0, pieces),
    ):
        base = (lax.rem(x + groups - back, groups) * pieces + first) * per
        for tile in range(tiles):
            for row in range(per):
                a_ref[tile, pl.ds(base + row, count, stride=per), :] = ref[
                    pl.ds(row * tiles + tile, count, stride=per * tiles), :
                ]
    extra = wide - rows
    r0 = lax.broadcasted_iota(jnp.int32, (extra, LANES), 0)
    c0 = lax.broadcasted_iota(jnp.int32, (extra, LANES), 1)
    for tile in range(blocks - 1):
        a_ref[tile, rows:wide, :] = jnp.zeros((extra, LANES), jnp.float32)
    a_ref[blocks - 1, rows:wide, :] = jnp.where(c0 == r0 + (LANES - extra), 1.0, 0.0)
    ri = lax.broadcasted_iota(jnp.int32, (LANES, LANES), 0)
    ci = lax.broadcasted_iota(jnp.int32, (LANES, LANES), 1)

    def block(i, j):
        return a_ref[j, i * LANES : (i + 1) * LANES, :]

    for i in range(blocks):
        m_ref[i] = jnp.where(ri == ci, 1.0 / jnp.where(ri == ci, block(i, i), 1.0), 0.0)

    def double(level, carry):
        rb, cb = ri >> level, ci >> level
        take = (rb >> 1 == cb >> 1) & (rb == cb + 1)
        mids = [full_dot(jnp.where(take, block(i, i), 0.0), m_ref[i]) for i in range(blocks)]
        news = [m_ref[i] - full_dot(m_ref[i], mids[i]) for i in range(blocks)]
        for i in range(blocks):
            m_ref[i] = news[i]
        return carry

    lax.fori_loop(0, 7, double, 0)
    inv = [m_ref[i] for i in range(blocks)]
    for i in range(blocks):
        for j in range(blocks):
            last = min((i + 1) * LANES, rows)
            if j > i:
                o_ref[i * LANES : last, j * LANES : (j + 1) * LANES] = jnp.zeros((last - i * LANES, LANES), jnp.float32)
    done = [[None] * blocks for _ in range(blocks)]
    for i in range(blocks):
        done[i][i] = inv[i]
        last = min((i + 1) * LANES, rows)
        for j in range(i):
            total = full_dot(block(i, j), done[j][j])
            for k in range(j + 1, i):
                total = total + full_dot(block(i, k), done[k][j])
            done[i][j] = -full_dot(inv[i], total)
        for j in range(i + 1):
            o_ref[i * LANES : last, j * LANES : (j + 1) * LANES] = done[i][j][: last - i * LANES]
    for tile in range(blocks, tiles):
        o_ref[:, tile * LANES : (tile + 1) * LANES] = a_ref[tile, :rows, :]


def order_kernel(rows, pieces, pad_rows, first, tiles, core_ref, own_ref, other_ref, o_ref, s_ref):
    per = rows // pieces

    def copy(source, base):
        base = pl.multiple_of(base, rows)
        for tile in range(tiles):

            def move(row, carry):
                s_ref[pl.ds(row, pieces, stride=per), :] = source[
                    pl.ds(first + row * tiles + tile, pieces, stride=pad_rows), :
                ]
                return carry

            lax.fori_loop(0, per, move, 0, unroll=3)
            high, low = halves(s_ref[...])
            o_ref[0, pl.ds(base, rows), tile * LANES : (tile + 1) * LANES] = high
            o_ref[1, pl.ds(base, rows), tile * LANES : (tile + 1) * LANES] = low

    core = core_ref[0]
    copy(own_ref, core * rows)
    copy(other_ref, (1 - core) * rows)


def pack_kernel(core_ref, own_ref, other_ref, o_ref):
    core = core_ref[0]
    rows = own_ref.shape[0]
    for start in range(0, rows, 192):
        here = slice(start, start + 192)
        high, low = halves(own_ref[here, :])
        o_ref[core, 0, here, :] = high
        o_ref[core, 1, here, :] = low
        high, low = halves(other_ref[here, :])
        o_ref[1 - core, 0, here, :] = high
        o_ref[1 - core, 1, here, :] = low


def solve(state, e_ref, x_ref, rows):
    wide = 640
    step = rows // 3

    def put_first(index, value):
        x_ref[pl.ds(pl.multiple_of(index * step, step), step), :] = value

    def put_second(index, value):
        x_ref[pl.ds(pl.multiple_of(rows + index * step, step), step), :] = value

    def take(index, value):
        here = pl.ds(pl.multiple_of(rows + index * step, step), step)
        state[here, :] = state[here, :] - value

    def product(left, right, put):
        def part(index, carry):
            here = pl.ds(pl.multiple_of(index * step, step), step)
            total = None
            for (which, start, size), operand in zip(left, right):
                pair = e_ref[which, 0, here, start : start + size], e_ref[which, 1, here, start : start + size]
                term = three_dot(pair, operand)
                total = term if total is None else total + term
            put(index, total)
            return carry

        lax.fori_loop(0, 3, part, 0)

    half, link = rows // 2, e_ref.shape[3] - wide
    product([(0, 0, wide)], [split_right(state[0:wide, :])], put_first)
    tail = jnp.concatenate([x_ref[half:rows, :], jnp.zeros((link - half, LANES), jnp.float32)], axis=0)
    head = x_ref[0:link, :]
    product([(1, wide, link), (0, wide, link)], [split_right(head), split_right(tail)], take)
    product([(1, 0, wide)], [split_right(state[rows : rows + wide, :])], put_second)


def place_kernel(got_ref, place_ref, *outs):
    cores, _, rows = got_ref.shape
    for core in range(cores):
        for index, out in enumerate(outs):
            out[core * rows : (core + 1) * rows, :] = lax.dot_general(
                got_ref[core],
                place_ref[:, index * LANES : (index + 1) * LANES],
                (((0,), (0,)), ((), ())),
                precision=HI,
                preferred_element_type=jnp.float32,
            )


def load_state(state, r_ref, span):
    state[0:span, :] = r_ref[...]
    state[span:, :] = jnp.zeros((state.shape[0] - span, LANES), jnp.float32)


class Fetch:
    def __init__(self, source, target, sems, parts, axis):
        size = target.shape[axis] // parts
        self.copies = []
        for part in range(parts):
            where = tuple(pl.ds(part * size, size) if dim == axis else slice(None) for dim in range(len(target.shape)))
            self.copies.append(pltpu.make_async_copy(source.at[where], target.at[where], sems.at[part]))

    def start(self):
        for copy in self.copies:
            copy.start()

    def wait(self):
        for copy in self.copies:
            copy.wait()


def subtract(state, l_ref, x_ref, fetch):
    x = split_right(x_ref[...])
    parts = len(fetch.copies)
    step = l_ref.shape[1] // parts
    for index, copy in enumerate(fetch.copies):
        copy.wait()
        here = slice(index * step, (index + 1) * step)
        state[here, :] = state[here, :] - three_dot((l_ref[0, here, :], l_ref[1, here, :]), x)


def pick(plane, first, first_ref, second, second_ref, to_ref):
    @pl.when(plane == first)
    def _():
        to_ref[...] = first_ref[...]

    @pl.when(plane == second)
    def _():
        to_ref[...] = second_ref[...]


PARTS = 3


def stage_kernel(rows, number, plane_ref, e_hbm, a_hbm, b_hbm, r_ref, *refs):
    plane = plane_ref[0]
    span = 2 * rows
    arrived = refs[: (0, 2, 3, 2)[number]]
    outs = refs[len(arrived) : len(arrived) + (2 if number == 1 else 1)]
    state, seen, e_buf, a_buf, b_buf, sems = refs[len(arrived) + len(outs) :]
    x_ref = outs[-1]
    e_copy = Fetch(e_hbm, e_buf, sems.at[0], 2, 0)
    a_copy = Fetch(a_hbm, a_buf, sems.at[1], PARTS, 1) if number in (1, 2) else None
    b_copy = Fetch(b_hbm, b_buf, sems.at[2], PARTS, 1) if number >= 2 else None
    other = {1: 3, 2: 0}.get(number)
    works = plane == number if other is None else (plane == number) | (plane == other)

    @pl.when(works)
    def _():
        if number in (1, 2):
            a_copy.start()

        @pl.when(plane == number)
        def _():
            if number >= 2:
                b_copy.start()
            e_copy.start()

        load_state(state, r_ref, span)
        if number in (1, 2):
            pick(plane, number, arrived[0], other, arrived[1], seen)
            if number == 2:

                @pl.when(plane == 0)
                def _():
                    state[...] = jnp.zeros_like(state)

            subtract(state, a_buf, seen, a_copy)
        if number == 3:
            state[0:span, :] = state[0:span, :] + arrived[0][...]

    if number == 1:
        outs[0][...] = jnp.where(plane == 3, state[0:span, :], r_ref[...])

    @pl.when(plane == number)
    def _():
        if number >= 2:
            subtract(state, b_buf, arrived[-1], b_copy)
        e_copy.wait()
        solve(state, e_buf, x_ref, rows)

    if number == 2:

        @pl.when(plane == 0)
        def _():
            x_ref[...] = state[0:span, :]

        @pl.when((plane == 1) | (plane == 3))
        def _():
            x_ref[...] = jnp.zeros_like(x_ref)
    else:

        @pl.when(plane != number)
        def _():
            x_ref[...] = jnp.zeros_like(x_ref)


def per_device(factor, right_side, occ_order, cabs_order):
    planes, cores = lax.axis_size("y"), lax.axis_size("core")
    plane, core = lax.axis_index("y"), lax.axis_index("core")
    pieces = lax.axis_size("x") * lax.axis_size("z")
    per, aux = factor.shape
    rows = per * pieces
    span = cores * rows
    occ_total, cabs_total = occ_order.shape[0], cabs_order.shape[0]
    cabs_local = right_side.shape[1] // occ_total
    large = pltpu.CompilerParams(vmem_limit_bytes=58 * 1024 * 1024)

    slots = occ_order.reshape(pieces, cores).T.reshape(occ_total)
    pick = (jnp.arange(cabs_local, dtype=jnp.int32)[None, :] * occ_total + slots[:, None]).reshape(-1, 1)
    spread = (pick == jnp.arange(right_side.shape[1], dtype=jnp.int32)[None, :]).astype(jnp.float32)
    sent = lax.dot_general(spread, right_side, (((1,), (1,)), ((), ())), precision=HI, preferred_element_type=jnp.float32)
    sent = sent.reshape(occ_total, cabs_local, rows)

    swap = [(0, 1), (1, 0)]
    smem = pl.BlockSpec(memory_space=pltpu.SMEM)
    here = pl.BlockSpec(memory_space=pltpu.VMEM)
    zs, xs = lax.axis_size("z"), lax.axis_size("x")
    diag = lax.dynamic_slice_in_dim(factor, plane * span, span, 1)
    low, high = diag[:, :rows], diag[:, rows:]
    half = rows // 2
    gap, short = jnp.zeros((per, 640 - rows), jnp.float32), jnp.zeros((per, 384 - half), jnp.float32)
    lent = lax.ppermute(low[:, half:], "core", [(1, 0)])
    diag = jnp.where(
        core == 0,
        jnp.concatenate([low, gap, lent, short], axis=1),
        jnp.concatenate([high, gap, low[:, :half], short], axis=1),
    )
    tiles = diag.shape[1] // LANES
    piece, sent = lax.optimization_barrier((diag.reshape(per * tiles, LANES), sent))
    near = lax.all_gather(piece, "z", axis=0, tiled=True)
    near, sent = lax.optimization_barrier((near, sent))
    got = lax.all_to_all(sent, ("core", "x", "z"), 0, 0, tiled=True)
    ahead = [(i, (i + 1) % xs) for i in range(xs)]
    behind = [(i, (i - 1) % xs) for i in range(xs)]
    left, right = lax.ppermute(near, "x", ahead), lax.ppermute(near, "x", behind)
    middle = near.shape[0] // 2
    ltiles = span // LANES
    lpad = (per * ltiles + 7) // 8 * 8

    def flat(block):
        return jnp.pad(block.reshape(per * ltiles, LANES), ((0, lpad - per * ltiles), (0, 0)))

    moved = lax.ppermute(factor[:, span : 2 * span], "y", [(3, 0)])
    block_a = jnp.where(plane == 0, moved, factor[:, :span])
    block_b = lax.dynamic_slice_in_dim(factor, jnp.maximum(plane - 1, 0) * span, span, 1)
    whole = lax.all_gather(jnp.concatenate([flat(block_a), flat(block_b)]), ("x", "z"), axis=0, tiled=True)

    far0, far1 = lax.ppermute(left[:middle], "x", ahead), lax.ppermute(right[middle:], "x", behind)
    far0, far1, got = lax.optimization_barrier((far0, far1, got))
    got = got.reshape(cores, cabs_total, rows)
    place = (jnp.arange(cabs_total, dtype=jnp.int32)[:, None] == cabs_order[None, :]).astype(jnp.float32)
    states = list(pl.pallas_call(
        place_kernel,
        out_shape=(jax.ShapeDtypeStruct((span, LANES), jnp.float32),) * (cabs_total // LANES),
        in_specs=[here, here],
        out_specs=(here,) * (cabs_total // LANES),
        compiler_params=large,
        name="place",
    )(got, place))
    mine = pl.pallas_call(
        functools.partial(invert_kernel, rows, xs, zs, tiles),
        out_shape=jax.ShapeDtypeStruct((rows, tiles * LANES), jnp.float32),
        in_specs=[smem] + [here] * 5,
        out_specs=here,
        scratch_shapes=[pltpu.VMEM((tiles, 640, LANES), jnp.float32), pltpu.VMEM((5, LANES, LANES), jnp.float32)],
        compiler_params=large,
        name="invert",
    )(lax.axis_index("x").reshape(1).astype(jnp.int32), near, left, far0, far1, right)
    theirs = lax.ppermute(mine, "core", swap)
    core_arg = core.reshape(1).astype(jnp.int32)
    plane_arg = plane.reshape(1).astype(jnp.int32)
    inverse = pl.pallas_call(
        pack_kernel,
        out_shape=jax.ShapeDtypeStruct((cores, 2, rows, tiles * LANES), jnp.bfloat16),
        in_specs=[smem, here, here],
        out_specs=here,
        compiler_params=large,
        name="pack",
    )(core_arg, mine, theirs)

    def after(value, token):
        value, token = lax.optimization_barrier((value, token.reshape(-1)[:1]))
        return value, (token != token).astype(jnp.int32)

    def ordered(which, whole, partner, zero):
        return pl.pallas_call(
            functools.partial(order_kernel, rows, pieces, 2 * lpad, which * lpad, ltiles),
            out_shape=jax.ShapeDtypeStruct((2, span, span), jnp.bfloat16),
            in_specs=[smem, here, here],
            out_specs=here,
            scratch_shapes=[pltpu.VMEM((rows, LANES), jnp.float32)],
            compiler_params=large,
            name="order",
        )(core_arg + zero, whole, partner)

    block = jax.ShapeDtypeStruct((span, LANES), jnp.float32)

    far_ref = pl.BlockSpec(memory_space=pltpu.HBM)

    def stage(number, *args):
        outs = 2 if number == 1 else 1
        return pl.pallas_call(
            functools.partial(stage_kernel, rows, number),
            out_shape=(block,) * outs,
            in_specs=[smem] + [far_ref] * 3 + [here] * (len(args) - 3),
            out_specs=(here,) * outs,
            scratch_shapes=[
                pltpu.VMEM((span + 64, LANES), jnp.float32),
                pltpu.VMEM((span, LANES), jnp.float32),
                pltpu.VMEM(inverse.shape, inverse.dtype),
                pltpu.VMEM((2, span, span), jnp.bfloat16),
                pltpu.VMEM((2, span, span), jnp.bfloat16),
                pltpu.SemaphoreType.DMA((3, PARTS)),
            ],
            compiler_params=large,
            cost_estimate=pl.CostEstimate(flops=2_000_000_000, bytes_accessed=4_000_000, transcendentals=0),
            name=f"stage{number}",
        )(plane_arg, *args)

    def send(value, pairs):
        return lax.ppermute(value, "y", pairs)

    x0s, chunks = [], []
    for state in states:
        x0s += stage(0, inverse, inverse, inverse, state)
    whole, zero = after(whole, x0s[0])
    partner = lax.ppermute(whole, "core", swap)
    a_mat = ordered(0, whole, partner, zero)
    x1s = []
    for index, (state, x0) in enumerate(zip(states, x0s)):
        to1, to3 = send(x0, [(0, 1)]), send(x0, [(0, 3)])
        to2 = send(to3, [(3, 2)])
        states[index], x1 = stage(1, inverse, a_mat, a_mat, state, to1, to3)
        x1s.append((x1, to2))
    token, zero = after(core_arg, x1s[0][0])
    b_mat = ordered(1, whole, partner, token - core_arg + zero)
    for state, x0, (x1, to2) in zip(states, x0s, x1s):
        near_x, to0 = send(x1, [(1, 2)]), send(x1, [(1, 0)])
        (x2,) = stage(2, inverse, a_mat, b_mat, state, to2, to0, near_x)
        part = send(x2, [(0, 3)])
        near_x = send(x2, [(2, 3)])
        (x3,) = stage(3, inverse, b_mat, b_mat, state, part, near_x)
        chunks.append(jnp.where(plane == 0, x0, jnp.where(plane == 1, x1, jnp.where(plane == 2, x2, x3))))
    solved = jnp.concatenate([x.T for x in chunks], axis=0)
    keep = jnp.where(core == 0, solved[:, :rows], solved[:, rows:])
    give = jnp.where(core == 0, solved[:, rows:], solved[:, :rows])
    came = lax.ppermute(give, "core", [(0, 1), (1, 0)])
    return jnp.where(core == 0, jnp.stack([keep, came]), jnp.stack([came, keep]))


def solution(mesh):
    grid = Mesh(mesh.devices.reshape(4, 2, 4, 8), ("y", "core", "x", "z"))
    in_specs = (P(("y", "core", "x", "z"), None), P(("y", "core"), ("x", "z")), P(), P())
    out_specs = P(("x", "z"), None, ("y", "core"))
    return jax.shard_map(per_device, mesh=grid, in_specs=in_specs, out_specs=out_specs, check_vma=False)
```

```python
import functools
import jax
import jax.numpy as jnp
from jax import lax
from jax.experimental import pallas as pl
from jax.experimental.pallas import tpu as pltpu
from jax.sharding import Mesh, PartitionSpec as P

HI = lax.Precision.HIGHEST
LANES = 128


def full_dot(left, right):
    return jnp.dot(left, right, precision=HI, preferred_element_type=jnp.float32)


def halves(value):
    high = value.astype(jnp.bfloat16)
    return high, (value - high.astype(jnp.float32)).astype(jnp.bfloat16)


def split_right(value):
    high, low = halves(value)
    return jnp.concatenate([high, low], axis=1), high


def three_dot(left, right):
    lh, ll = left
    both, rh = right
    dot = functools.partial(jnp.dot, preferred_element_type=jnp.float32)
    wide = dot(lh, both)
    return wide[:, :LANES] + (wide[:, LANES:] + dot(ll, rh))


def invert_kernel(rows, groups, pieces, tiles, x_ref, own_ref, left_ref, far0_ref, far1_ref, right_ref, o_ref, a_ref, m_ref):
    per = rows // (groups * pieces)
    wide = 640
    blocks = wide // LANES
    x = x_ref[0]
    half = pieces // 2
    for ref, back, first, count in (
        (own_ref, 0, 0, pieces),
        (left_ref, 1, 0, pieces),
        (far0_ref, 2, 0, half),
        (far1_ref, 2, half, half),
        (right_ref, 3, 0, pieces),
    ):
        base = (lax.rem(x + groups - back, groups) * pieces + first) * per
        for tile in range(tiles):
            for row in range(per):
                a_ref[tile, pl.ds(base + row, count, stride=per), :] = ref[
                    pl.ds(row * tiles + tile, count, stride=per * tiles), :
                ]
    extra = wide - rows
    r0 = lax.broadcasted_iota(jnp.int32, (extra, LANES), 0)
    c0 = lax.broadcasted_iota(jnp.int32, (extra, LANES), 1)
    for tile in range(blocks - 1):
        a_ref[tile, rows:wide, :] = jnp.zeros((extra, LANES), jnp.float32)
    a_ref[blocks - 1, rows:wide, :] = jnp.where(c0 == r0 + (LANES - extra), 1.0, 0.0)
    ri = lax.broadcasted_iota(jnp.int32, (LANES, LANES), 0)
    ci = lax.broadcasted_iota(jnp.int32, (LANES, LANES), 1)

    def block(i, j):
        return a_ref[j, i * LANES : (i + 1) * LANES, :]

    for i in range(blocks):
        m_ref[i] = jnp.where(ri == ci, 1.0 / jnp.where(ri == ci, block(i, i), 1.0), 0.0)

    def double(level, carry):
        rb, cb = ri >> level, ci >> level
        take = (rb >> 1 == cb >> 1) & (rb == cb + 1)
        mids = [full_dot(jnp.where(take, block(i, i), 0.0), m_ref[i]) for i in range(blocks)]
        news = [m_ref[i] - full_dot(m_ref[i], mids[i]) for i in range(blocks)]
        for i in range(blocks):
            m_ref[i] = news[i]
        return carry

    lax.fori_loop(0, 7, double, 0)
    inv = [m_ref[i] for i in range(blocks)]
    for i in range(blocks):
        for j in range(blocks):
            last = min((i + 1) * LANES, rows)
            if j > i:
                o_ref[i * LANES : last, j * LANES : (j + 1) * LANES] = jnp.zeros((last - i * LANES, LANES), jnp.float32)
    done = [[None] * blocks for _ in range(blocks)]
    for i in range(blocks):
        done[i][i] = inv[i]
        last = min((i + 1) * LANES, rows)
        for j in range(i):
            total = full_dot(block(i, j), done[j][j])
            for k in range(j + 1, i):
                total = total + full_dot(block(i, k), done[k][j])
            done[i][j] = -full_dot(inv[i], total)
        for j in range(i + 1):
            o_ref[i * LANES : last, j * LANES : (j + 1) * LANES] = done[i][j][: last - i * LANES]
    for tile in range(blocks, tiles):
        o_ref[:, tile * LANES : (tile + 1) * LANES] = a_ref[tile, :rows, :]


def order_kernel(rows, groups, pieces, pad_rows, tiles, turned, where_ref, own_ref, other_ref, o_ref, s_ref):
    per = rows // (groups * pieces)

    def copy(source, base):
        base = pl.multiple_of(base, rows)
        for tile in range(tiles):

            def move(row, carry):
                for group in range(groups):
                    place = lax.rem(where_ref[1] + groups - group, groups) if turned else group
                    s_ref[pl.ds(place * pieces * per + row, pieces, stride=per), :] = source[
                        pl.ds(group * pieces * pad_rows + row * tiles + tile, pieces, stride=pad_rows), :
                    ]
                return carry

            lax.fori_loop(0, per, move, 0, unroll=3)
            high, low = halves(s_ref[...])
            o_ref[0, pl.ds(base, rows), tile * LANES : (tile + 1) * LANES] = high
            o_ref[1, pl.ds(base, rows), tile * LANES : (tile + 1) * LANES] = low

    core = where_ref[0]
    copy(own_ref, core * rows)
    copy(other_ref, (1 - core) * rows)


def pack_kernel(core_ref, own_ref, other_ref, o_ref):
    core = core_ref[0]
    rows = own_ref.shape[0]
    for start in range(0, rows, 192):
        here = slice(start, start + 192)
        high, low = halves(own_ref[here, :])
        o_ref[core, 0, here, :] = high
        o_ref[core, 1, here, :] = low
        high, low = halves(other_ref[here, :])
        o_ref[1 - core, 0, here, :] = high
        o_ref[1 - core, 1, here, :] = low


def solve(state, e_ref, x_ref, rows):
    wide = 640
    step = rows // 3

    def put_first(index, value):
        x_ref[pl.ds(pl.multiple_of(index * step, step), step), :] = value

    def put_second(index, value):
        x_ref[pl.ds(pl.multiple_of(rows + index * step, step), step), :] = value

    def take(index, value):
        here = pl.ds(pl.multiple_of(rows + index * step, step), step)
        state[here, :] = state[here, :] - value

    def product(left, right, put):
        def part(index, carry):
            here = pl.ds(pl.multiple_of(index * step, step), step)
            total = None
            for (which, start, size), operand in zip(left, right):
                pair = e_ref[which, 0, here, start : start + size], e_ref[which, 1, here, start : start + size]
                term = three_dot(pair, operand)
                total = term if total is None else total + term
            put(index, total)
            return carry

        lax.fori_loop(0, 3, part, 0)

    half, link = rows // 2, e_ref.shape[3] - wide
    product([(0, 0, wide)], [split_right(state[0:wide, :])], put_first)
    tail = jnp.concatenate([x_ref[half:rows, :], jnp.zeros((link - half, LANES), jnp.float32)], axis=0)
    head = x_ref[0:link, :]
    product([(1, wide, link), (0, wide, link)], [split_right(head), split_right(tail)], take)
    product([(1, 0, wide)], [split_right(state[rows : rows + wide, :])], put_second)


def place_kernel(got_ref, place_ref, *outs):
    cores, _, rows = got_ref.shape
    for core in range(cores):
        for index, out in enumerate(outs):
            out[core * rows : (core + 1) * rows, :] = lax.dot_general(
                got_ref[core],
                place_ref[:, index * LANES : (index + 1) * LANES],
                (((0,), (0,)), ((), ())),
                precision=HI,
                preferred_element_type=jnp.float32,
            )


def load_state(state, r_ref, span):
    state[0:span, :] = r_ref[...]
    state[span:, :] = jnp.zeros((state.shape[0] - span, LANES), jnp.float32)


def subtract(state, l_ref, x_ref):
    x = split_right(x_ref[...])
    step = l_ref.shape[1] // 4

    def part(index, carry):
        here = pl.ds(pl.multiple_of(index * step, step), step)
        state[here, :] = state[here, :] - three_dot((l_ref[0, here, :], l_ref[1, here, :]), x)
        return carry

    lax.fori_loop(0, 4, part, 0)


def pick(plane, first, first_ref, second, second_ref, to_ref):
    @pl.when(plane == first)
    def _():
        to_ref[...] = first_ref[...]

    @pl.when(plane == second)
    def _():
        to_ref[...] = second_ref[...]


def stage_kernel(rows, number, plane_ref, *refs):
    plane = plane_ref[0]
    span = 2 * rows
    e_ref, refs = refs[0], refs[1:]
    a_ref, refs = (refs[0], refs[1:]) if number in (1, 2) else (None, refs)
    b_ref, refs = (refs[0], refs[1:]) if number >= 2 else (None, refs)
    r_ref, refs = refs[0], refs[1:]
    arrived = refs[: (0, 2, 3, 2)[number]]
    outs = refs[len(arrived) : len(arrived) + (2 if number == 1 else 1)]
    state, seen = refs[len(arrived) + len(outs) :]
    x_ref = outs[-1]
    other = {1: 3, 2: 0}.get(number)
    works = plane == number if other is None else (plane == number) | (plane == other)

    @pl.when(works)
    def _():
        load_state(state, r_ref, span)
        if number in (1, 2):
            pick(plane, number, arrived[0], other, arrived[1], seen)
            if number == 2:

                @pl.when(plane == 0)
                def _():
                    state[...] = jnp.zeros_like(state)

            subtract(state, a_ref, seen)
        if number == 3:
            state[0:span, :] = state[0:span, :] + arrived[0][...]

    if number == 1:
        outs[0][...] = jnp.where(plane == 3, state[0:span, :], r_ref[...])

    @pl.when(plane == number)
    def _():
        if number >= 2:
            subtract(state, b_ref, arrived[-1])
        solve(state, e_ref, x_ref, rows)

    if number == 2:

        @pl.when(plane == 0)
        def _():
            x_ref[...] = state[0:span, :]

        @pl.when((plane == 1) | (plane == 3))
        def _():
            x_ref[...] = jnp.zeros_like(x_ref)
    else:

        @pl.when(plane != number)
        def _():
            x_ref[...] = jnp.zeros_like(x_ref)


def per_device(factor, right_side, occ_order, cabs_order):
    planes, cores = lax.axis_size("y"), lax.axis_size("core")
    plane, core = lax.axis_index("y"), lax.axis_index("core")
    pieces = lax.axis_size("x") * lax.axis_size("z")
    per, aux = factor.shape
    rows = per * pieces
    span = cores * rows
    occ_total, cabs_total = occ_order.shape[0], cabs_order.shape[0]
    cabs_local = right_side.shape[1] // occ_total
    cheap = pl.CostEstimate(flops=1000, bytes_accessed=1000, transcendentals=0)
    small = pltpu.CompilerParams(vmem_limit_bytes=8 * 1024 * 1024)
    large = pltpu.CompilerParams(vmem_limit_bytes=24 * 1024 * 1024)

    slots = occ_order.reshape(pieces, cores).T.reshape(occ_total)
    pick = (jnp.arange(cabs_local, dtype=jnp.int32)[None, :] * occ_total + slots[:, None]).reshape(-1, 1)
    spread = (pick == jnp.arange(right_side.shape[1], dtype=jnp.int32)[None, :]).astype(jnp.float32)
    sent = lax.dot_general(spread, right_side, (((1,), (1,)), ((), ())), precision=HI, preferred_element_type=jnp.float32)
    sent = sent.reshape(occ_total, cabs_local, rows)

    swap = [(0, 1), (1, 0)]
    smem = pl.BlockSpec(memory_space=pltpu.SMEM)
    here = pl.BlockSpec(memory_space=pltpu.VMEM)
    zs, xs = lax.axis_size("z"), lax.axis_size("x")
    diag = lax.dynamic_slice_in_dim(factor, plane * span, span, 1)
    low, high = diag[:, :rows], diag[:, rows:]
    half = rows // 2
    gap, short = jnp.zeros((per, 640 - rows), jnp.float32), jnp.zeros((per, 384 - half), jnp.float32)
    lent = lax.ppermute(low[:, half:], "core", [(1, 0)])
    diag = jnp.where(
        core == 0,
        jnp.concatenate([low, gap, lent, short], axis=1),
        jnp.concatenate([high, gap, low[:, :half], short], axis=1),
    )
    tiles = diag.shape[1] // LANES
    piece, sent = lax.optimization_barrier((diag.reshape(per * tiles, LANES), sent))
    near = lax.all_gather(piece, "z", axis=0, tiled=True)
    ahead = [(i, (i + 1) % xs) for i in range(xs)]
    behind = [(i, (i - 1) % xs) for i in range(xs)]

    def flat(block):
        return jnp.pad(block.reshape(per * ltiles, LANES), ((0, lpad - per * ltiles), (0, 0)))

    ltiles = span // LANES
    lpad = (per * ltiles + 7) // 8 * 8
    moved = lax.ppermute(factor[:, span : 2 * span], "y", [(3, 0)])
    flat_a = flat(jnp.where(plane == 0, moved, factor[:, :span]))
    flat_b = flat(lax.dynamic_slice_in_dim(factor, jnp.maximum(plane - 1, 0) * span, span, 1))
    near, flat_a, flat_b, sent = lax.optimization_barrier((near, flat_a, flat_b, sent))
    got = lax.all_to_all(sent, ("core", "x", "z"), 0, 0, tiled=True)
    left, right = lax.ppermute(near, "x", ahead), lax.ppermute(near, "x", behind)
    near_a = lax.all_gather(flat_a, "z", axis=0, tiled=True)
    near_b = lax.all_gather(flat_b, "z", axis=0, tiled=True)
    left, right, near_a, near_b = lax.optimization_barrier((left, right, near_a, near_b))

    def far(left, right):
        middle = left.shape[0] // 2
        return lax.ppermute(left[:middle], "x", ahead), lax.ppermute(right[middle:], "x", behind)

    far0, far1 = far(left, right)
    far0, far1, got, near_a = lax.optimization_barrier((far0, far1, got, near_a))
    left_a, right_a = lax.ppermute(near_a, "x", ahead), lax.ppermute(near_a, "x", behind)
    got = got.reshape(cores, cabs_total, rows)
    place = (jnp.arange(cabs_total, dtype=jnp.int32)[:, None] == cabs_order[None, :]).astype(jnp.float32)
    states = list(pl.pallas_call(
        place_kernel,
        out_shape=(jax.ShapeDtypeStruct((span, LANES), jnp.float32),) * (cabs_total // LANES),
        in_specs=[here, here],
        out_specs=(here,) * (cabs_total // LANES),
        compiler_params=small,
        cost_estimate=cheap,
        name="place",
    )(got, place))
    mine = pl.pallas_call(
        functools.partial(invert_kernel, rows, xs, zs, tiles),
        out_shape=jax.ShapeDtypeStruct((rows, tiles * LANES), jnp.float32),
        in_specs=[smem] + [here] * 5,
        out_specs=here,
        scratch_shapes=[pltpu.VMEM((tiles, 640, LANES), jnp.float32), pltpu.VMEM((5, LANES, LANES), jnp.float32)],
        compiler_params=large,
        cost_estimate=cheap,
        name="invert",
    )(lax.axis_index("x").reshape(1).astype(jnp.int32), near, left, far0, far1, right)
    theirs = lax.ppermute(mine, "core", swap)
    far0_a, far1_a = far(left_a, right_a)
    theirs, far0_a, far1_a, near_b = lax.optimization_barrier((theirs, far0_a, far1_a, near_b))
    left_b, right_b = lax.ppermute(near_b, "x", ahead), lax.ppermute(near_b, "x", behind)
    whole_a = jnp.concatenate([near_a, left_a, far0_a, far1_a, right_a])
    core_arg = core.reshape(1).astype(jnp.int32)
    plane_arg = plane.reshape(1).astype(jnp.int32)
    inverse = pl.pallas_call(
        pack_kernel,
        out_shape=jax.ShapeDtypeStruct((cores, 2, rows, tiles * LANES), jnp.bfloat16),
        in_specs=[smem, here, here],
        out_specs=here,
        compiler_params=small,
        cost_estimate=cheap,
        name="pack",
    )(core_arg, mine, theirs)

    def after(value, tokens):
        value, token = lax.optimization_barrier((value, sum(token[0, :1] for token in tokens)))
        return value, (token != token).astype(jnp.int32)

    def ordered(whole, tokens, turned):
        _, zero = after(core_arg, tokens)
        partner = lax.ppermute(whole, "core", swap)
        where = jnp.concatenate([core_arg + zero, lax.axis_index("x").reshape(1).astype(jnp.int32)])
        return pl.pallas_call(
            functools.partial(order_kernel, rows, xs, zs, lpad, ltiles, turned),
            out_shape=jax.ShapeDtypeStruct((2, span, span), jnp.bfloat16),
            in_specs=[smem, here, here],
            out_specs=here,
            scratch_shapes=[pltpu.VMEM((rows, LANES), jnp.float32)],
            compiler_params=small,
            cost_estimate=pl.CostEstimate(flops=1_000_000, bytes_accessed=16_000_000, transcendentals=0),
            name="order",
        )(where, whole, partner)

    block = jax.ShapeDtypeStruct((span, LANES), jnp.float32)

    def stage(number, *args):
        outs = 2 if number == 1 else 1
        return pl.pallas_call(
            functools.partial(stage_kernel, rows, number),
            out_shape=(block,) * outs,
            in_specs=[smem] + [here] * len(args),
            out_specs=(here,) * outs,
            scratch_shapes=[pltpu.VMEM((span + 64, LANES), jnp.float32), pltpu.VMEM((span, LANES), jnp.float32)],
            compiler_params=small,
            cost_estimate=pl.CostEstimate(flops=30_000_000_000, bytes_accessed=4_000_000, transcendentals=0),
            name=f"stage{number}",
        )(plane_arg, *args)

    def send(value, pairs):
        return lax.ppermute(value, "y", pairs)

    x0s, chunks = [], []
    for state in states:
        x0s += stage(0, inverse, state)
    a_mat = ordered(whole_a, x0s, True)
    left_b, right_b, token = lax.optimization_barrier((left_b, right_b, a_mat[0, :1].astype(jnp.float32)))
    whole_b = jnp.concatenate([near_b, left_b, *far(left_b, right_b), right_b])
    x1s, nexts = [], []
    for index, (state, x0) in enumerate(zip(list(states), x0s)):
        to1, to3 = send(x0, [(0, 1)]), send(x0, [(0, 3)])
        to2 = send(to3, [(3, 2)])
        states[index], x1 = stage(1, inverse, a_mat, state, to1, to3)
        near_x, to0 = send(x1, [(1, 2)]), send(x1, [(1, 0)])
        x1s.append((x1, to2))
        nexts.append((near_x, to0))
    b_mat = ordered(whole_b, [x1 for x1, _ in x1s] + [token], True)
    for state, x0, (x1, to2), (near_x, to0) in zip(states, x0s, x1s, nexts):
        (x2,) = stage(2, inverse, a_mat, b_mat, state, to2, to0, near_x)
        part = send(x2, [(0, 3)])
        near_x = send(x2, [(2, 3)])
        (x3,) = stage(3, inverse, b_mat, state, part, near_x)
        chunks.append(jnp.where(plane == 0, x0, jnp.where(plane == 1, x1, jnp.where(plane == 2, x2, x3))))
    solved = jnp.concatenate([x.T for x in chunks], axis=0)
    keep = jnp.where(core == 0, solved[:, :rows], solved[:, rows:])
    give = jnp.where(core == 0, solved[:, rows:], solved[:, :rows])
    came = lax.ppermute(give, "core", [(0, 1), (1, 0)])
    return jnp.where(core == 0, jnp.stack([keep, came]), jnp.stack([came, keep]))


def solution(mesh):
    grid = Mesh(mesh.devices.reshape(4, 2, 4, 8), ("y", "core", "x", "z"))
    in_specs = (P(("y", "core", "x", "z"), None), P(("y", "core"), ("x", "z")), P(), P())
    out_specs = P(("x", "z"), None, ("y", "core"))
    return jax.shard_map(per_device, mesh=grid, in_specs=in_specs, out_specs=out_specs, check_vma=False)
```

```python
import functools
import jax
import jax.numpy as jnp
from jax import lax
from jax.experimental import pallas as pl
from jax.experimental.pallas import tpu as pltpu
from jax.sharding import Mesh, PartitionSpec as P

HI = lax.Precision.HIGHEST
LANES = 128


def full_dot(left, right):
    return jnp.dot(left, right, precision=HI, preferred_element_type=jnp.float32)


def halves(value):
    high = value.astype(jnp.bfloat16)
    return high, (value - high.astype(jnp.float32)).astype(jnp.bfloat16)


def split_right(value):
    high, low = halves(value)
    return jnp.concatenate([high, low], axis=1), high


def three_dot(left, right):
    lh, ll = left
    both, rh = right
    dot = functools.partial(jnp.dot, preferred_element_type=jnp.float32)
    wide = dot(lh, both)
    return wide[:, :LANES] + (wide[:, LANES:] + dot(ll, rh))


def invert_kernel(rows, groups, pieces, tiles, x_ref, own_ref, left_ref, far0_ref, far1_ref, right_ref, o_ref, a_ref, m_ref):
    per = rows // (groups * pieces)
    wide = 640
    blocks = wide // LANES
    x = x_ref[0]
    half = pieces // 2
    for ref, back, first, count in (
        (own_ref, 0, 0, pieces),
        (left_ref, 1, 0, pieces),
        (far0_ref, 2, 0, half),
        (far1_ref, 2, half, half),
        (right_ref, 3, 0, pieces),
    ):
        base = (lax.rem(x + groups - back, groups) * pieces + first) * per
        for tile in range(tiles):
            for row in range(per):
                a_ref[tile, pl.ds(base + row, count, stride=per), :] = ref[
                    pl.ds(row * tiles + tile, count, stride=per * tiles), :
                ]
    extra = wide - rows
    r0 = lax.broadcasted_iota(jnp.int32, (extra, LANES), 0)
    c0 = lax.broadcasted_iota(jnp.int32, (extra, LANES), 1)
    for tile in range(blocks - 1):
        a_ref[tile, rows:wide, :] = jnp.zeros((extra, LANES), jnp.float32)
    a_ref[blocks - 1, rows:wide, :] = jnp.where(c0 == r0 + (LANES - extra), 1.0, 0.0)
    ri = lax.broadcasted_iota(jnp.int32, (LANES, LANES), 0)
    ci = lax.broadcasted_iota(jnp.int32, (LANES, LANES), 1)

    def block(i, j):
        return a_ref[j, i * LANES : (i + 1) * LANES, :]

    for i in range(blocks):
        m_ref[i] = jnp.where(ri == ci, 1.0 / jnp.where(ri == ci, block(i, i), 1.0), 0.0)

    def double(level, carry):
        rb, cb = ri >> level, ci >> level
        take = (rb >> 1 == cb >> 1) & (rb == cb + 1)
        mids = [full_dot(jnp.where(take, block(i, i), 0.0), m_ref[i]) for i in range(blocks)]
        news = [m_ref[i] - full_dot(m_ref[i], mids[i]) for i in range(blocks)]
        for i in range(blocks):
            m_ref[i] = news[i]
        return carry

    lax.fori_loop(0, 7, double, 0)
    inv = [m_ref[i] for i in range(blocks)]
    for i in range(blocks):
        for j in range(blocks):
            last = min((i + 1) * LANES, rows)
            if j > i:
                o_ref[i * LANES : last, j * LANES : (j + 1) * LANES] = jnp.zeros((last - i * LANES, LANES), jnp.float32)
    done = [[None] * blocks for _ in range(blocks)]
    for i in range(blocks):
        done[i][i] = inv[i]
        last = min((i + 1) * LANES, rows)
        for j in range(i):
            total = full_dot(block(i, j), done[j][j])
            for k in range(j + 1, i):
                total = total + full_dot(block(i, k), done[k][j])
            done[i][j] = -full_dot(inv[i], total)
        for j in range(i + 1):
            o_ref[i * LANES : last, j * LANES : (j + 1) * LANES] = done[i][j][: last - i * LANES]
    for tile in range(blocks, tiles):
        o_ref[:, tile * LANES : (tile + 1) * LANES] = a_ref[tile, :rows, :]


def order_kernel(rows, groups, pieces, pad_rows, tiles, x_ref, own_ref, left_ref, far0_ref, far1_ref, right_ref, o_ref, s_ref):
    per = rows // (groups * pieces)
    half = pieces // 2
    x = x_ref[0]
    for tile in range(tiles):
        for ref, back, first, count in (
            (own_ref, 0, 0, pieces),
            (left_ref, 1, 0, pieces),
            (far0_ref, 2, 0, half),
            (far1_ref, 2, half, half),
            (right_ref, 3, 0, pieces),
        ):
            base = (lax.rem(x + groups - back, groups) * pieces + first) * per

            def move(row, carry, ref=ref, base=base, count=count):
                s_ref[pl.ds(base + row, count, stride=per), :] = ref[
                    pl.ds(row * tiles + tile, count, stride=pad_rows), :
                ]
                return carry

            lax.fori_loop(0, per, move, 0, unroll=6)
        o_ref[:, tile * LANES : (tile + 1) * LANES] = s_ref[...]


def pack_kernel(core_ref, own_ref, other_ref, o_ref):
    core = core_ref[0]
    rows = own_ref.shape[0]
    for start in range(0, rows, 192):
        here = slice(start, start + 192)
        high, low = halves(own_ref[here, :])
        o_ref[core, 0, here, :] = high
        o_ref[core, 1, here, :] = low
        high, low = halves(other_ref[here, :])
        o_ref[1 - core, 0, here, :] = high
        o_ref[1 - core, 1, here, :] = low


def solve(state, e_ref, x_ref, rows):
    wide = 640
    step = rows // 3

    def put_first(index, value):
        x_ref[pl.ds(pl.multiple_of(index * step, step), step), :] = value

    def put_second(index, value):
        x_ref[pl.ds(pl.multiple_of(rows + index * step, step), step), :] = value

    def take(index, value):
        here = pl.ds(pl.multiple_of(rows + index * step, step), step)
        state[here, :] = state[here, :] - value

    def product(left, right, put):
        def part(index, carry):
            here = pl.ds(pl.multiple_of(index * step, step), step)
            total = None
            for (which, start, size), operand in zip(left, right):
                pair = e_ref[which, 0, here, start : start + size], e_ref[which, 1, here, start : start + size]
                term = three_dot(pair, operand)
                total = term if total is None else total + term
            put(index, total)
            return carry

        lax.fori_loop(0, 3, part, 0)

    half, link = rows // 2, e_ref.shape[3] - wide
    product([(0, 0, wide)], [split_right(state[0:wide, :])], put_first)
    tail = jnp.concatenate([x_ref[half:rows, :], jnp.zeros((link - half, LANES), jnp.float32)], axis=0)
    head = x_ref[0:link, :]
    product([(1, wide, link), (0, wide, link)], [split_right(head), split_right(tail)], take)
    product([(1, 0, wide)], [split_right(state[rows : rows + wide, :])], put_second)


def place_kernel(got_ref, place_ref, *outs):
    cores, _, rows = got_ref.shape
    for core in range(cores):
        for index, out in enumerate(outs):
            out[core * rows : (core + 1) * rows, :] = lax.dot_general(
                got_ref[core],
                place_ref[:, index * LANES : (index + 1) * LANES],
                (((0,), (0,)), ((), ())),
                precision=HI,
                preferred_element_type=jnp.float32,
            )


def load_state(state, r_ref, span):
    state[0:span, :] = r_ref[...]
    state[span:, :] = jnp.zeros((state.shape[0] - span, LANES), jnp.float32)


def subtract(state, l_ref, x_ref):
    x = split_right(x_ref[...])
    cores, _, rows, _ = l_ref.shape
    step = rows // 2

    def part(index, carry):
        core, piece = index // 2, index % 2
        here = pl.ds(pl.multiple_of(piece * step, step), step)
        there = pl.ds(pl.multiple_of(index * step, step), step)
        state[there, :] = state[there, :] - three_dot((l_ref[core, 0, here, :], l_ref[core, 1, here, :]), x)
        return carry

    lax.fori_loop(0, 2 * cores, part, 0)


def pick(plane, first, first_ref, second, second_ref, to_ref):
    @pl.when(plane == first)
    def _():
        to_ref[...] = first_ref[...]

    @pl.when(plane == second)
    def _():
        to_ref[...] = second_ref[...]


def stage_kernel(rows, number, plane_ref, *refs):
    plane = plane_ref[0]
    span = 2 * rows
    e_ref, refs = refs[0], refs[1:]
    a_ref, refs = (refs[0], refs[1:]) if number in (1, 2) else (None, refs)
    b_ref, refs = (refs[0], refs[1:]) if number >= 2 else (None, refs)
    r_ref, refs = refs[0], refs[1:]
    arrived = refs[: (0, 2, 3, 2)[number]]
    outs = refs[len(arrived) : len(arrived) + (2 if number == 1 else 1)]
    state, seen = refs[len(arrived) + len(outs) :]
    x_ref = outs[-1]
    other = {1: 3, 2: 0}.get(number)
    works = plane == number if other is None else (plane == number) | (plane == other)

    @pl.when(works)
    def _():
        load_state(state, r_ref, span)
        if number in (1, 2):
            pick(plane, number, arrived[0], other, arrived[1], seen)
            if number == 2:

                @pl.when(plane == 0)
                def _():
                    state[...] = jnp.zeros_like(state)

            subtract(state, a_ref, seen)
        if number == 3:
            state[0:span, :] = state[0:span, :] + arrived[0][...]

    if number == 1:
        outs[0][...] = jnp.where(plane == 3, state[0:span, :], r_ref[...])

    @pl.when(plane == number)
    def _():
        if number >= 2:
            subtract(state, b_ref, arrived[-1])
        solve(state, e_ref, x_ref, rows)

    if number == 2:

        @pl.when(plane == 0)
        def _():
            x_ref[...] = state[0:span, :]

        @pl.when((plane == 1) | (plane == 3))
        def _():
            x_ref[...] = jnp.zeros_like(x_ref)
    else:

        @pl.when(plane != number)
        def _():
            x_ref[...] = jnp.zeros_like(x_ref)


def per_device(factor, right_side, occ_order, cabs_order):
    planes, cores = lax.axis_size("y"), lax.axis_size("core")
    plane, core = lax.axis_index("y"), lax.axis_index("core")
    pieces = lax.axis_size("x") * lax.axis_size("z")
    per, aux = factor.shape
    rows = per * pieces
    span = cores * rows
    occ_total, cabs_total = occ_order.shape[0], cabs_order.shape[0]
    cabs_local = right_side.shape[1] // occ_total
    cheap = pl.CostEstimate(flops=1000, bytes_accessed=1000, transcendentals=0)
    small = pltpu.CompilerParams(vmem_limit_bytes=8 * 1024 * 1024)
    large = pltpu.CompilerParams(vmem_limit_bytes=24 * 1024 * 1024)

    slots = occ_order.reshape(pieces, cores).T.reshape(occ_total)
    pick = (jnp.arange(cabs_local, dtype=jnp.int32)[None, :] * occ_total + slots[:, None]).reshape(-1, 1)
    spread = (pick == jnp.arange(right_side.shape[1], dtype=jnp.int32)[None, :]).astype(jnp.float32)
    sent = lax.dot_general(spread, right_side, (((1,), (1,)), ((), ())), precision=HI, preferred_element_type=jnp.float32)
    sent = sent.reshape(occ_total, cabs_local, rows)

    swap = [(0, 1), (1, 0)]
    x_arg = lax.axis_index("x").reshape(1).astype(jnp.int32)
    smem = pl.BlockSpec(memory_space=pltpu.SMEM)
    here = pl.BlockSpec(memory_space=pltpu.VMEM)
    zs, xs = lax.axis_size("z"), lax.axis_size("x")
    diag = lax.dynamic_slice_in_dim(factor, plane * span, span, 1)
    low, high = diag[:, :rows], diag[:, rows:]
    half = rows // 2
    gap, short = jnp.zeros((per, 640 - rows), jnp.float32), jnp.zeros((per, 384 - half), jnp.float32)
    lent = lax.ppermute(low[:, half:], "core", [(1, 0)])
    diag = jnp.where(
        core == 0,
        jnp.concatenate([low, gap, lent, short], axis=1),
        jnp.concatenate([high, gap, low[:, :half], short], axis=1),
    )
    tiles = diag.shape[1] // LANES

    def spread(part):
        copies = jnp.broadcast_to(part[None], (zs, *part.shape))
        return lax.all_to_all(copies, "z", 0, 0, tiled=True).reshape(zs * part.shape[0], LANES)

    piece, sent = lax.optimization_barrier((diag.reshape(per * tiles, LANES), sent))
    near = spread(piece)
    ahead = [(i, (i + 1) % xs) for i in range(xs)]
    behind = [(i, (i - 1) % xs) for i in range(xs)]

    def flat(block):
        return jnp.pad(block.reshape(per * ltiles, LANES), ((0, lpad - per * ltiles), (0, 0)))

    ltiles = span // LANES
    lpad = (per * ltiles + 7) // 8 * 8
    moved = lax.ppermute(factor[:, span : 2 * span], "y", [(3, 0)])
    flat_a = flat(jnp.where(plane == 0, moved, factor[:, :span]))
    flat_b = flat(lax.dynamic_slice_in_dim(factor, jnp.maximum(plane - 1, 0) * span, span, 1))
    near, sent = lax.optimization_barrier((near, sent))
    got = lax.all_to_all(sent, ("core", "x", "z"), 0, 0, tiled=True)
    left, right = lax.ppermute(near, "x", ahead), lax.ppermute(near, "x", behind)
    left, right, flat_a, flat_b = lax.optimization_barrier((left, right, flat_a, flat_b))
    near_a = spread(flat_a)

    def far(left, right):
        middle = left.shape[0] // 2
        return lax.ppermute(left[:middle], "x", ahead), lax.ppermute(right[middle:], "x", behind)

    far0, far1 = far(left, right)
    near_b = spread(flat_b)
    far0, far1, got, near_a = lax.optimization_barrier((far0, far1, got, near_a))
    left_a, right_a = lax.ppermute(near_a, "x", ahead), lax.ppermute(near_a, "x", behind)
    got = got.reshape(cores, cabs_total, rows)
    place = (jnp.arange(cabs_total, dtype=jnp.int32)[:, None] == cabs_order[None, :]).astype(jnp.float32)
    states = list(pl.pallas_call(
        place_kernel,
        out_shape=(jax.ShapeDtypeStruct((span, LANES), jnp.float32),) * (cabs_total // LANES),
        in_specs=[here, here],
        out_specs=(here,) * (cabs_total // LANES),
        compiler_params=small,
        cost_estimate=cheap,
        name="place",
    )(got, place))
    mine = pl.pallas_call(
        functools.partial(invert_kernel, rows, xs, zs, tiles),
        out_shape=jax.ShapeDtypeStruct((rows, tiles * LANES), jnp.float32),
        in_specs=[smem] + [here] * 5,
        out_specs=here,
        scratch_shapes=[pltpu.VMEM((tiles, 640, LANES), jnp.float32), pltpu.VMEM((5, LANES, LANES), jnp.float32)],
        compiler_params=pltpu.CompilerParams(vmem_limit_bytes=12 * 1024 * 1024),
        cost_estimate=cheap,
        name="invert",
    )(x_arg, near, left, far0, far1, right)
    theirs = lax.ppermute(mine, "core", swap)
    far0_a, far1_a = far(left_a, right_a)
    theirs, far0_a, far1_a, near_b = lax.optimization_barrier((theirs, far0_a, far1_a, near_b))
    left_b, right_b = lax.ppermute(near_b, "x", ahead), lax.ppermute(near_b, "x", behind)
    whole_a = near_a, left_a, far0_a, far1_a, right_a
    core_arg = core.reshape(1).astype(jnp.int32)
    plane_arg = plane.reshape(1).astype(jnp.int32)
    inverse = pl.pallas_call(
        pack_kernel,
        out_shape=jax.ShapeDtypeStruct((cores, 2, rows, tiles * LANES), jnp.bfloat16),
        in_specs=[smem, here, here],
        out_specs=here,
        compiler_params=small,
        cost_estimate=cheap,
        name="pack",
    )(core_arg, mine, theirs)

    def after(value, tokens):
        value, token = lax.optimization_barrier((value, sum(token[0, :1] for token in tokens)))
        return value, (token != token).astype(jnp.int32)

    def paired(own, zero):
        other = lax.ppermute(own, "core", swap)
        return pl.pallas_call(
            pack_kernel,
            out_shape=jax.ShapeDtypeStruct((cores, 2, *own.shape), jnp.bfloat16),
            in_specs=[smem, here, here],
            out_specs=here,
            compiler_params=small,
            cost_estimate=pl.CostEstimate(flops=1_000_000, bytes_accessed=8_000_000, transcendentals=0),
            name="pack",
        )(core_arg + zero, own, other)

    def ordered(pieces, tokens):
        _, zero = after(core_arg, tokens)
        own = pl.pallas_call(
            functools.partial(order_kernel, rows, xs, zs, lpad, ltiles),
            out_shape=jax.ShapeDtypeStruct((rows, span), jnp.float32),
            in_specs=[smem] + [here] * 5,
            out_specs=here,
            scratch_shapes=[pltpu.VMEM((rows, LANES), jnp.float32)],
            compiler_params=small,
            cost_estimate=pl.CostEstimate(flops=1_000_000, bytes_accessed=8_000_000, transcendentals=0),
            name="order",
        )(x_arg, *pieces)
        return paired(own, zero)

    block = jax.ShapeDtypeStruct((span, LANES), jnp.float32)

    def stage(number, *args):
        outs = 2 if number == 1 else 1
        return pl.pallas_call(
            functools.partial(stage_kernel, rows, number),
            out_shape=(block,) * outs,
            in_specs=[smem] + [here] * len(args),
            out_specs=(here,) * outs,
            scratch_shapes=[pltpu.VMEM((span + 64, LANES), jnp.float32), pltpu.VMEM((span, LANES), jnp.float32)],
            compiler_params=small,
            cost_estimate=pl.CostEstimate(flops=30_000_000_000, bytes_accessed=4_000_000, transcendentals=0),
            name=f"stage{number}",
        )(plane_arg, *args)

    def send(value, pairs):
        return lax.ppermute(value, "y", pairs)

    x0s, chunks = [], []
    for state in states:
        x0s += stage(0, inverse, state)
    a_mat = ordered(whole_a, x0s)
    left_b, right_b, token = lax.optimization_barrier((left_b, right_b, a_mat[0, 0, :1].astype(jnp.float32)))
    whole_b = near_b, left_b, *far(left_b, right_b), right_b
    x1s, nexts = [], []
    for index, (state, x0) in enumerate(zip(list(states), x0s)):
        to1, to3 = send(x0, [(0, 1)]), send(x0, [(0, 3)])
        to2 = send(to3, [(3, 2)])
        states[index], x1 = stage(1, inverse, a_mat, state, to1, to3)
        near_x, to0 = send(x1, [(1, 2)]), send(x1, [(1, 0)])
        x1s.append((x1, to2))
        nexts.append((near_x, to0))
    b_mat = ordered(whole_b, [x1 for x1, _ in x1s] + [token])
    for state, x0, (x1, to2), (near_x, to0) in zip(states, x0s, x1s, nexts):
        (x2,) = stage(2, inverse, a_mat, b_mat, state, to2, to0, near_x)
        part = send(x2, [(0, 3)])
        near_x = send(x2, [(2, 3)])
        (x3,) = stage(3, inverse, b_mat, state, part, near_x)
        chunks.append(jnp.where(plane == 0, x0, jnp.where(plane == 1, x1, jnp.where(plane == 2, x2, x3))))
    solved = jnp.concatenate([x.T for x in chunks], axis=0)
    keep = jnp.where(core == 0, solved[:, :rows], solved[:, rows:])
    give = jnp.where(core == 0, solved[:, rows:], solved[:, :rows])
    came = lax.ppermute(give, "core", [(0, 1), (1, 0)])
    return jnp.where(core == 0, jnp.stack([keep, came]), jnp.stack([came, keep]))


def solution(mesh):
    grid = Mesh(mesh.devices.reshape(4, 2, 4, 8), ("y", "core", "x", "z"))
    in_specs = (P(("y", "core", "x", "z"), None), P(("y", "core"), ("x", "z")), P(), P())
    out_specs = P(("x", "z"), None, ("y", "core"))
    return jax.shard_map(per_device, mesh=grid, in_specs=in_specs, out_specs=out_specs, check_vma=False)
```

```python
import functools
import jax
import jax.numpy as jnp
from jax import lax
from jax.experimental import pallas as pl
from jax.experimental.pallas import tpu as pltpu
from jax.sharding import Mesh, PartitionSpec as P

HI = lax.Precision.HIGHEST
LANES = 128


def full_dot(left, right):
    return jnp.dot(left, right, precision=HI, preferred_element_type=jnp.float32)


def halves(value):
    high = value.astype(jnp.bfloat16)
    return high, (value - high.astype(jnp.float32)).astype(jnp.bfloat16)


def split_right(value):
    high, low = halves(value)
    return jnp.concatenate([high, low], axis=1), high


def three_dot(left, right):
    lh, ll = left
    both, rh = right
    dot = functools.partial(jnp.dot, preferred_element_type=jnp.float32)
    wide = dot(lh, both)
    return wide[:, :LANES] + (wide[:, LANES:] + dot(ll, rh))


def invert_kernel(rows, groups, pieces, tiles, x_ref, own_ref, left_ref, far0_ref, far1_ref, right_ref, o_ref, a_ref, m_ref):
    per = rows // (groups * pieces)
    wide = 640
    blocks = wide // LANES
    x = x_ref[0]
    half = pieces // 2
    for ref, back, first, count in (
        (own_ref, 0, 0, pieces),
        (left_ref, 1, 0, pieces),
        (far0_ref, 2, 0, half),
        (far1_ref, 2, half, half),
        (right_ref, 3, 0, pieces),
    ):
        base = (lax.rem(x + groups - back, groups) * pieces + first) * per
        for tile in range(tiles):
            for row in range(per):
                a_ref[tile, pl.ds(base + row, count, stride=per), :] = ref[
                    pl.ds(row * tiles + tile, count, stride=per * tiles), :
                ]
    extra = wide - rows
    r0 = lax.broadcasted_iota(jnp.int32, (extra, LANES), 0)
    c0 = lax.broadcasted_iota(jnp.int32, (extra, LANES), 1)
    for tile in range(blocks - 1):
        a_ref[tile, rows:wide, :] = jnp.zeros((extra, LANES), jnp.float32)
    a_ref[blocks - 1, rows:wide, :] = jnp.where(c0 == r0 + (LANES - extra), 1.0, 0.0)
    ri = lax.broadcasted_iota(jnp.int32, (LANES, LANES), 0)
    ci = lax.broadcasted_iota(jnp.int32, (LANES, LANES), 1)

    def block(i, j):
        return a_ref[j, i * LANES : (i + 1) * LANES, :]

    for i in range(blocks):
        m_ref[i] = jnp.where(ri == ci, 1.0 / jnp.where(ri == ci, block(i, i), 1.0), 0.0)

    def double(level, carry):
        rb, cb = ri >> level, ci >> level
        take = (rb >> 1 == cb >> 1) & (rb == cb + 1)
        mids = [full_dot(jnp.where(take, block(i, i), 0.0), m_ref[i]) for i in range(blocks)]
        news = [m_ref[i] - full_dot(m_ref[i], mids[i]) for i in range(blocks)]
        for i in range(blocks):
            m_ref[i] = news[i]
        return carry

    lax.fori_loop(0, 7, double, 0)
    inv = [m_ref[i] for i in range(blocks)]
    for i in range(blocks):
        for j in range(blocks):
            last = min((i + 1) * LANES, rows)
            if j > i:
                o_ref[i * LANES : last, j * LANES : (j + 1) * LANES] = jnp.zeros((last - i * LANES, LANES), jnp.float32)
    done = [[None] * blocks for _ in range(blocks)]
    for i in range(blocks):
        done[i][i] = inv[i]
        last = min((i + 1) * LANES, rows)
        for j in range(i):
            total = full_dot(block(i, j), done[j][j])
            for k in range(j + 1, i):
                total = total + full_dot(block(i, k), done[k][j])
            done[i][j] = -full_dot(inv[i], total)
        for j in range(i + 1):
            o_ref[i * LANES : last, j * LANES : (j + 1) * LANES] = done[i][j][: last - i * LANES]
    for tile in range(blocks, tiles):
        o_ref[:, tile * LANES : (tile + 1) * LANES] = a_ref[tile, :rows, :]


def order_kernel(rows, pieces, pad_rows, first, tiles, whole_ref, o_ref, s_ref):
    per = rows // pieces
    for tile in range(tiles):

        def move(row, carry):
            s_ref[pl.ds(row, pieces, stride=per), :] = whole_ref[
                pl.ds(first + row * tiles + tile, pieces, stride=pad_rows), :
            ]
            return carry

        lax.fori_loop(0, per, move, 0, unroll=6)
        o_ref[:, tile * LANES : (tile + 1) * LANES] = s_ref[...]


def pack_kernel(core_ref, own_ref, other_ref, o_ref):
    core = core_ref[0]
    rows = own_ref.shape[0]
    for start in range(0, rows, 192):
        here = slice(start, start + 192)
        high, low = halves(own_ref[here, :])
        o_ref[core, 0, here, :] = high
        o_ref[core, 1, here, :] = low
        high, low = halves(other_ref[here, :])
        o_ref[1 - core, 0, here, :] = high
        o_ref[1 - core, 1, here, :] = low


def solve(state, e_ref, x_ref, rows):
    wide = 640
    step = rows // 3

    def put_first(index, value):
        x_ref[pl.ds(pl.multiple_of(index * step, step), step), :] = value

    def put_second(index, value):
        x_ref[pl.ds(pl.multiple_of(rows + index * step, step), step), :] = value

    def take(index, value):
        here = pl.ds(pl.multiple_of(rows + index * step, step), step)
        state[here, :] = state[here, :] - value

    def product(left, right, put):
        def part(index, carry):
            here = pl.ds(pl.multiple_of(index * step, step), step)
            total = None
            for (which, start, size), operand in zip(left, right):
                pair = e_ref[which, 0, here, start : start + size], e_ref[which, 1, here, start : start + size]
                term = three_dot(pair, operand)
                total = term if total is None else total + term
            put(index, total)
            return carry

        lax.fori_loop(0, 3, part, 0)

    half, link = rows // 2, e_ref.shape[3] - wide
    product([(0, 0, wide)], [split_right(state[0:wide, :])], put_first)
    tail = jnp.concatenate([x_ref[half:rows, :], jnp.zeros((link - half, LANES), jnp.float32)], axis=0)
    head = x_ref[0:link, :]
    product([(1, wide, link), (0, wide, link)], [split_right(head), split_right(tail)], take)
    product([(1, 0, wide)], [split_right(state[rows : rows + wide, :])], put_second)


def place_kernel(got_ref, place_ref, *outs):
    cores, _, rows = got_ref.shape
    for core in range(cores):
        for index, out in enumerate(outs):
            out[core * rows : (core + 1) * rows, :] = lax.dot_general(
                got_ref[core],
                place_ref[:, index * LANES : (index + 1) * LANES],
                (((0,), (0,)), ((), ())),
                precision=HI,
                preferred_element_type=jnp.float32,
            )


def load_state(state, r_ref, span):
    state[0:span, :] = r_ref[...]
    state[span:, :] = jnp.zeros((state.shape[0] - span, LANES), jnp.float32)


def subtract(state, l_ref, x_ref):
    x = split_right(x_ref[...])
    cores, _, rows, _ = l_ref.shape
    step = rows // 2

    def part(index, carry):
        core, piece = index // 2, index % 2
        here = pl.ds(pl.multiple_of(piece * step, step), step)
        there = pl.ds(pl.multiple_of(index * step, step), step)
        state[there, :] = state[there, :] - three_dot((l_ref[core, 0, here, :], l_ref[core, 1, here, :]), x)
        return carry

    lax.fori_loop(0, 2 * cores, part, 0)


def pick(plane, first, first_ref, second, second_ref, to_ref):
    @pl.when(plane == first)
    def _():
        to_ref[...] = first_ref[...]

    @pl.when(plane == second)
    def _():
        to_ref[...] = second_ref[...]


def stage_kernel(rows, number, plane_ref, *refs):
    plane = plane_ref[0]
    span = 2 * rows
    e_ref, refs = refs[0], refs[1:]
    a_ref, refs = (refs[0], refs[1:]) if number in (1, 2) else (None, refs)
    b_ref, refs = (refs[0], refs[1:]) if number >= 2 else (None, refs)
    r_ref, refs = refs[0], refs[1:]
    arrived = refs[: (0, 2, 3, 2)[number]]
    outs = refs[len(arrived) : len(arrived) + (2 if number == 1 else 1)]
    state, seen = refs[len(arrived) + len(outs) :]
    x_ref = outs[-1]
    other = {1: 3, 2: 0}.get(number)
    works = plane == number if other is None else (plane == number) | (plane == other)

    @pl.when(works)
    def _():
        load_state(state, r_ref, span)
        if number in (1, 2):
            pick(plane, number, arrived[0], other, arrived[1], seen)
            if number == 2:

                @pl.when(plane == 0)
                def _():
                    state[...] = jnp.zeros_like(state)

            subtract(state, a_ref, seen)
        if number == 3:
            state[0:span, :] = state[0:span, :] + arrived[0][...]

    if number == 1:
        outs[0][...] = jnp.where(plane == 3, state[0:span, :], r_ref[...])

    @pl.when(plane == number)
    def _():
        if number >= 2:
            subtract(state, b_ref, arrived[-1])
        solve(state, e_ref, x_ref, rows)

    if number == 2:

        @pl.when(plane == 0)
        def _():
            x_ref[...] = state[0:span, :]

        @pl.when((plane == 1) | (plane == 3))
        def _():
            x_ref[...] = jnp.zeros_like(x_ref)
    else:

        @pl.when(plane != number)
        def _():
            x_ref[...] = jnp.zeros_like(x_ref)


def per_device(factor, right_side, occ_order, cabs_order):
    planes, cores = lax.axis_size("y"), lax.axis_size("core")
    plane, core = lax.axis_index("y"), lax.axis_index("core")
    pieces = lax.axis_size("x") * lax.axis_size("z")
    per, aux = factor.shape
    rows = per * pieces
    span = cores * rows
    occ_total, cabs_total = occ_order.shape[0], cabs_order.shape[0]
    cabs_local = right_side.shape[1] // occ_total
    cheap = pl.CostEstimate(flops=1000, bytes_accessed=1000, transcendentals=0)
    small = pltpu.CompilerParams(vmem_limit_bytes=8 * 1024 * 1024)
    large = pltpu.CompilerParams(vmem_limit_bytes=24 * 1024 * 1024)

    slots = occ_order.reshape(pieces, cores).T.reshape(occ_total)
    pick = (jnp.arange(cabs_local, dtype=jnp.int32)[None, :] * occ_total + slots[:, None]).reshape(-1, 1)
    spread = (pick == jnp.arange(right_side.shape[1], dtype=jnp.int32)[None, :]).astype(jnp.float32)
    sent = lax.dot_general(spread, right_side, (((1,), (1,)), ((), ())), precision=HI, preferred_element_type=jnp.float32)
    sent = sent.reshape(occ_total, cabs_local, rows)

    swap = [(0, 1), (1, 0)]
    x_arg = lax.axis_index("x").reshape(1).astype(jnp.int32)
    smem = pl.BlockSpec(memory_space=pltpu.SMEM)
    here = pl.BlockSpec(memory_space=pltpu.VMEM)
    zs, xs = lax.axis_size("z"), lax.axis_size("x")
    diag = lax.dynamic_slice_in_dim(factor, plane * span, span, 1)
    low, high = diag[:, :rows], diag[:, rows:]
    half = rows // 2
    gap, short = jnp.zeros((per, 640 - rows), jnp.float32), jnp.zeros((per, 384 - half), jnp.float32)
    lent = lax.ppermute(low[:, half:], "core", [(1, 0)])
    diag = jnp.where(
        core == 0,
        jnp.concatenate([low, gap, lent, short], axis=1),
        jnp.concatenate([high, gap, low[:, :half], short], axis=1),
    )
    tiles = diag.shape[1] // LANES

    def spread(part):
        copies = jnp.broadcast_to(part[None], (zs, *part.shape))
        return lax.all_to_all(copies, "z", 0, 0, tiled=True).reshape(zs * part.shape[0], LANES)

    got = lax.all_to_all(sent, ("core", "x", "z"), 0, 0, tiled=True)
    marker = lax.ppermute(sent[:1, :, :LANES], "core", swap)
    piece, marker = lax.optimization_barrier((diag.reshape(per * tiles, LANES), marker))
    x_arg = x_arg + (marker[0, 0, :1] != marker[0, 0, :1]).astype(jnp.int32)
    near = spread(piece)
    ahead = [(i, (i + 1) % xs) for i in range(xs)]
    behind = [(i, (i - 1) % xs) for i in range(xs)]

    def flat(block):
        return jnp.pad(block.reshape(per * ltiles, LANES), ((0, lpad - per * ltiles), (0, 0)))

    ltiles = span // LANES
    lpad = (per * ltiles + 7) // 8 * 8
    moved = lax.ppermute(factor[:, span : 2 * span], "y", [(3, 0)])
    flat_a = flat(jnp.where(plane == 0, moved, factor[:, :span]))
    flat_b = flat(lax.dynamic_slice_in_dim(factor, jnp.maximum(plane - 1, 0) * span, span, 1))
    left, right = lax.ppermute(near, "x", ahead), lax.ppermute(near, "x", behind)
    whole = lax.all_gather(jnp.concatenate([flat_a, flat_b]), ("x", "z"), axis=0, tiled=True)

    def far(left, right):
        middle = left.shape[0] // 2
        return lax.ppermute(left[:middle], "x", ahead), lax.ppermute(right[middle:], "x", behind)

    far0, far1 = far(left, right)
    far0, far1, got = lax.optimization_barrier((far0, far1, got))
    got = got.reshape(cores, cabs_total, rows)
    place = (jnp.arange(cabs_total, dtype=jnp.int32)[:, None] == cabs_order[None, :]).astype(jnp.float32)
    states = list(pl.pallas_call(
        place_kernel,
        out_shape=(jax.ShapeDtypeStruct((span, LANES), jnp.float32),) * (cabs_total // LANES),
        in_specs=[here, here],
        out_specs=(here,) * (cabs_total // LANES),
        compiler_params=small,
        cost_estimate=cheap,
        name="place",
    )(got, place))
    mine = pl.pallas_call(
        functools.partial(invert_kernel, rows, xs, zs, tiles),
        out_shape=jax.ShapeDtypeStruct((rows, tiles * LANES), jnp.float32),
        in_specs=[smem] + [here] * 5,
        out_specs=here,
        scratch_shapes=[pltpu.VMEM((tiles, 640, LANES), jnp.float32), pltpu.VMEM((5, LANES, LANES), jnp.float32)],
        compiler_params=pltpu.CompilerParams(vmem_limit_bytes=12 * 1024 * 1024),
        cost_estimate=cheap,
        name="invert",
    )(x_arg, near, left, far0, far1, right)
    theirs = lax.ppermute(mine, "core", swap)
    core_arg = core.reshape(1).astype(jnp.int32)
    plane_arg = plane.reshape(1).astype(jnp.int32)
    inverse = pl.pallas_call(
        pack_kernel,
        out_shape=jax.ShapeDtypeStruct((cores, 2, rows, tiles * LANES), jnp.bfloat16),
        in_specs=[smem, here, here],
        out_specs=here,
        compiler_params=small,
        cost_estimate=cheap,
        name="pack",
    )(core_arg, mine, theirs)

    def after(value, tokens):
        value, token = lax.optimization_barrier((value, sum(token[0, :1] for token in tokens)))
        return value, (token != token).astype(jnp.int32)

    def paired(own, zero):
        other = lax.ppermute(own, "core", swap)
        return pl.pallas_call(
            pack_kernel,
            out_shape=jax.ShapeDtypeStruct((cores, 2, *own.shape), jnp.bfloat16),
            in_specs=[smem, here, here],
            out_specs=here,
            compiler_params=small,
            cost_estimate=pl.CostEstimate(flops=1_000_000, bytes_accessed=8_000_000, transcendentals=0),
            name="pack",
        )(core_arg + zero, own, other)

    def ordered(which, whole, zero):
        own = pl.pallas_call(
            functools.partial(order_kernel, rows, pieces, 2 * lpad, which * lpad, ltiles),
            out_shape=jax.ShapeDtypeStruct((rows, span), jnp.float32),
            in_specs=[here],
            out_specs=here,
            scratch_shapes=[pltpu.VMEM((rows, LANES), jnp.float32)],
            compiler_params=small,
            cost_estimate=pl.CostEstimate(flops=1_000_000, bytes_accessed=8_000_000, transcendentals=0),
            name="order",
        )(whole)
        return paired(own, zero)

    block = jax.ShapeDtypeStruct((span, LANES), jnp.float32)

    def stage(number, *args):
        outs = 2 if number == 1 else 1
        return pl.pallas_call(
            functools.partial(stage_kernel, rows, number),
            out_shape=(block,) * outs,
            in_specs=[smem] + [here] * len(args),
            out_specs=(here,) * outs,
            scratch_shapes=[pltpu.VMEM((span + 64, LANES), jnp.float32), pltpu.VMEM((span, LANES), jnp.float32)],
            compiler_params=small,
            cost_estimate=pl.CostEstimate(flops=30_000_000_000, bytes_accessed=4_000_000, transcendentals=0),
            name=f"stage{number}",
        )(plane_arg, *args)

    def send(value, pairs):
        return lax.ppermute(value, "y", pairs)

    x0s, chunks = [], []
    for state in states:
        x0s += stage(0, inverse, state)
    firsts = [(send(x0, [(0, 1)]), send(x0, [(0, 3)])) for x0 in x0s]
    whole, zero = after(whole, [*firsts[0], x0s[-1]])
    a_mat = ordered(0, whole, zero)
    x1s, nexts = [], []
    for index, (state, (to1, to3)) in enumerate(zip(list(states), firsts)):
        to2 = send(to3, [(3, 2)])
        states[index], x1 = stage(1, inverse, a_mat, state, to1, to3)
        near_x, to0 = send(x1, [(1, 2)]), send(x1, [(1, 0)])
        x1s.append((x1, to2))
        nexts.append((near_x, to0))
    _, zero = after(core_arg, [x1 for x1, _ in x1s])
    b_mat = ordered(1, whole, zero)
    for state, x0, (x1, to2), (near_x, to0) in zip(states, x0s, x1s, nexts):
        (x2,) = stage(2, inverse, a_mat, b_mat, state, to2, to0, near_x)
        part = send(x2, [(0, 3)])
        near_x = send(x2, [(2, 3)])
        (x3,) = stage(3, inverse, b_mat, state, part, near_x)
        chunks.append(jnp.where(plane == 0, x0, jnp.where(plane == 1, x1, jnp.where(plane == 2, x2, x3))))
    solved = jnp.concatenate([x.T for x in chunks], axis=0)
    keep = jnp.where(core == 0, solved[:, :rows], solved[:, rows:])
    give = jnp.where(core == 0, solved[:, rows:], solved[:, :rows])
    came = lax.ppermute(give, "core", [(0, 1), (1, 0)])
    return jnp.where(core == 0, jnp.stack([keep, came]), jnp.stack([came, keep]))


def solution(mesh):
    grid = Mesh(mesh.devices.reshape(4, 2, 4, 8), ("y", "core", "x", "z"))
    in_specs = (P(("y", "core", "x", "z"), None), P(("y", "core"), ("x", "z")), P(), P())
    out_specs = P(("x", "z"), None, ("y", "core"))
    return jax.shard_map(per_device, mesh=grid, in_specs=in_specs, out_specs=out_specs, check_vma=False)
```

```python
import functools
import jax
import jax.numpy as jnp
from jax import lax
from jax.experimental import pallas as pl
from jax.experimental.pallas import tpu as pltpu
from jax.sharding import Mesh, PartitionSpec as P

HI = lax.Precision.HIGHEST
LANES = 128


def full_dot(left, right):
    return jnp.dot(left, right, precision=HI, preferred_element_type=jnp.float32)


def halves(value):
    high = value.astype(jnp.bfloat16)
    return high, (value - high.astype(jnp.float32)).astype(jnp.bfloat16)


def split_right(value):
    high, low = halves(value)
    return jnp.concatenate([high, low], axis=1), high


def three_dot(left, right):
    lh, ll = left
    both, rh = right
    dot = functools.partial(jnp.dot, preferred_element_type=jnp.float32)
    wide = dot(lh, both)
    return wide[:, :LANES] + (wide[:, LANES:] + dot(ll, rh))


def invert_kernel(rows, groups, pieces, tiles, x_ref, own_ref, left_ref, far0_ref, far1_ref, right_ref, o_ref, a_ref, m_ref):
    per = rows // (groups * pieces)
    wide = 640
    blocks = wide // LANES
    x = x_ref[0]
    half = pieces // 2
    for ref, back, first, count in (
        (own_ref, 0, 0, pieces),
        (left_ref, 1, 0, pieces),
        (far0_ref, 2, 0, half),
        (far1_ref, 2, half, half),
        (right_ref, 3, 0, pieces),
    ):
        base = (lax.rem(x + groups - back, groups) * pieces + first) * per
        for tile in range(tiles):
            for row in range(per):
                a_ref[tile, pl.ds(base + row, count, stride=per), :] = ref[
                    pl.ds(row * tiles + tile, count, stride=per * tiles), :
                ]
    extra = wide - rows
    r0 = lax.broadcasted_iota(jnp.int32, (extra, LANES), 0)
    c0 = lax.broadcasted_iota(jnp.int32, (extra, LANES), 1)
    for tile in range(blocks - 1):
        a_ref[tile, rows:wide, :] = jnp.zeros((extra, LANES), jnp.float32)
    a_ref[blocks - 1, rows:wide, :] = jnp.where(c0 == r0 + (LANES - extra), 1.0, 0.0)
    ri = lax.broadcasted_iota(jnp.int32, (LANES, LANES), 0)
    ci = lax.broadcasted_iota(jnp.int32, (LANES, LANES), 1)

    def block(i, j):
        return a_ref[j, i * LANES : (i + 1) * LANES, :]

    for i in range(blocks):
        m_ref[i] = jnp.where(ri == ci, 1.0 / jnp.where(ri == ci, block(i, i), 1.0), 0.0)

    def double(level, carry):
        rb, cb = ri >> level, ci >> level
        take = (rb >> 1 == cb >> 1) & (rb == cb + 1)
        mids = [full_dot(jnp.where(take, block(i, i), 0.0), m_ref[i]) for i in range(blocks)]
        news = [m_ref[i] - full_dot(m_ref[i], mids[i]) for i in range(blocks)]
        for i in range(blocks):
            m_ref[i] = news[i]
        return carry

    lax.fori_loop(0, 7, double, 0)
    inv = [m_ref[i] for i in range(blocks)]
    for i in range(blocks):
        for j in range(blocks):
            last = min((i + 1) * LANES, rows)
            if j > i:
                o_ref[i * LANES : last, j * LANES : (j + 1) * LANES] = jnp.zeros((last - i * LANES, LANES), jnp.float32)
    done = [[None] * blocks for _ in range(blocks)]
    for i in range(blocks):
        done[i][i] = inv[i]
        last = min((i + 1) * LANES, rows)
        for j in range(i):
            total = full_dot(block(i, j), done[j][j])
            for k in range(j + 1, i):
                total = total + full_dot(block(i, k), done[k][j])
            done[i][j] = -full_dot(inv[i], total)
        for j in range(i + 1):
            o_ref[i * LANES : last, j * LANES : (j + 1) * LANES] = done[i][j][: last - i * LANES]
    for tile in range(blocks, tiles):
        o_ref[:, tile * LANES : (tile + 1) * LANES] = a_ref[tile, :rows, :]


def order_kernel(rows, pieces, pad_rows, tiles, whole_ref, o_ref, s_ref):
    per = rows // pieces
    whole_ref = whole_ref.reshape(pieces * pad_rows, LANES)
    for tile in range(tiles):

        def move(row, carry):
            s_ref[pl.ds(row, pieces, stride=per), :] = whole_ref[
                pl.ds(row * tiles + tile, pieces, stride=pad_rows), :
            ]
            return carry

        lax.fori_loop(0, per, move, 0, unroll=6)
        o_ref[:, tile * LANES : (tile + 1) * LANES] = s_ref[...]


def pack_kernel(core_ref, own_ref, other_ref, o_ref):
    core = core_ref[0]
    rows = own_ref.shape[0]
    for start in range(0, rows, 192):
        here = slice(start, start + 192)
        high, low = halves(own_ref[here, :])
        o_ref[core, 0, here, :] = high
        o_ref[core, 1, here, :] = low
        high, low = halves(other_ref[here, :])
        o_ref[1 - core, 0, here, :] = high
        o_ref[1 - core, 1, here, :] = low


def solve(state, e_ref, x_ref, rows):
    wide = 640
    step = rows // 3

    def put_first(index, value):
        x_ref[pl.ds(pl.multiple_of(index * step, step), step), :] = value

    def put_second(index, value):
        x_ref[pl.ds(pl.multiple_of(rows + index * step, step), step), :] = value

    def take(index, value):
        here = pl.ds(pl.multiple_of(rows + index * step, step), step)
        state[here, :] = state[here, :] - value

    def product(left, right, put):
        def part(index, carry):
            here = pl.ds(pl.multiple_of(index * step, step), step)
            total = None
            for (which, start, size), operand in zip(left, right):
                pair = e_ref[which, 0, here, start : start + size], e_ref[which, 1, here, start : start + size]
                term = three_dot(pair, operand)
                total = term if total is None else total + term
            put(index, total)
            return carry

        lax.fori_loop(0, 3, part, 0)

    half, link = rows // 2, e_ref.shape[3] - wide
    product([(0, 0, wide)], [split_right(state[0:wide, :])], put_first)
    tail = jnp.concatenate([x_ref[half:rows, :], jnp.zeros((link - half, LANES), jnp.float32)], axis=0)
    head = x_ref[0:link, :]
    product([(1, wide, link), (0, wide, link)], [split_right(head), split_right(tail)], take)
    product([(1, 0, wide)], [split_right(state[rows : rows + wide, :])], put_second)


def place_kernel(got_ref, place_ref, *outs):
    cores, _, rows = got_ref.shape
    for core in range(cores):
        for index, out in enumerate(outs):
            out[core * rows : (core + 1) * rows, :] = lax.dot_general(
                got_ref[core],
                place_ref[:, index * LANES : (index + 1) * LANES],
                (((0,), (0,)), ((), ())),
                precision=HI,
                preferred_element_type=jnp.float32,
            )


def load_state(state, r_ref, span):
    state[0:span, :] = r_ref[...]
    state[span:, :] = jnp.zeros((state.shape[0] - span, LANES), jnp.float32)


def subtract(state, l_ref, x_ref):
    x = split_right(x_ref[...])
    cores, _, rows, _ = l_ref.shape
    step = rows // 2

    def part(index, carry):
        core, piece = index // 2, index % 2
        here = pl.ds(pl.multiple_of(piece * step, step), step)
        there = pl.ds(pl.multiple_of(index * step, step), step)
        state[there, :] = state[there, :] - three_dot((l_ref[core, 0, here, :], l_ref[core, 1, here, :]), x)
        return carry

    lax.fori_loop(0, 2 * cores, part, 0)


def pick(plane, first, first_ref, second, second_ref, to_ref):
    @pl.when(plane == first)
    def _():
        to_ref[...] = first_ref[...]

    @pl.when(plane == second)
    def _():
        to_ref[...] = second_ref[...]


def stage_kernel(rows, number, plane_ref, *refs):
    plane = plane_ref[0]
    span = 2 * rows
    e_ref, refs = refs[0], refs[1:]
    a_ref, refs = (refs[0], refs[1:]) if number in (1, 2) else (None, refs)
    b_ref, refs = (refs[0], refs[1:]) if number >= 2 else (None, refs)
    r_ref, refs = refs[0], refs[1:]
    arrived = refs[: (0, 2, 3, 2)[number]]
    outs = refs[len(arrived) : len(arrived) + (2 if number == 1 else 1)]
    state, seen = refs[len(arrived) + len(outs) :]
    x_ref = outs[-1]
    other = {1: 3, 2: 0}.get(number)
    works = plane == number if other is None else (plane == number) | (plane == other)

    @pl.when(works)
    def _():
        load_state(state, r_ref, span)
        if number in (1, 2):
            pick(plane, number, arrived[0], other, arrived[1], seen)
            if number == 2:

                @pl.when(plane == 0)
                def _():
                    state[...] = jnp.zeros_like(state)

            subtract(state, a_ref, seen)
        if number == 3:
            state[0:span, :] = state[0:span, :] + arrived[0][...]

    if number == 1:
        outs[0][...] = jnp.where(plane == 3, state[0:span, :], r_ref[...])

    @pl.when(plane == number)
    def _():
        if number >= 2:
            subtract(state, b_ref, arrived[-1])
        solve(state, e_ref, x_ref, rows)

    if number == 2:

        @pl.when(plane == 0)
        def _():
            x_ref[...] = state[0:span, :]

        @pl.when((plane == 1) | (plane == 3))
        def _():
            x_ref[...] = jnp.zeros_like(x_ref)
    else:

        @pl.when(plane != number)
        def _():
            x_ref[...] = jnp.zeros_like(x_ref)


def per_device(factor, right_side, occ_order, cabs_order):
    planes, cores = lax.axis_size("y"), lax.axis_size("core")
    plane, core = lax.axis_index("y"), lax.axis_index("core")
    pieces = lax.axis_size("x") * lax.axis_size("z")
    per, aux = factor.shape
    rows = per * pieces
    span = cores * rows
    occ_total, cabs_total = occ_order.shape[0], cabs_order.shape[0]
    cabs_local = right_side.shape[1] // occ_total
    cheap = pl.CostEstimate(flops=1000, bytes_accessed=1000, transcendentals=0)
    small = pltpu.CompilerParams(vmem_limit_bytes=8 * 1024 * 1024)
    large = pltpu.CompilerParams(vmem_limit_bytes=24 * 1024 * 1024)

    slots = occ_order.reshape(pieces, cores).T.reshape(occ_total)
    pick = (jnp.arange(cabs_local, dtype=jnp.int32)[None, :] * occ_total + slots[:, None]).reshape(-1, 1)
    spread = (pick == jnp.arange(right_side.shape[1], dtype=jnp.int32)[None, :]).astype(jnp.float32)
    sent = lax.dot_general(spread, right_side, (((1,), (1,)), ((), ())), precision=HI, preferred_element_type=jnp.float32)
    sent = sent.reshape(occ_total, cabs_local, rows)

    swap = [(0, 1), (1, 0)]
    x_arg = lax.axis_index("x").reshape(1).astype(jnp.int32)
    smem = pl.BlockSpec(memory_space=pltpu.SMEM)
    here = pl.BlockSpec(memory_space=pltpu.VMEM)
    zs, xs = lax.axis_size("z"), lax.axis_size("x")
    diag = lax.dynamic_slice_in_dim(factor, plane * span, span, 1)
    low, high = diag[:, :rows], diag[:, rows:]
    half = rows // 2
    gap, short = jnp.zeros((per, 640 - rows), jnp.float32), jnp.zeros((per, 384 - half), jnp.float32)
    lent = lax.ppermute(low[:, half:], "core", [(1, 0)])
    diag = jnp.where(
        core == 0,
        jnp.concatenate([low, gap, lent, short], axis=1),
        jnp.concatenate([high, gap, low[:, :half], short], axis=1),
    )
    tiles = diag.shape[1] // LANES

    def spread(part):
        copies = jnp.broadcast_to(part[None], (zs, *part.shape))
        return lax.all_to_all(copies, "z", 0, 0, tiled=True).reshape(zs * part.shape[0], LANES)

    got = lax.all_to_all(sent, ("core", "x", "z"), 0, 0, tiled=True)
    marker = lax.ppermute(sent[:1, :, :LANES], "core", swap)
    piece, marker = lax.optimization_barrier((diag.reshape(per * tiles, LANES), marker))
    x_arg = x_arg + (marker[0, 0, :1] != marker[0, 0, :1]).astype(jnp.int32)
    near = spread(piece)
    ahead = [(i, (i + 1) % xs) for i in range(xs)]
    behind = [(i, (i - 1) % xs) for i in range(xs)]

    def flat(block):
        return jnp.pad(block.reshape(per * ltiles, LANES), ((0, lpad - per * ltiles), (0, 0)))

    ltiles = span // LANES
    lpad = (per * ltiles + 7) // 8 * 8
    moved = lax.ppermute(factor[:, span : 2 * span], "y", [(3, 0)])
    flat_a = flat(jnp.where(plane == 0, moved, factor[:, :span]))
    flat_b = flat(lax.dynamic_slice_in_dim(factor, jnp.maximum(plane - 1, 0) * span, span, 1))
    left, right = lax.ppermute(near, "x", ahead), lax.ppermute(near, "x", behind)
    whole = lax.all_gather(jnp.concatenate([flat_a, flat_b]), ("x", "z"), axis=0, tiled=True)

    def far(left, right):
        middle = left.shape[0] // 2
        return lax.ppermute(left[:middle], "x", ahead), lax.ppermute(right[middle:], "x", behind)

    far0, far1 = far(left, right)
    far0, far1, got = lax.optimization_barrier((far0, far1, got))
    got = got.reshape(cores, cabs_total, rows)
    place = (jnp.arange(cabs_total, dtype=jnp.int32)[:, None] == cabs_order[None, :]).astype(jnp.float32)
    states = list(pl.pallas_call(
        place_kernel,
        out_shape=(jax.ShapeDtypeStruct((span, LANES), jnp.float32),) * (cabs_total // LANES),
        in_specs=[here, here],
        out_specs=(here,) * (cabs_total // LANES),
        compiler_params=small,
        cost_estimate=cheap,
        name="place",
    )(got, place))
    mine = pl.pallas_call(
        functools.partial(invert_kernel, rows, xs, zs, tiles),
        out_shape=jax.ShapeDtypeStruct((rows, tiles * LANES), jnp.float32),
        in_specs=[smem] + [here] * 5,
        out_specs=here,
        scratch_shapes=[pltpu.VMEM((tiles, 640, LANES), jnp.float32), pltpu.VMEM((5, LANES, LANES), jnp.float32)],
        compiler_params=pltpu.CompilerParams(vmem_limit_bytes=12 * 1024 * 1024),
        cost_estimate=cheap,
        name="invert",
    )(x_arg, near, left, far0, far1, right)
    theirs = lax.ppermute(mine, "core", swap)
    core_arg = core.reshape(1).astype(jnp.int32)
    plane_arg = plane.reshape(1).astype(jnp.int32)
    inverse = pl.pallas_call(
        pack_kernel,
        out_shape=jax.ShapeDtypeStruct((cores, 2, rows, tiles * LANES), jnp.bfloat16),
        in_specs=[smem, here, here],
        out_specs=here,
        compiler_params=small,
        cost_estimate=cheap,
        name="pack",
    )(core_arg, mine, theirs)

    def after(value, tokens):
        value, token = lax.optimization_barrier((value, sum(token[0, :1] for token in tokens)))
        return value, (token != token).astype(jnp.int32)

    def paired(own, zero):
        other = lax.ppermute(own, "core", swap)
        return pl.pallas_call(
            pack_kernel,
            out_shape=jax.ShapeDtypeStruct((cores, 2, *own.shape), jnp.bfloat16),
            in_specs=[smem, here, here],
            out_specs=here,
            compiler_params=small,
            cost_estimate=pl.CostEstimate(flops=1_000_000, bytes_accessed=8_000_000, transcendentals=0),
            name="pack",
        )(core_arg + zero, own, other)

    def ordered(which, whole, zero):
        own = pl.pallas_call(
            functools.partial(order_kernel, rows, pieces, lpad, ltiles),
            out_shape=jax.ShapeDtypeStruct((rows, span), jnp.float32),
            grid=(1,),
            in_specs=[pl.BlockSpec((pieces, 1, lpad, LANES), lambda i: (0, which, 0, 0), pipeline_mode=pl.Buffered(1))],
            out_specs=here,
            scratch_shapes=[pltpu.VMEM((rows, LANES), jnp.float32)],
            compiler_params=small,
            cost_estimate=pl.CostEstimate(flops=1_000_000, bytes_accessed=8_000_000, transcendentals=0),
            name="order",
        )(whole.reshape(pieces, 2, lpad, LANES))
        return paired(own, zero)

    block = jax.ShapeDtypeStruct((span, LANES), jnp.float32)

    def stage(number, *args):
        outs = 2 if number == 1 else 1
        return pl.pallas_call(
            functools.partial(stage_kernel, rows, number),
            out_shape=(block,) * outs,
            in_specs=[smem] + [here] * len(args),
            out_specs=(here,) * outs,
            scratch_shapes=[pltpu.VMEM((span + 64, LANES), jnp.float32), pltpu.VMEM((span, LANES), jnp.float32)],
            compiler_params=small,
            cost_estimate=pl.CostEstimate(flops=30_000_000_000, bytes_accessed=4_000_000, transcendentals=0),
            name=f"stage{number}",
        )(plane_arg, *args)

    def send(value, pairs):
        return lax.ppermute(value, "y", pairs)

    x0s, chunks = [], []
    for state in states:
        x0s += stage(0, inverse, state)
    firsts = [(send(x0, [(0, 1)]), send(x0, [(0, 3)])) for x0 in x0s]
    whole, zero = after(whole, [*firsts[0], x0s[-1]])
    a_mat = ordered(0, whole, zero)
    x1s, nexts, tokens = [], [], []
    for index, (state, (to1, to3)) in enumerate(zip(list(states), firsts)):
        if index > 0:
            to1, to3, token = lax.optimization_barrier((to1, to3, x1s[-1][0][:1]))
            tokens.append(token)
        to2 = send(to3, [(3, 2)])
        states[index], x1 = stage(1, inverse, a_mat, state, to1, to3)
        near_x, to0 = send(x1, [(1, 2)]), send(x1, [(1, 0)])
        x1s.append((x1, to2))
        nexts.append((near_x, to0))
    _, zero = after(core_arg, [x1 for x1, _ in x1s] + tokens)
    b_mat = ordered(1, whole, zero)
    for state, x0, (x1, to2), (near_x, to0) in zip(states, x0s, x1s, nexts):
        (x2,) = stage(2, inverse, a_mat, b_mat, state, to2, to0, near_x)
        part = send(x2, [(0, 3)])
        near_x = send(x2, [(2, 3)])
        (x3,) = stage(3, inverse, b_mat, state, part, near_x)
        chunks.append(jnp.where(plane == 0, x0, jnp.where(plane == 1, x1, jnp.where(plane == 2, x2, x3))))
    solved = jnp.concatenate([x.T for x in chunks], axis=0)
    keep = jnp.where(core == 0, solved[:, :rows], solved[:, rows:])
    give = jnp.where(core == 0, solved[:, rows:], solved[:, :rows])
    came = lax.ppermute(give, "core", [(0, 1), (1, 0)])
    return jnp.where(core == 0, jnp.stack([keep, came]), jnp.stack([came, keep]))


def solution(mesh):
    grid = Mesh(mesh.devices.reshape(4, 2, 4, 8), ("y", "core", "x", "z"))
    in_specs = (P(("y", "core", "x", "z"), None), P(("y", "core"), ("x", "z")), P(), P())
    out_specs = P(("x", "z"), None, ("y", "core"))
    return jax.shard_map(per_device, mesh=grid, in_specs=in_specs, out_specs=out_specs, check_vma=False)
```

```python
import functools
import jax
import jax.numpy as jnp
from jax import lax
from jax.experimental import pallas as pl
from jax.experimental.pallas import tpu as pltpu
from jax.sharding import Mesh, PartitionSpec as P

HI = lax.Precision.HIGHEST
LANES = 128


def full_dot(left, right):
    return jnp.dot(left, right, precision=HI, preferred_element_type=jnp.float32)


def halves(value):
    high = value.astype(jnp.bfloat16)
    return high, (value - high.astype(jnp.float32)).astype(jnp.bfloat16)


def split_right(value):
    high, low = halves(value)
    return jnp.concatenate([high, low], axis=1), high


def three_dot(left, right):
    lh, ll = left
    both, rh = right
    dot = functools.partial(jnp.dot, preferred_element_type=jnp.float32)
    wide = dot(lh, both)
    return wide[:, :LANES] + (wide[:, LANES:] + dot(ll, rh))


def invert_kernel(rows, groups, pieces, tiles, x_ref, own_ref, left_ref, far0_ref, far1_ref, right_ref, o_ref, a_ref, m_ref):
    per = rows // (groups * pieces)
    wide = 640
    blocks = wide // LANES
    x = x_ref[0]
    half = pieces // 2
    for ref, back, first, count in (
        (own_ref, 0, 0, pieces),
        (left_ref, 1, 0, pieces),
        (far0_ref, 2, 0, half),
        (far1_ref, 2, half, half),
        (right_ref, 3, 0, pieces),
    ):
        base = (lax.rem(x + groups - back, groups) * pieces + first) * per
        for tile in range(tiles):
            for row in range(per):
                a_ref[tile, pl.ds(base + row, count, stride=per), :] = ref[
                    pl.ds(row * tiles + tile, count, stride=per * tiles), :
                ]
    extra = wide - rows
    r0 = lax.broadcasted_iota(jnp.int32, (extra, LANES), 0)
    c0 = lax.broadcasted_iota(jnp.int32, (extra, LANES), 1)
    for tile in range(blocks - 1):
        a_ref[tile, rows:wide, :] = jnp.zeros((extra, LANES), jnp.float32)
    a_ref[blocks - 1, rows:wide, :] = jnp.where(c0 == r0 + (LANES - extra), 1.0, 0.0)
    ri = lax.broadcasted_iota(jnp.int32, (LANES, LANES), 0)
    ci = lax.broadcasted_iota(jnp.int32, (LANES, LANES), 1)

    def block(i, j):
        return a_ref[j, i * LANES : (i + 1) * LANES, :]

    for i in range(blocks):
        m_ref[i] = jnp.where(ri == ci, 1.0 / jnp.where(ri == ci, block(i, i), 1.0), 0.0)

    def double(level, carry):
        rb, cb = ri >> level, ci >> level
        take = (rb >> 1 == cb >> 1) & (rb == cb + 1)
        mids = [full_dot(jnp.where(take, block(i, i), 0.0), m_ref[i]) for i in range(blocks)]
        news = [m_ref[i] - full_dot(m_ref[i], mids[i]) for i in range(blocks)]
        for i in range(blocks):
            m_ref[i] = news[i]
        return carry

    lax.fori_loop(0, 7, double, 0)
    inv = [m_ref[i] for i in range(blocks)]
    for i in range(blocks):
        for j in range(blocks):
            last = min((i + 1) * LANES, rows)
            if j > i:
                o_ref[i * LANES : last, j * LANES : (j + 1) * LANES] = jnp.zeros((last - i * LANES, LANES), jnp.float32)
    done = [[None] * blocks for _ in range(blocks)]
    for i in range(blocks):
        done[i][i] = inv[i]
        last = min((i + 1) * LANES, rows)
        for j in range(i):
            total = full_dot(block(i, j), done[j][j])
            for k in range(j + 1, i):
                total = total + full_dot(block(i, k), done[k][j])
            done[i][j] = -full_dot(inv[i], total)
        for j in range(i + 1):
            o_ref[i * LANES : last, j * LANES : (j + 1) * LANES] = done[i][j][: last - i * LANES]
    for tile in range(blocks, tiles):
        o_ref[:, tile * LANES : (tile + 1) * LANES] = a_ref[tile, :rows, :]


def order_kernel(rows, pieces, pad_rows, tiles, whole_ref, o_ref, s_ref):
    per = rows // pieces
    whole_ref = whole_ref.reshape(pieces * pad_rows, LANES)
    for tile in range(tiles):

        def move(row, carry):
            s_ref[pl.ds(row, pieces, stride=per), :] = whole_ref[
                pl.ds(row * tiles + tile, pieces, stride=pad_rows), :
            ]
            return carry

        lax.fori_loop(0, per, move, 0, unroll=6)
        o_ref[:, tile * LANES : (tile + 1) * LANES] = s_ref[...]


def pack_kernel(core_ref, own_ref, other_ref, o_ref):
    core = core_ref[0]
    rows = own_ref.shape[0]
    for start in range(0, rows, 192):
        here = slice(start, start + 192)
        high, low = halves(own_ref[here, :])
        o_ref[core, 0, here, :] = high
        o_ref[core, 1, here, :] = low
        high, low = halves(other_ref[here, :])
        o_ref[1 - core, 0, here, :] = high
        o_ref[1 - core, 1, here, :] = low


def solve(state, e_ref, x_ref, rows):
    wide = 640
    step = rows // 3

    def put_first(index, value):
        x_ref[pl.ds(pl.multiple_of(index * step, step), step), :] = value

    def put_second(index, value):
        x_ref[pl.ds(pl.multiple_of(rows + index * step, step), step), :] = value

    def take(index, value):
        here = pl.ds(pl.multiple_of(rows + index * step, step), step)
        state[here, :] = state[here, :] - value

    def product(left, right, put):
        def part(index, carry):
            here = pl.ds(pl.multiple_of(index * step, step), step)
            total = None
            for (which, start, size), operand in zip(left, right):
                pair = e_ref[which, 0, here, start : start + size], e_ref[which, 1, here, start : start + size]
                term = three_dot(pair, operand)
                total = term if total is None else total + term
            put(index, total)
            return carry

        lax.fori_loop(0, 3, part, 0)

    half, link = rows // 2, e_ref.shape[3] - wide
    product([(0, 0, wide)], [split_right(state[0:wide, :])], put_first)
    tail = jnp.concatenate([x_ref[half:rows, :], jnp.zeros((link - half, LANES), jnp.float32)], axis=0)
    head = x_ref[0:link, :]
    product([(1, wide, link), (0, wide, link)], [split_right(head), split_right(tail)], take)
    product([(1, 0, wide)], [split_right(state[rows : rows + wide, :])], put_second)


def place_kernel(got_ref, place_ref, *outs):
    cores, _, rows = got_ref.shape
    for core in range(cores):
        for index, out in enumerate(outs):
            out[core * rows : (core + 1) * rows, :] = lax.dot_general(
                got_ref[core],
                place_ref[:, index * LANES : (index + 1) * LANES],
                (((0,), (0,)), ((), ())),
                precision=HI,
                preferred_element_type=jnp.float32,
            )


def load_state(state, r_ref, span):
    state[0:span, :] = r_ref[...]
    state[span:, :] = jnp.zeros((state.shape[0] - span, LANES), jnp.float32)


def subtract(state, l_ref, x_ref):
    x = split_right(x_ref[...])
    cores, _, rows, _ = l_ref.shape
    step = rows // 2

    def part(index, carry):
        core, piece = index // 2, index % 2
        here = pl.ds(pl.multiple_of(piece * step, step), step)
        there = pl.ds(pl.multiple_of(index * step, step), step)
        state[there, :] = state[there, :] - three_dot((l_ref[core, 0, here, :], l_ref[core, 1, here, :]), x)
        return carry

    lax.fori_loop(0, 2 * cores, part, 0)


def pick(plane, first, first_ref, second, second_ref, to_ref):
    @pl.when(plane == first)
    def _():
        to_ref[...] = first_ref[...]

    @pl.when(plane == second)
    def _():
        to_ref[...] = second_ref[...]


def stage_kernel(rows, number, plane_ref, *refs):
    plane = plane_ref[0]
    span = 2 * rows
    e_ref, refs = refs[0], refs[1:]
    a_ref, refs = (refs[0], refs[1:]) if number in (1, 2) else (None, refs)
    b_ref, refs = (refs[0], refs[1:]) if number >= 2 else (None, refs)
    r_ref, refs = refs[0], refs[1:]
    arrived = refs[: (0, 2, 3, 2)[number]]
    outs = refs[len(arrived) : len(arrived) + (2 if number == 1 else 1)]
    state, seen = refs[len(arrived) + len(outs) :]
    x_ref = outs[-1]
    other = {1: 3, 2: 0}.get(number)
    works = plane == number if other is None else (plane == number) | (plane == other)

    @pl.when(works)
    def _():
        load_state(state, r_ref, span)
        if number in (1, 2):
            pick(plane, number, arrived[0], other, arrived[1], seen)
            if number == 2:

                @pl.when(plane == 0)
                def _():
                    state[...] = jnp.zeros_like(state)

            subtract(state, a_ref, seen)
        if number == 3:
            state[0:span, :] = state[0:span, :] + arrived[0][...]

    if number == 1:
        outs[0][...] = jnp.where(plane == 3, state[0:span, :], r_ref[...])

    @pl.when(plane == number)
    def _():
        if number >= 2:
            subtract(state, b_ref, arrived[-1])
        solve(state, e_ref, x_ref, rows)

    if number == 2:

        @pl.when(plane == 0)
        def _():
            x_ref[...] = state[0:span, :]

        @pl.when((plane == 1) | (plane == 3))
        def _():
            x_ref[...] = jnp.zeros_like(x_ref)
    else:

        @pl.when(plane != number)
        def _():
            x_ref[...] = jnp.zeros_like(x_ref)


def per_device(factor, right_side, occ_order, cabs_order):
    planes, cores = lax.axis_size("y"), lax.axis_size("core")
    plane, core = lax.axis_index("y"), lax.axis_index("core")
    pieces = lax.axis_size("x") * lax.axis_size("z")
    per, aux = factor.shape
    rows = per * pieces
    span = cores * rows
    occ_total, cabs_total = occ_order.shape[0], cabs_order.shape[0]
    cabs_local = right_side.shape[1] // occ_total
    cheap = pl.CostEstimate(flops=1000, bytes_accessed=1000, transcendentals=0)
    small = pltpu.CompilerParams(vmem_limit_bytes=8 * 1024 * 1024)
    large = pltpu.CompilerParams(vmem_limit_bytes=24 * 1024 * 1024)

    slots = occ_order.reshape(pieces, cores).T.reshape(occ_total)
    pick = (jnp.arange(cabs_local, dtype=jnp.int32)[None, :] * occ_total + slots[:, None]).reshape(-1, 1)
    spread = (pick == jnp.arange(right_side.shape[1], dtype=jnp.int32)[None, :]).astype(jnp.float32)
    sent = lax.dot_general(spread, right_side, (((1,), (1,)), ((), ())), precision=HI, preferred_element_type=jnp.float32)
    sent = sent.reshape(occ_total, cabs_local, rows)

    def flat(block):
        return jnp.pad(block.reshape(per * ltiles, LANES), ((0, lpad - per * ltiles), (0, 0)))

    ltiles = span // LANES
    lpad = (per * ltiles + 7) // 8 * 8
    moved = lax.ppermute(factor[:, span : 2 * span], "y", [(3, 0)])
    flat_a = flat(jnp.where(plane == 0, moved, factor[:, :span]))
    flat_b = flat(lax.dynamic_slice_in_dim(factor, jnp.maximum(plane - 1, 0) * span, span, 1))
    flats = jnp.concatenate([flat_a, flat_b])

    swap = [(0, 1), (1, 0)]
    x_arg = lax.axis_index("x").reshape(1).astype(jnp.int32)
    smem = pl.BlockSpec(memory_space=pltpu.SMEM)
    here = pl.BlockSpec(memory_space=pltpu.VMEM)
    zs, xs = lax.axis_size("z"), lax.axis_size("x")
    diag = lax.dynamic_slice_in_dim(factor, plane * span, span, 1)
    low, high = diag[:, :rows], diag[:, rows:]
    half = rows // 2
    gap, short = jnp.zeros((per, 640 - rows), jnp.float32), jnp.zeros((per, 384 - half), jnp.float32)
    lent = lax.ppermute(low[:, half:], "core", [(1, 0)])
    diag = jnp.where(
        core == 0,
        jnp.concatenate([low, gap, lent, short], axis=1),
        jnp.concatenate([high, gap, low[:, :half], short], axis=1),
    )
    tiles = diag.shape[1] // LANES

    def spread(part):
        copies = jnp.broadcast_to(part[None], (zs, *part.shape))
        return lax.all_to_all(copies, "z", 0, 0, tiled=True).reshape(zs * part.shape[0], LANES)

    got = lax.all_to_all(sent, ("core", "x", "z"), 0, 0, tiled=True)
    piece = diag.reshape(per * tiles, LANES)
    piece, flats = lax.optimization_barrier((piece, flats))
    whole = lax.all_gather(flats, ("x", "z"), axis=0, tiled=True)
    near = spread(piece)
    ahead = [(i, (i + 1) % xs) for i in range(xs)]
    behind = [(i, (i - 1) % xs) for i in range(xs)]

    left, right = lax.ppermute(near, "x", ahead), lax.ppermute(near, "x", behind)
    def far(left, right):
        middle = left.shape[0] // 2
        return lax.ppermute(left[:middle], "x", ahead), lax.ppermute(right[middle:], "x", behind)

    far0, far1 = far(left, right)
    far0, far1, got = lax.optimization_barrier((far0, far1, got))
    got = got.reshape(cores, cabs_total, rows)
    place = (jnp.arange(cabs_total, dtype=jnp.int32)[:, None] == cabs_order[None, :]).astype(jnp.float32)
    states = list(pl.pallas_call(
        place_kernel,
        out_shape=(jax.ShapeDtypeStruct((span, LANES), jnp.float32),) * (cabs_total // LANES),
        in_specs=[here, here],
        out_specs=(here,) * (cabs_total // LANES),
        compiler_params=small,
        cost_estimate=cheap,
        name="place",
    )(got, place))
    mine = pl.pallas_call(
        functools.partial(invert_kernel, rows, xs, zs, tiles),
        out_shape=jax.ShapeDtypeStruct((rows, tiles * LANES), jnp.float32),
        in_specs=[smem] + [here] * 5,
        out_specs=here,
        scratch_shapes=[pltpu.VMEM((tiles, 640, LANES), jnp.float32), pltpu.VMEM((5, LANES, LANES), jnp.float32)],
        compiler_params=pltpu.CompilerParams(vmem_limit_bytes=12 * 1024 * 1024),
        cost_estimate=cheap,
        name="invert",
    )(x_arg, near, left, far0, far1, right)
    theirs = lax.ppermute(mine, "core", swap)
    core_arg = core.reshape(1).astype(jnp.int32)
    plane_arg = plane.reshape(1).astype(jnp.int32)
    inverse = pl.pallas_call(
        pack_kernel,
        out_shape=jax.ShapeDtypeStruct((cores, 2, rows, tiles * LANES), jnp.bfloat16),
        in_specs=[smem, here, here],
        out_specs=here,
        compiler_params=small,
        cost_estimate=cheap,
        name="pack",
    )(core_arg, mine, theirs)

    def after(value, tokens):
        value, token = lax.optimization_barrier((value, sum(token[0, :1] for token in tokens)))
        return value, (token != token).astype(jnp.int32)

    def paired(own, zero):
        other = lax.ppermute(own, "core", swap)
        return pl.pallas_call(
            pack_kernel,
            out_shape=jax.ShapeDtypeStruct((cores, 2, *own.shape), jnp.bfloat16),
            in_specs=[smem, here, here],
            out_specs=here,
            compiler_params=small,
            cost_estimate=pl.CostEstimate(flops=1_000_000, bytes_accessed=8_000_000, transcendentals=0),
            name="pack",
        )(core_arg + zero, own, other)

    def ordered(which, whole, zero):
        own = pl.pallas_call(
            functools.partial(order_kernel, rows, pieces, lpad, ltiles),
            out_shape=jax.ShapeDtypeStruct((rows, span), jnp.float32),
            grid=(1,),
            in_specs=[pl.BlockSpec((pieces, 1, lpad, LANES), lambda i: (0, which, 0, 0), pipeline_mode=pl.Buffered(1))],
            out_specs=here,
            scratch_shapes=[pltpu.VMEM((rows, LANES), jnp.float32)],
            compiler_params=small,
            cost_estimate=pl.CostEstimate(flops=1_000_000, bytes_accessed=8_000_000, transcendentals=0),
            name="order",
        )(whole.reshape(pieces, 2, lpad, LANES))
        return paired(own, zero)

    block = jax.ShapeDtypeStruct((span, LANES), jnp.float32)

    def stage(number, *args):
        outs = 2 if number == 1 else 1
        return pl.pallas_call(
            functools.partial(stage_kernel, rows, number),
            out_shape=(block,) * outs,
            in_specs=[smem] + [here] * len(args),
            out_specs=(here,) * outs,
            scratch_shapes=[pltpu.VMEM((span + 64, LANES), jnp.float32), pltpu.VMEM((span, LANES), jnp.float32)],
            compiler_params=small,
            cost_estimate=pl.CostEstimate(flops=30_000_000_000, bytes_accessed=4_000_000, transcendentals=0),
            name=f"stage{number}",
        )(plane_arg, *args)

    def send(value, pairs):
        return lax.ppermute(value, "y", pairs)

    x0s, chunks = [], []
    for state in states:
        x0s += stage(0, inverse, state)
    firsts = [(send(x0, [(0, 1)]), send(x0, [(0, 3)])) for x0 in x0s]
    whole, zero = after(whole, [*firsts[0], x0s[-1]])
    a_mat = ordered(0, whole, zero)
    x1s, nexts, tokens = [], [], []
    for index, (state, (to1, to3)) in enumerate(zip(list(states), firsts)):
        if index > 0:
            to1, to3, token = lax.optimization_barrier((to1, to3, x1s[-1][0][:1]))
            tokens.append(token)
        to2 = send(to3, [(3, 2)])
        states[index], x1 = stage(1, inverse, a_mat, state, to1, to3)
        near_x, to0 = send(x1, [(1, 2)]), send(x1, [(1, 0)])
        x1s.append((x1, to2))
        nexts.append((near_x, to0))
    _, zero = after(core_arg, [x1 for x1, _ in x1s] + tokens)
    b_mat = ordered(1, whole, zero)
    for state, x0, (x1, to2), (near_x, to0) in zip(states, x0s, x1s, nexts):
        (x2,) = stage(2, inverse, a_mat, b_mat, state, to2, to0, near_x)
        part = send(x2, [(0, 3)])
        near_x = send(x2, [(2, 3)])
        (x3,) = stage(3, inverse, b_mat, state, part, near_x)
        chunks.append(jnp.where(plane == 0, x0, jnp.where(plane == 1, x1, jnp.where(plane == 2, x2, x3))))
    solved = jnp.concatenate([x.T for x in chunks], axis=0)
    keep = jnp.where(core == 0, solved[:, :rows], solved[:, rows:])
    give = jnp.where(core == 0, solved[:, rows:], solved[:, :rows])
    came = lax.ppermute(give, "core", [(0, 1), (1, 0)])
    return jnp.where(core == 0, jnp.stack([keep, came]), jnp.stack([came, keep]))


def solution(mesh):
    grid = Mesh(mesh.devices.reshape(4, 2, 4, 8), ("y", "core", "x", "z"))
    in_specs = (P(("y", "core", "x", "z"), None), P(("y", "core"), ("x", "z")), P(), P())
    out_specs = P(("x", "z"), None, ("y", "core"))
    return jax.shard_map(per_device, mesh=grid, in_specs=in_specs, out_specs=out_specs, check_vma=False)
```

```python
import functools
import jax
import jax.numpy as jnp
from jax import lax
from jax.experimental import pallas as pl
from jax.experimental.pallas import tpu as pltpu
from jax.sharding import Mesh, PartitionSpec as P

HI = lax.Precision.HIGHEST
LANES = 128


def full_dot(left, right):
    return jnp.dot(left, right, precision=HI, preferred_element_type=jnp.float32)


def halves(value):
    high = value.astype(jnp.bfloat16)
    return high, (value - high.astype(jnp.float32)).astype(jnp.bfloat16)


def split_right(value):
    high, low = halves(value)
    return jnp.concatenate([high, low], axis=1), high


def three_dot(left, right):
    lh, ll = left
    both, rh = right
    dot = functools.partial(jnp.dot, preferred_element_type=jnp.float32)
    wide = dot(lh, both)
    return wide[:, :LANES] + (wide[:, LANES:] + dot(ll, rh))


def invert_kernel(rows, groups, pieces, tiles, x_ref, own_ref, left_ref, far0_ref, far1_ref, right_ref, o_ref, a_ref, m_ref):
    per = rows // (groups * pieces)
    wide = 640
    blocks = wide // LANES
    x = x_ref[0]
    half = pieces // 2
    for ref, back, first, count in (
        (own_ref, 0, 0, pieces),
        (left_ref, 1, 0, pieces),
        (far0_ref, 2, 0, half),
        (far1_ref, 2, half, half),
        (right_ref, 3, 0, pieces),
    ):
        base = (lax.rem(x + groups - back, groups) * pieces + first) * per
        for tile in range(tiles):
            for row in range(per):
                a_ref[tile, pl.ds(base + row, count, stride=per), :] = ref[
                    pl.ds(row * tiles + tile, count, stride=per * tiles), :
                ]
    extra = wide - rows
    r0 = lax.broadcasted_iota(jnp.int32, (extra, LANES), 0)
    c0 = lax.broadcasted_iota(jnp.int32, (extra, LANES), 1)
    for tile in range(blocks - 1):
        a_ref[tile, rows:wide, :] = jnp.zeros((extra, LANES), jnp.float32)
    a_ref[blocks - 1, rows:wide, :] = jnp.where(c0 == r0 + (LANES - extra), 1.0, 0.0)
    ri = lax.broadcasted_iota(jnp.int32, (LANES, LANES), 0)
    ci = lax.broadcasted_iota(jnp.int32, (LANES, LANES), 1)

    def block(i, j):
        return a_ref[j, i * LANES : (i + 1) * LANES, :]

    for i in range(blocks):
        m_ref[i] = jnp.where(ri == ci, 1.0 / jnp.where(ri == ci, block(i, i), 1.0), 0.0)

    def double(level, carry):
        rb, cb = ri >> level, ci >> level
        take = (rb >> 1 == cb >> 1) & (rb == cb + 1)
        mids = [full_dot(jnp.where(take, block(i, i), 0.0), m_ref[i]) for i in range(blocks)]
        news = [m_ref[i] - full_dot(m_ref[i], mids[i]) for i in range(blocks)]
        for i in range(blocks):
            m_ref[i] = news[i]
        return carry

    lax.fori_loop(0, 7, double, 0)
    inv = [m_ref[i] for i in range(blocks)]
    for i in range(blocks):
        for j in range(blocks):
            last = min((i + 1) * LANES, rows)
            if j > i:
                o_ref[i * LANES : last, j * LANES : (j + 1) * LANES] = jnp.zeros((last - i * LANES, LANES), jnp.float32)
    done = [[None] * blocks for _ in range(blocks)]
    for i in range(blocks):
        done[i][i] = inv[i]
        last = min((i + 1) * LANES, rows)
        for j in range(i):
            total = full_dot(block(i, j), done[j][j])
            for k in range(j + 1, i):
                total = total + full_dot(block(i, k), done[k][j])
            done[i][j] = -full_dot(inv[i], total)
        for j in range(i + 1):
            o_ref[i * LANES : last, j * LANES : (j + 1) * LANES] = done[i][j][: last - i * LANES]
    for tile in range(blocks, tiles):
        o_ref[:, tile * LANES : (tile + 1) * LANES] = a_ref[tile, :rows, :]


def order_kernel(rows, pieces, pad_rows, tiles, whole_ref, o_ref, s_ref):
    per = rows // pieces
    whole_ref = whole_ref.reshape(pieces * pad_rows, LANES)
    for tile in range(tiles):

        def move(row, carry):
            s_ref[pl.ds(row, pieces, stride=per), :] = whole_ref[
                pl.ds(row * tiles + tile, pieces, stride=pad_rows), :
            ]
            return carry

        lax.fori_loop(0, per, move, 0, unroll=6)
        o_ref[:, tile * LANES : (tile + 1) * LANES] = s_ref[...]


def pack_kernel(core_ref, own_ref, other_ref, o_ref):
    core = core_ref[0]
    rows = own_ref.shape[0]
    for start in range(0, rows, 192):
        here = slice(start, start + 192)
        high, low = halves(own_ref[here, :])
        o_ref[core, 0, here, :] = high
        o_ref[core, 1, here, :] = low
        high, low = halves(other_ref[here, :])
        o_ref[1 - core, 0, here, :] = high
        o_ref[1 - core, 1, here, :] = low


def solve(state, e_ref, x_ref, rows):
    wide = 640
    step = rows // 3

    def put_first(index, value):
        x_ref[pl.ds(pl.multiple_of(index * step, step), step), :] = value

    def put_second(index, value):
        x_ref[pl.ds(pl.multiple_of(rows + index * step, step), step), :] = value

    def take(index, value):
        here = pl.ds(pl.multiple_of(rows + index * step, step), step)
        state[here, :] = state[here, :] - value

    def product(left, right, put):
        def part(index, carry):
            here = pl.ds(pl.multiple_of(index * step, step), step)
            total = None
            for (which, start, size), operand in zip(left, right):
                pair = e_ref[which, 0, here, start : start + size], e_ref[which, 1, here, start : start + size]
                term = three_dot(pair, operand)
                total = term if total is None else total + term
            put(index, total)
            return carry

        lax.fori_loop(0, 3, part, 0)

    half, link = rows // 2, e_ref.shape[3] - wide
    product([(0, 0, wide)], [split_right(state[0:wide, :])], put_first)
    tail = jnp.concatenate([x_ref[half:rows, :], jnp.zeros((link - half, LANES), jnp.float32)], axis=0)
    head = x_ref[0:link, :]
    product([(1, wide, link), (0, wide, link)], [split_right(head), split_right(tail)], take)
    product([(1, 0, wide)], [split_right(state[rows : rows + wide, :])], put_second)


def place_kernel(got_ref, place_ref, *outs):
    cores, _, rows = got_ref.shape
    for core in range(cores):
        for index, out in enumerate(outs):
            out[core * rows : (core + 1) * rows, :] = lax.dot_general(
                got_ref[core],
                place_ref[:, index * LANES : (index + 1) * LANES],
                (((0,), (0,)), ((), ())),
                precision=HI,
                preferred_element_type=jnp.float32,
            )


def load_state(state, r_ref, span):
    state[0:span, :] = r_ref[...]
    state[span:, :] = jnp.zeros((state.shape[0] - span, LANES), jnp.float32)


def subtract(state, l_ref, x_ref):
    x = split_right(x_ref[...])
    cores, _, rows, _ = l_ref.shape
    step = rows // 2

    def part(index, carry):
        core, piece = index // 2, index % 2
        here = pl.ds(pl.multiple_of(piece * step, step), step)
        there = pl.ds(pl.multiple_of(index * step, step), step)
        state[there, :] = state[there, :] - three_dot((l_ref[core, 0, here, :], l_ref[core, 1, here, :]), x)
        return carry

    lax.fori_loop(0, 2 * cores, part, 0)


def pick(plane, first, first_ref, second, second_ref, to_ref):
    @pl.when(plane == first)
    def _():
        to_ref[...] = first_ref[...]

    @pl.when(plane == second)
    def _():
        to_ref[...] = second_ref[...]


def stage_kernel(rows, number, plane_ref, *refs):
    plane = plane_ref[0]
    span = 2 * rows
    e_ref, refs = refs[0], refs[1:]
    a_ref, refs = (refs[0], refs[1:]) if number in (1, 2) else (None, refs)
    b_ref, refs = (refs[0], refs[1:]) if number >= 2 else (None, refs)
    r_ref, refs = refs[0], refs[1:]
    arrived = refs[: (0, 2, 3, 2)[number]]
    outs = refs[len(arrived) : len(arrived) + (2 if number == 1 else 1)]
    state, seen = refs[len(arrived) + len(outs) :]
    x_ref = outs[-1]
    other = {1: 3, 2: 0}.get(number)
    works = plane == number if other is None else (plane == number) | (plane == other)

    @pl.when(works)
    def _():
        load_state(state, r_ref, span)
        if number in (1, 2):
            pick(plane, number, arrived[0], other, arrived[1], seen)
            if number == 2:

                @pl.when(plane == 0)
                def _():
                    state[...] = jnp.zeros_like(state)

            subtract(state, a_ref, seen)
        if number == 3:
            state[0:span, :] = state[0:span, :] + arrived[0][...]

    if number == 1:
        outs[0][...] = jnp.where(plane == 3, state[0:span, :], r_ref[...])

    @pl.when(plane == number)
    def _():
        if number >= 2:
            subtract(state, b_ref, arrived[-1])
        solve(state, e_ref, x_ref, rows)

    if number == 2:

        @pl.when(plane == 0)
        def _():
            x_ref[...] = state[0:span, :]

        @pl.when((plane == 1) | (plane == 3))
        def _():
            x_ref[...] = jnp.zeros_like(x_ref)
    else:

        @pl.when(plane != number)
        def _():
            x_ref[...] = jnp.zeros_like(x_ref)


def per_device(factor, right_side, occ_order, cabs_order):
    planes, cores = lax.axis_size("y"), lax.axis_size("core")
    plane, core = lax.axis_index("y"), lax.axis_index("core")
    pieces = lax.axis_size("x") * lax.axis_size("z")
    per, aux = factor.shape
    rows = per * pieces
    span = cores * rows
    occ_total, cabs_total = occ_order.shape[0], cabs_order.shape[0]
    cabs_local = right_side.shape[1] // occ_total
    cheap = pl.CostEstimate(flops=1000, bytes_accessed=1000, transcendentals=0)
    small = pltpu.CompilerParams(vmem_limit_bytes=8 * 1024 * 1024)
    large = pltpu.CompilerParams(vmem_limit_bytes=24 * 1024 * 1024)

    slots = occ_order.reshape(pieces, cores).T.reshape(occ_total)
    pick = (jnp.arange(cabs_local, dtype=jnp.int32)[None, :] * occ_total + slots[:, None]).reshape(-1, 1)
    spread = (pick == jnp.arange(right_side.shape[1], dtype=jnp.int32)[None, :]).astype(jnp.float32)
    sent = lax.dot_general(spread, right_side, (((1,), (1,)), ((), ())), precision=HI, preferred_element_type=jnp.float32)
    sent = sent.reshape(occ_total, cabs_local, rows)

    def flat(block):
        return jnp.pad(block.reshape(per * ltiles, LANES), ((0, lpad - per * ltiles), (0, 0)))

    ltiles = span // LANES
    lpad = (per * ltiles + 7) // 8 * 8
    moved = lax.ppermute(factor[:, span : 2 * span], "y", [(3, 0)])
    flat_a = flat(jnp.where(plane == 0, moved, factor[:, :span]))
    flat_b = flat(lax.dynamic_slice_in_dim(factor, jnp.maximum(plane - 1, 0) * span, span, 1))
    flats = jnp.concatenate([flat_a, flat_b])

    swap = [(0, 1), (1, 0)]
    x_arg = lax.axis_index("x").reshape(1).astype(jnp.int32)
    smem = pl.BlockSpec(memory_space=pltpu.SMEM)
    here = pl.BlockSpec(memory_space=pltpu.VMEM)
    zs, xs = lax.axis_size("z"), lax.axis_size("x")
    diag = lax.dynamic_slice_in_dim(factor, plane * span, span, 1)
    low, high = diag[:, :rows], diag[:, rows:]
    half = rows // 2
    gap, short = jnp.zeros((per, 640 - rows), jnp.float32), jnp.zeros((per, 384 - half), jnp.float32)
    lent = lax.ppermute(low[:, half:], "core", [(1, 0)])
    diag = jnp.where(
        core == 0,
        jnp.concatenate([low, gap, lent, short], axis=1),
        jnp.concatenate([high, gap, low[:, :half], short], axis=1),
    )
    tiles = diag.shape[1] // LANES

    def spread(part):
        copies = jnp.broadcast_to(part[None], (zs, *part.shape))
        return lax.all_to_all(copies, "z", 0, 0, tiled=True).reshape(zs * part.shape[0], LANES)

    got = lax.all_to_all(sent, ("core", "x", "z"), 0, 0, tiled=True)
    piece = diag.reshape(per * tiles, LANES)
    whole = lax.all_gather(flats, ("x", "z"), axis=0, tiled=True)
    near = spread(piece)
    ahead = [(i, (i + 1) % xs) for i in range(xs)]
    behind = [(i, (i - 1) % xs) for i in range(xs)]

    left, right = lax.ppermute(near, "x", ahead), lax.ppermute(near, "x", behind)
    def far(left, right):
        middle = left.shape[0] // 2
        return lax.ppermute(left[:middle], "x", ahead), lax.ppermute(right[middle:], "x", behind)

    far0, far1 = far(left, right)
    far0, far1, got = lax.optimization_barrier((far0, far1, got))
    got = got.reshape(cores, cabs_total, rows)
    place = (jnp.arange(cabs_total, dtype=jnp.int32)[:, None] == cabs_order[None, :]).astype(jnp.float32)
    states = list(pl.pallas_call(
        place_kernel,
        out_shape=(jax.ShapeDtypeStruct((span, LANES), jnp.float32),) * (cabs_total // LANES),
        in_specs=[here, here],
        out_specs=(here,) * (cabs_total // LANES),
        compiler_params=small,
        cost_estimate=cheap,
        name="place",
    )(got, place))
    mine = pl.pallas_call(
        functools.partial(invert_kernel, rows, xs, zs, tiles),
        out_shape=jax.ShapeDtypeStruct((rows, tiles * LANES), jnp.float32),
        in_specs=[smem] + [here] * 5,
        out_specs=here,
        scratch_shapes=[pltpu.VMEM((tiles, 640, LANES), jnp.float32), pltpu.VMEM((5, LANES, LANES), jnp.float32)],
        compiler_params=pltpu.CompilerParams(vmem_limit_bytes=12 * 1024 * 1024),
        cost_estimate=cheap,
        name="invert",
    )(x_arg, near, left, far0, far1, right)
    theirs = lax.ppermute(mine, "core", swap)
    core_arg = core.reshape(1).astype(jnp.int32)
    plane_arg = plane.reshape(1).astype(jnp.int32)
    inverse = pl.pallas_call(
        pack_kernel,
        out_shape=jax.ShapeDtypeStruct((cores, 2, rows, tiles * LANES), jnp.bfloat16),
        in_specs=[smem, here, here],
        out_specs=here,
        compiler_params=small,
        cost_estimate=cheap,
        name="pack",
    )(core_arg, mine, theirs)

    def after(value, tokens):
        value, token = lax.optimization_barrier((value, sum(token[0, :1] for token in tokens)))
        return value, (token != token).astype(jnp.int32)

    def paired(own, zero):
        other = lax.ppermute(own, "core", swap)
        return pl.pallas_call(
            pack_kernel,
            out_shape=jax.ShapeDtypeStruct((cores, 2, *own.shape), jnp.bfloat16),
            in_specs=[smem, here, here],
            out_specs=here,
            compiler_params=small,
            cost_estimate=pl.CostEstimate(flops=1_000_000, bytes_accessed=8_000_000, transcendentals=0),
            name="pack",
        )(core_arg + zero, own, other)

    def ordered(which, whole, zero):
        own = pl.pallas_call(
            functools.partial(order_kernel, rows, pieces, lpad, ltiles),
            out_shape=jax.ShapeDtypeStruct((rows, span), jnp.float32),
            grid=(1,),
            in_specs=[pl.BlockSpec((pieces, 1, lpad, LANES), lambda i: (0, which, 0, 0), pipeline_mode=pl.Buffered(1))],
            out_specs=here,
            scratch_shapes=[pltpu.VMEM((rows, LANES), jnp.float32)],
            compiler_params=small,
            cost_estimate=pl.CostEstimate(flops=1_000_000, bytes_accessed=8_000_000, transcendentals=0),
            name="order",
        )(whole.reshape(pieces, 2, lpad, LANES))
        return paired(own, zero)

    block = jax.ShapeDtypeStruct((span, LANES), jnp.float32)

    def stage(number, *args):
        outs = 2 if number == 1 else 1
        return pl.pallas_call(
            functools.partial(stage_kernel, rows, number),
            out_shape=(block,) * outs,
            in_specs=[smem] + [here] * len(args),
            out_specs=(here,) * outs,
            scratch_shapes=[pltpu.VMEM((span + 64, LANES), jnp.float32), pltpu.VMEM((span, LANES), jnp.float32)],
            compiler_params=small,
            cost_estimate=pl.CostEstimate(flops=30_000_000_000, bytes_accessed=4_000_000, transcendentals=0),
            name=f"stage{number}",
        )(plane_arg, *args)

    def send(value, pairs):
        return lax.ppermute(value, "y", pairs)

    x0s, chunks = [], []
    for state in states:
        x0s += stage(0, inverse, state)
    firsts = [(send(x0, [(0, 1)]), send(x0, [(0, 3)])) for x0 in x0s[:1]] + [None]
    whole, *first, x0s[-1] = lax.optimization_barrier((whole, *firsts[0], x0s[-1]))
    firsts[0] = tuple(first)
    firsts[-1] = send(x0s[-1], [(0, 1)]), send(x0s[-1], [(0, 3)])
    a_mat = ordered(0, whole, 0)
    x1s, nexts, tokens = [], [], []
    for index, (state, (to1, to3)) in enumerate(zip(list(states), firsts)):
        if index > 0:
            to1, to3, token = lax.optimization_barrier((to1, to3, x1s[-1][0][:1]))
            tokens.append(token)
        to2 = send(to3, [(3, 2)])
        states[index], x1 = stage(1, inverse, a_mat, state, to1, to3)
        near_x, to0 = send(x1, [(1, 2)]), send(x1, [(1, 0)])
        x1s.append((x1, to2))
        nexts.append((near_x, to0))
    _, zero = after(core_arg, [x1 for x1, _ in x1s] + tokens)
    b_mat = ordered(1, whole, zero)
    for state, x0, (x1, to2), (near_x, to0) in zip(states, x0s, x1s, nexts):
        (x2,) = stage(2, inverse, a_mat, b_mat, state, to2, to0, near_x)
        part = send(x2, [(0, 3)])
        near_x = send(x2, [(2, 3)])
        (x3,) = stage(3, inverse, b_mat, state, part, near_x)
        chunks.append(jnp.where(plane == 0, x0, jnp.where(plane == 1, x1, jnp.where(plane == 2, x2, x3))))
    solved = jnp.concatenate([x.T for x in chunks], axis=0)
    keep = jnp.where(core == 0, solved[:, :rows], solved[:, rows:])
    give = jnp.where(core == 0, solved[:, rows:], solved[:, :rows])
    came = lax.ppermute(give, "core", [(0, 1), (1, 0)])
    return jnp.where(core == 0, jnp.stack([keep, came]), jnp.stack([came, keep]))


def solution(mesh):
    grid = Mesh(mesh.devices.reshape(4, 2, 4, 8), ("y", "core", "x", "z"))
    in_specs = (P(("y", "core", "x", "z"), None), P(("y", "core"), ("x", "z")), P(), P())
    out_specs = P(("x", "z"), None, ("y", "core"))
    return jax.shard_map(per_device, mesh=grid, in_specs=in_specs, out_specs=out_specs, check_vma=False)
```

```python
import functools
import jax
import jax.numpy as jnp
from jax import lax
from jax.experimental import pallas as pl
from jax.experimental.pallas import tpu as pltpu
from jax.sharding import Mesh, PartitionSpec as P

HI = lax.Precision.HIGHEST
LANES = 128


def halves(value):
    high = value.astype(jnp.bfloat16)
    return high, (value - high.astype(jnp.float32)).astype(jnp.bfloat16)


def split_right(value):
    high, low = halves(value)
    return jnp.concatenate([high, low], axis=1), high


def three_dot(left, right):
    lh, ll = left
    both, rh = right
    dot = functools.partial(jnp.dot, preferred_element_type=jnp.float32)
    wide = dot(lh, both)
    return wide[:, :LANES] + (wide[:, LANES:] + dot(ll, rh))


def full_dot(left, right):
    return three_dot(halves(left), split_right(right))


def invert_kernel(rows, groups, pieces, tiles, x_ref, own_ref, left_ref, far0_ref, far1_ref, right_ref, o_ref, a_ref, m_ref):
    per = rows // (groups * pieces)
    wide = 640
    blocks = wide // LANES
    x = x_ref[0]
    half = pieces // 2
    for ref, back, first, count in (
        (own_ref, 0, 0, pieces),
        (left_ref, 1, 0, pieces),
        (far0_ref, 2, 0, half),
        (far1_ref, 2, half, half),
        (right_ref, 3, 0, pieces),
    ):
        base = (lax.rem(x + groups - back, groups) * pieces + first) * per
        for tile in range(tiles):
            for row in range(per):
                a_ref[tile, pl.ds(base + row, count, stride=per), :] = ref[
                    pl.ds(row * tiles + tile, count, stride=per * tiles), :
                ]
    extra = wide - rows
    r0 = lax.broadcasted_iota(jnp.int32, (extra, LANES), 0)
    c0 = lax.broadcasted_iota(jnp.int32, (extra, LANES), 1)
    for tile in range(blocks - 1):
        a_ref[tile, rows:wide, :] = jnp.zeros((extra, LANES), jnp.float32)
    a_ref[blocks - 1, rows:wide, :] = jnp.where(c0 == r0 + (LANES - extra), 1.0, 0.0)
    ri = lax.broadcasted_iota(jnp.int32, (LANES, LANES), 0)
    ci = lax.broadcasted_iota(jnp.int32, (LANES, LANES), 1)

    def block(i, j):
        return a_ref[j, i * LANES : (i + 1) * LANES, :]

    for i in range(blocks):
        m_ref[i] = jnp.where(ri == ci, 1.0 / jnp.where(ri == ci, block(i, i), 1.0), 0.0)

    def double(level, carry):
        rb, cb = ri >> level, ci >> level
        take = (rb >> 1 == cb >> 1) & (rb == cb + 1)
        mids = [full_dot(jnp.where(take, block(i, i), 0.0), m_ref[i]) for i in range(blocks)]
        news = [m_ref[i] - full_dot(m_ref[i], mids[i]) for i in range(blocks)]
        for i in range(blocks):
            m_ref[i] = news[i]
        return carry

    lax.fori_loop(0, 7, double, 0)
    inv = [m_ref[i] for i in range(blocks)]
    for i in range(blocks):
        for j in range(blocks):
            last = min((i + 1) * LANES, rows)
            if j > i:
                o_ref[i * LANES : last, j * LANES : (j + 1) * LANES] = jnp.zeros((last - i * LANES, LANES), jnp.float32)
    done = [[None] * blocks for _ in range(blocks)]
    for i in range(blocks):
        done[i][i] = inv[i]
        last = min((i + 1) * LANES, rows)
        for j in range(i):
            total = full_dot(block(i, j), done[j][j])
            for k in range(j + 1, i):
                total = total + full_dot(block(i, k), done[k][j])
            done[i][j] = -full_dot(inv[i], total)
        for j in range(i + 1):
            o_ref[i * LANES : last, j * LANES : (j + 1) * LANES] = done[i][j][: last - i * LANES]
    for tile in range(blocks, tiles):
        o_ref[:, tile * LANES : (tile + 1) * LANES] = a_ref[tile, :rows, :]


def order_kernel(rows, pieces, pad_rows, tiles, whole_ref, *refs):
    per = rows // pieces
    outs, s_ref = refs[:-1], refs[-1]
    for block, out in enumerate(outs):
        for tile in range(tiles):

            def move(row, carry, block=block, tile=tile):
                s_ref[pl.ds(row, pieces, stride=per), :] = whole_ref[
                    pl.ds(block * pad_rows + row * tiles + tile, pieces, stride=len(outs) * pad_rows), :
                ]
                return carry

            lax.fori_loop(0, per, move, 0, unroll=6)
            out[:, tile * LANES : (tile + 1) * LANES] = s_ref[...]


def pack_kernel(core_ref, own_ref, other_ref, o_ref):
    core = core_ref[0]
    rows = own_ref.shape[0]
    for start in range(0, rows, 192):
        here = slice(start, start + 192)
        high, low = halves(own_ref[here, :])
        o_ref[core, 0, here, :] = high
        o_ref[core, 1, here, :] = low
        high, low = halves(other_ref[here, :])
        o_ref[1 - core, 0, here, :] = high
        o_ref[1 - core, 1, here, :] = low


def solve(state, e_ref, x_ref, rows):
    wide = 640
    step = rows // 3

    def put_first(index, value):
        x_ref[pl.ds(pl.multiple_of(index * step, step), step), :] = value

    def put_second(index, value):
        x_ref[pl.ds(pl.multiple_of(rows + index * step, step), step), :] = value

    def take(index, value):
        here = pl.ds(pl.multiple_of(rows + index * step, step), step)
        state[here, :] = state[here, :] - value

    def product(left, right, put):
        def part(index, carry):
            here = pl.ds(pl.multiple_of(index * step, step), step)
            total = None
            for (which, start, size), operand in zip(left, right):
                pair = e_ref[which, 0, here, start : start + size], e_ref[which, 1, here, start : start + size]
                term = three_dot(pair, operand)
                total = term if total is None else total + term
            put(index, total)
            return carry

        lax.fori_loop(0, 3, part, 0)

    half, link = rows // 2, e_ref.shape[3] - wide
    product([(0, 0, wide)], [split_right(state[0:wide, :])], put_first)
    tail = jnp.concatenate([x_ref[half:rows, :], jnp.zeros((link - half, LANES), jnp.float32)], axis=0)
    head = x_ref[0:link, :]
    product([(1, wide, link), (0, wide, link)], [split_right(head), split_right(tail)], take)
    product([(1, 0, wide)], [split_right(state[rows : rows + wide, :])], put_second)


def place_kernel(got_ref, place_ref, *outs):
    cores, _, rows = got_ref.shape
    for core in range(cores):
        for index, out in enumerate(outs):
            out[core * rows : (core + 1) * rows, :] = lax.dot_general(
                got_ref[core],
                place_ref[:, index * LANES : (index + 1) * LANES],
                (((0,), (0,)), ((), ())),
                precision=HI,
                preferred_element_type=jnp.float32,
            )


def load_state(state, r_ref, span):
    state[0:span, :] = r_ref[...]
    state[span:, :] = jnp.zeros((state.shape[0] - span, LANES), jnp.float32)


def subtract(state, l_ref, x_ref):
    x = split_right(x_ref[...])
    cores, _, rows, _ = l_ref.shape
    step = rows // 2

    def part(index, carry):
        core, piece = index // 2, index % 2
        here = pl.ds(pl.multiple_of(piece * step, step), step)
        there = pl.ds(pl.multiple_of(index * step, step), step)
        state[there, :] = state[there, :] - three_dot((l_ref[core, 0, here, :], l_ref[core, 1, here, :]), x)
        return carry

    lax.fori_loop(0, 2 * cores, part, 0)


def pick(plane, first, first_ref, second, second_ref, to_ref):
    @pl.when(plane == first)
    def _():
        to_ref[...] = first_ref[...]

    @pl.when(plane == second)
    def _():
        to_ref[...] = second_ref[...]


def stage_kernel(rows, number, plane_ref, *refs):
    plane = plane_ref[0]
    span = 2 * rows
    e_ref, refs = refs[0], refs[1:]
    a_ref, refs = (refs[0], refs[1:]) if number in (1, 2) else (None, refs)
    b_ref, refs = (refs[0], refs[1:]) if number >= 2 else (None, refs)
    r_ref, refs = refs[0], refs[1:]
    arrived = refs[: (0, 2, 3, 2)[number]]
    outs = refs[len(arrived) : len(arrived) + (2 if number == 1 else 1)]
    state, seen = refs[len(arrived) + len(outs) :]
    x_ref = outs[-1]
    other = {1: 3, 2: 0}.get(number)
    works = plane == number if other is None else (plane == number) | (plane == other)

    @pl.when(works)
    def _():
        load_state(state, r_ref, span)
        if number in (1, 2):
            pick(plane, number, arrived[0], other, arrived[1], seen)
            if number == 2:

                @pl.when(plane == 0)
                def _():
                    state[...] = jnp.zeros_like(state)

            subtract(state, a_ref, seen)
        if number == 3:
            state[0:span, :] = state[0:span, :] + arrived[0][...]

    if number == 1:
        outs[0][...] = jnp.where(plane == 3, state[0:span, :], r_ref[...])

    @pl.when(plane == number)
    def _():
        if number >= 2:
            subtract(state, b_ref, arrived[-1])
        solve(state, e_ref, x_ref, rows)

    if number == 2:

        @pl.when(plane == 0)
        def _():
            x_ref[...] = state[0:span, :]

        @pl.when((plane == 1) | (plane == 3))
        def _():
            x_ref[...] = jnp.zeros_like(x_ref)
    else:

        @pl.when(plane != number)
        def _():
            x_ref[...] = jnp.zeros_like(x_ref)


def per_device(factor, right_side, occ_order, cabs_order):
    planes, cores = lax.axis_size("y"), lax.axis_size("core")
    plane, core = lax.axis_index("y"), lax.axis_index("core")
    pieces = lax.axis_size("x") * lax.axis_size("z")
    per, aux = factor.shape
    rows = per * pieces
    span = cores * rows
    occ_total, cabs_total = occ_order.shape[0], cabs_order.shape[0]
    cabs_local = right_side.shape[1] // occ_total
    cheap = pl.CostEstimate(flops=1000, bytes_accessed=1000, transcendentals=0)
    small = pltpu.CompilerParams(vmem_limit_bytes=8 * 1024 * 1024)
    large = pltpu.CompilerParams(vmem_limit_bytes=24 * 1024 * 1024)

    slots = occ_order.reshape(pieces, cores).T.reshape(occ_total)
    pick = (jnp.arange(cabs_local, dtype=jnp.int32)[None, :] * occ_total + slots[:, None]).reshape(-1, 1)
    spread = (pick == jnp.arange(right_side.shape[1], dtype=jnp.int32)[None, :]).astype(jnp.float32)
    sent = lax.dot_general(spread, right_side, (((1,), (1,)), ((), ())), precision=HI, preferred_element_type=jnp.float32)
    sent = sent.reshape(occ_total, cabs_local, rows)

    def flat(block):
        return jnp.pad(block.reshape(per * ltiles, LANES), ((0, lpad - per * ltiles), (0, 0)))

    ltiles = span // LANES
    lpad = (per * ltiles + 7) // 8 * 8
    moved = lax.ppermute(factor[:, span : 2 * span], "y", [(3, 0)])
    flat_a = flat(jnp.where(plane == 0, moved, factor[:, :span]))
    flat_b = flat(lax.dynamic_slice_in_dim(factor, jnp.maximum(plane - 1, 0) * span, span, 1))
    flats = jnp.concatenate([flat_a, flat_b])

    swap = [(0, 1), (1, 0)]
    x_arg = lax.axis_index("x").reshape(1).astype(jnp.int32)
    smem = pl.BlockSpec(memory_space=pltpu.SMEM)
    here = pl.BlockSpec(memory_space=pltpu.VMEM)
    zs, xs = lax.axis_size("z"), lax.axis_size("x")
    diag = lax.dynamic_slice_in_dim(factor, plane * span, span, 1)
    low, high = diag[:, :rows], diag[:, rows:]
    half = rows // 2
    gap, short = jnp.zeros((per, 640 - rows), jnp.float32), jnp.zeros((per, 384 - half), jnp.float32)
    lent = lax.ppermute(low[:, half:], "core", [(1, 0)])
    diag = jnp.where(
        core == 0,
        jnp.concatenate([low, gap, lent, short], axis=1),
        jnp.concatenate([high, gap, low[:, :half], short], axis=1),
    )
    tiles = diag.shape[1] // LANES

    def spread(part):
        copies = jnp.broadcast_to(part[None], (zs, *part.shape))
        return lax.all_to_all(copies, "z", 0, 0, tiled=True).reshape(zs * part.shape[0], LANES)

    got = lax.all_to_all(sent, ("core", "x", "z"), 0, 0, tiled=True)
    piece = diag.reshape(per * tiles, LANES)
    whole = lax.all_gather(flats, ("x", "z"), axis=0, tiled=True)
    near = spread(piece)
    ahead = [(i, (i + 1) % xs) for i in range(xs)]
    behind = [(i, (i - 1) % xs) for i in range(xs)]

    left, right = lax.ppermute(near, "x", ahead), lax.ppermute(near, "x", behind)
    def far(left, right):
        middle = left.shape[0] // 2
        return lax.ppermute(left[:middle], "x", ahead), lax.ppermute(right[middle:], "x", behind)

    far0, far1 = far(left, right)
    far0, far1, got = lax.optimization_barrier((far0, far1, got))
    got = got.reshape(cores, cabs_total, rows)
    place = (jnp.arange(cabs_total, dtype=jnp.int32)[:, None] == cabs_order[None, :]).astype(jnp.float32)
    states = list(pl.pallas_call(
        place_kernel,
        out_shape=(jax.ShapeDtypeStruct((span, LANES), jnp.float32),) * (cabs_total // LANES),
        in_specs=[here, here],
        out_specs=(here,) * (cabs_total // LANES),
        compiler_params=small,
        cost_estimate=cheap,
        name="place",
    )(got, place))
    mine = pl.pallas_call(
        functools.partial(invert_kernel, rows, xs, zs, tiles),
        out_shape=jax.ShapeDtypeStruct((rows, tiles * LANES), jnp.float32),
        in_specs=[smem] + [here] * 5,
        out_specs=here,
        scratch_shapes=[pltpu.VMEM((tiles, 640, LANES), jnp.float32), pltpu.VMEM((5, LANES, LANES), jnp.float32)],
        compiler_params=pltpu.CompilerParams(vmem_limit_bytes=12 * 1024 * 1024),
        cost_estimate=cheap,
        name="invert",
    )(x_arg, near, left, far0, far1, right)
    theirs = lax.ppermute(mine, "core", swap)
    core_arg = core.reshape(1).astype(jnp.int32)
    plane_arg = plane.reshape(1).astype(jnp.int32)
    inverse = pl.pallas_call(
        pack_kernel,
        out_shape=jax.ShapeDtypeStruct((cores, 2, rows, tiles * LANES), jnp.bfloat16),
        in_specs=[smem, here, here],
        out_specs=here,
        compiler_params=small,
        cost_estimate=cheap,
        name="pack",
    )(core_arg, mine, theirs)

    def after(value, tokens):
        value, token = lax.optimization_barrier((value, sum(token[0, :1] for token in tokens)))
        return value, (token != token).astype(jnp.int32)

    def paired(own, zero):
        other = lax.ppermute(own, "core", swap)
        return pl.pallas_call(
            pack_kernel,
            out_shape=jax.ShapeDtypeStruct((cores, 2, *own.shape), jnp.bfloat16),
            in_specs=[smem, here, here],
            out_specs=here,
            compiler_params=small,
            cost_estimate=pl.CostEstimate(flops=1_000_000, bytes_accessed=8_000_000, transcendentals=0),
            name="pack",
        )(core_arg + zero, own, other)

    def ordered(whole):
        return pl.pallas_call(
            functools.partial(order_kernel, rows, pieces, lpad, ltiles),
            out_shape=(jax.ShapeDtypeStruct((rows, span), jnp.float32),) * 2,
            in_specs=[here],
            out_specs=(here, here),
            scratch_shapes=[pltpu.VMEM((rows, LANES), jnp.float32)],
            compiler_params=small,
            cost_estimate=pl.CostEstimate(flops=1_000_000, bytes_accessed=16_000_000, transcendentals=0),
            name="order",
        )(whole)

    block = jax.ShapeDtypeStruct((span, LANES), jnp.float32)

    def stage(number, *args):
        outs = 2 if number == 1 else 1
        return pl.pallas_call(
            functools.partial(stage_kernel, rows, number),
            out_shape=(block,) * outs,
            in_specs=[smem] + [here] * len(args),
            out_specs=(here,) * outs,
            scratch_shapes=[pltpu.VMEM((span + 64, LANES), jnp.float32), pltpu.VMEM((span, LANES), jnp.float32)],
            compiler_params=small,
            cost_estimate=pl.CostEstimate(flops=30_000_000_000, bytes_accessed=4_000_000, transcendentals=0),
            name=f"stage{number}",
        )(plane_arg, *args)

    def send(value, pairs):
        return lax.ppermute(value, "y", pairs)

    x0s, chunks = [], []
    for state in states:
        x0s += stage(0, inverse, state)
    firsts = [(send(x0, [(0, 1)]), send(x0, [(0, 3)])) for x0 in x0s[:1]] + [None]
    whole, *first, x0s[-1] = lax.optimization_barrier((whole, *firsts[0], x0s[-1]))
    firsts[0] = tuple(first)
    firsts[-1] = send(x0s[-1], [(0, 1)]), send(x0s[-1], [(0, 3)])
    own_a, own_b = ordered(whole)
    a_mat = paired(own_a, 0)
    x1s, nexts, tokens = [], [], []
    for index, (state, (to1, to3)) in enumerate(zip(list(states), firsts)):
        if index > 0:
            to1, to3, token = lax.optimization_barrier((to1, to3, x1s[-1][0][:1]))
            tokens.append(token)
        to2 = send(to3, [(3, 2)])
        states[index], x1 = stage(1, inverse, a_mat, state, to1, to3)
        near_x, to0 = send(x1, [(1, 2)]), send(x1, [(1, 0)])
        x1s.append((x1, to2))
        nexts.append((near_x, to0))
    _, zero = after(core_arg, [x1 for x1, _ in x1s] + tokens)
    b_mat = paired(own_b, zero)
    for state, x0, (x1, to2), (near_x, to0) in zip(states, x0s, x1s, nexts):
        (x2,) = stage(2, inverse, a_mat, b_mat, state, to2, to0, near_x)
        part = send(x2, [(0, 3)])
        near_x = send(x2, [(2, 3)])
        (x3,) = stage(3, inverse, b_mat, state, part, near_x)
        chunks.append(jnp.where(plane == 0, x0, jnp.where(plane == 1, x1, jnp.where(plane == 2, x2, x3))))
    solved = jnp.concatenate([x.T for x in chunks], axis=0)
    keep = jnp.where(core == 0, solved[:, :rows], solved[:, rows:])
    give = jnp.where(core == 0, solved[:, rows:], solved[:, :rows])
    came = lax.ppermute(give, "core", [(0, 1), (1, 0)])
    return jnp.where(core == 0, jnp.stack([keep, came]), jnp.stack([came, keep]))


def solution(mesh):
    grid = Mesh(mesh.devices.reshape(4, 2, 4, 8), ("y", "core", "x", "z"))
    in_specs = (P(("y", "core", "x", "z"), None), P(("y", "core"), ("x", "z")), P(), P())
    out_specs = P(("x", "z"), None, ("y", "core"))
    return jax.shard_map(per_device, mesh=grid, in_specs=in_specs, out_specs=out_specs, check_vma=False)
```

```python
import functools
import jax
import jax.numpy as jnp
from jax import lax
from jax.experimental import pallas as pl
from jax.experimental.pallas import tpu as pltpu
from jax.sharding import Mesh, PartitionSpec as P

HI = lax.Precision.HIGHEST
LANES = 128


def halves(value):
    high = value.astype(jnp.bfloat16)
    return high, (value - high.astype(jnp.float32)).astype(jnp.bfloat16)


def split_right(value):
    high, low = halves(value)
    return jnp.concatenate([high, low], axis=1), high


def three_dot(left, right):
    lh, ll = left
    both, rh = right
    dot = functools.partial(jnp.dot, preferred_element_type=jnp.float32)
    wide = dot(lh, both)
    return wide[:, :LANES] + (wide[:, LANES:] + dot(ll, rh))


def full_dot(left, right):
    return three_dot(halves(left), split_right(right))


def invert_kernel(rows, groups, pieces, tiles, x_ref, own_ref, left_ref, far0_ref, far1_ref, right_ref, o_ref, a_ref, m_ref):
    per = rows // (groups * pieces)
    wide = 640
    blocks = wide // LANES
    x = x_ref[0]
    half = pieces // 2
    for ref, back, first, count in (
        (own_ref, 0, 0, pieces),
        (left_ref, 1, 0, pieces),
        (far0_ref, 2, 0, half),
        (far1_ref, 2, half, half),
        (right_ref, 3, 0, pieces),
    ):
        base = (lax.rem(x + groups - back, groups) * pieces + first) * per
        for tile in range(tiles):
            for row in range(per):
                a_ref[tile, pl.ds(base + row, count, stride=per), :] = ref[
                    pl.ds(row * tiles + tile, count, stride=per * tiles), :
                ]
    extra = wide - rows
    r0 = lax.broadcasted_iota(jnp.int32, (extra, LANES), 0)
    c0 = lax.broadcasted_iota(jnp.int32, (extra, LANES), 1)
    for tile in range(blocks - 1):
        a_ref[tile, rows:wide, :] = jnp.zeros((extra, LANES), jnp.float32)
    a_ref[blocks - 1, rows:wide, :] = jnp.where(c0 == r0 + (LANES - extra), 1.0, 0.0)
    ri = lax.broadcasted_iota(jnp.int32, (LANES, LANES), 0)
    ci = lax.broadcasted_iota(jnp.int32, (LANES, LANES), 1)

    def block(i, j):
        return a_ref[j, i * LANES : (i + 1) * LANES, :]

    for i in range(blocks):
        m_ref[i] = jnp.where(ri == ci, 1.0 / jnp.where(ri == ci, block(i, i), 1.0), 0.0)

    def double(level, carry):
        rb, cb = ri >> level, ci >> level
        take = (rb >> 1 == cb >> 1) & (rb == cb + 1)
        mids = [full_dot(jnp.where(take, block(i, i), 0.0), m_ref[i]) for i in range(blocks)]
        news = [m_ref[i] - full_dot(m_ref[i], mids[i]) for i in range(blocks)]
        for i in range(blocks):
            m_ref[i] = news[i]
        return carry

    lax.fori_loop(0, 7, double, 0)
    inv = [m_ref[i] for i in range(blocks)]
    for i in range(blocks):
        for j in range(blocks):
            last = min((i + 1) * LANES, rows)
            if j > i:
                o_ref[i * LANES : last, j * LANES : (j + 1) * LANES] = jnp.zeros((last - i * LANES, LANES), jnp.float32)
    done = [[None] * blocks for _ in range(blocks)]
    for i in range(blocks):
        done[i][i] = inv[i]
        last = min((i + 1) * LANES, rows)
        for j in range(i):
            total = full_dot(block(i, j), done[j][j])
            for k in range(j + 1, i):
                total = total + full_dot(block(i, k), done[k][j])
            done[i][j] = -full_dot(inv[i], total)
        for j in range(i + 1):
            o_ref[i * LANES : last, j * LANES : (j + 1) * LANES] = done[i][j][: last - i * LANES]
    for tile in range(blocks, tiles):
        o_ref[:, tile * LANES : (tile + 1) * LANES] = a_ref[tile, :rows, :]


def order_kernel(rows, pieces, pad_rows, tiles, whole_ref, *refs):
    per = rows // pieces
    outs, s_ref = refs[:-1], refs[-1]
    for block, out in enumerate(outs):
        for tile in range(tiles):

            def move(row, carry, block=block, tile=tile):
                s_ref[pl.ds(row, pieces, stride=per), :] = whole_ref[
                    pl.ds(block * pad_rows + row * tiles + tile, pieces, stride=len(outs) * pad_rows), :
                ]
                return carry

            lax.fori_loop(0, per, move, 0, unroll=6)
            out[:, tile * LANES : (tile + 1) * LANES] = s_ref[...]


def pack_kernel(core_ref, own_ref, other_ref, o_ref):
    core = core_ref[0]
    rows = own_ref.shape[0]
    for start in range(0, rows, 192):
        here = slice(start, start + 192)
        high, low = halves(own_ref[here, :])
        o_ref[core, 0, here, :] = high
        o_ref[core, 1, here, :] = low
        high, low = halves(other_ref[here, :])
        o_ref[1 - core, 0, here, :] = high
        o_ref[1 - core, 1, here, :] = low


def solve(state, e_ref, x_ref, rows):
    wide = 640
    step = rows // 3

    def put_first(index, value):
        x_ref[pl.ds(pl.multiple_of(index * step, step), step), :] = value

    def put_second(index, value):
        x_ref[pl.ds(pl.multiple_of(rows + index * step, step), step), :] = value

    def take(index, value):
        here = pl.ds(pl.multiple_of(rows + index * step, step), step)
        state[here, :] = state[here, :] - value

    def product(left, right, put):
        def part(index, carry):
            here = pl.ds(pl.multiple_of(index * step, step), step)
            total = None
            for (which, start, size), operand in zip(left, right):
                pair = e_ref[which, 0, here, start : start + size], e_ref[which, 1, here, start : start + size]
                term = three_dot(pair, operand)
                total = term if total is None else total + term
            put(index, total)
            return carry

        lax.fori_loop(0, 3, part, 0)

    half, link = rows // 2, e_ref.shape[3] - wide
    product([(0, 0, wide)], [split_right(state[0:wide, :])], put_first)
    tail = jnp.concatenate([x_ref[half:rows, :], jnp.zeros((link - half, LANES), jnp.float32)], axis=0)
    head = x_ref[0:link, :]
    product([(1, wide, link), (0, wide, link)], [split_right(head), split_right(tail)], take)
    product([(1, 0, wide)], [split_right(state[rows : rows + wide, :])], put_second)


def place_kernel(got_ref, place_ref, *outs):
    cores, _, rows = got_ref.shape
    for core in range(cores):
        for index, out in enumerate(outs):
            out[core * rows : (core + 1) * rows, :] = lax.dot_general(
                got_ref[core],
                place_ref[:, index * LANES : (index + 1) * LANES],
                (((0,), (0,)), ((), ())),
                precision=HI,
                preferred_element_type=jnp.float32,
            )


def load_state(state, r_ref, span):
    state[0:span, :] = r_ref[...]
    state[span:, :] = jnp.zeros((state.shape[0] - span, LANES), jnp.float32)


def subtract(state, l_ref, x_ref):
    x = split_right(x_ref[...])
    cores, _, rows, _ = l_ref.shape
    step = rows // 2

    def part(index, carry):
        core, piece = index // 2, index % 2
        here = pl.ds(pl.multiple_of(piece * step, step), step)
        there = pl.ds(pl.multiple_of(index * step, step), step)
        state[there, :] = state[there, :] - three_dot((l_ref[core, 0, here, :], l_ref[core, 1, here, :]), x)
        return carry

    lax.fori_loop(0, 2 * cores, part, 0)


def pick(plane, first, first_ref, second, second_ref, to_ref):
    @pl.when(plane == first)
    def _():
        to_ref[...] = first_ref[...]

    @pl.when(plane == second)
    def _():
        to_ref[...] = second_ref[...]


def early_kernel(plane_ref, a_ref, r_ref, seen_ref, out_ref):
    out_ref[...] = r_ref[...]

    @pl.when(plane_ref[0] == 2)
    def _():
        subtract(out_ref, a_ref, seen_ref)


def stage_kernel(rows, number, plane_ref, *refs):
    plane = plane_ref[0]
    span = 2 * rows
    e_ref, refs = refs[0], refs[1:]
    a_ref, refs = (refs[0], refs[1:]) if number in (1, 2) else (None, refs)
    b_ref, refs = (refs[0], refs[1:]) if number >= 2 else (None, refs)
    r_ref, refs = refs[0], refs[1:]
    arrived = refs[: (0, 2, 3, 2)[number]]
    outs = refs[len(arrived) : len(arrived) + (2 if number == 1 else 1)]
    state, seen = refs[len(arrived) + len(outs) :]
    x_ref = outs[-1]
    other = {1: 3, 2: 0}.get(number)
    works = plane == number if other is None else (plane == number) | (plane == other)

    @pl.when(works)
    def _():
        load_state(state, r_ref, span)
        if number in (1, 2):
            pick(plane, number, arrived[0], other, arrived[1], seen)
            if number == 2:

                @pl.when(plane == 0)
                def _():
                    state[...] = jnp.zeros_like(state)

            if number == 1:
                subtract(state, a_ref, seen)
            else:

                @pl.when(plane == 0)
                def _():
                    subtract(state, a_ref, seen)

        if number == 3:
            state[0:span, :] = state[0:span, :] + arrived[0][...]

    if number == 1:
        outs[0][...] = jnp.where(plane == 3, state[0:span, :], r_ref[...])

    @pl.when(plane == number)
    def _():
        if number >= 2:
            subtract(state, b_ref, arrived[-1])
        solve(state, e_ref, x_ref, rows)

    if number == 2:

        @pl.when(plane == 0)
        def _():
            x_ref[...] = state[0:span, :]

        @pl.when((plane == 1) | (plane == 3))
        def _():
            x_ref[...] = jnp.zeros_like(x_ref)
    else:

        @pl.when(plane != number)
        def _():
            x_ref[...] = jnp.zeros_like(x_ref)


def per_device(factor, right_side, occ_order, cabs_order):
    planes, cores = lax.axis_size("y"), lax.axis_size("core")
    plane, core = lax.axis_index("y"), lax.axis_index("core")
    pieces = lax.axis_size("x") * lax.axis_size("z")
    per, aux = factor.shape
    rows = per * pieces
    span = cores * rows
    occ_total, cabs_total = occ_order.shape[0], cabs_order.shape[0]
    cabs_local = right_side.shape[1] // occ_total
    cheap = pl.CostEstimate(flops=1000, bytes_accessed=1000, transcendentals=0)
    small = pltpu.CompilerParams(vmem_limit_bytes=8 * 1024 * 1024)
    large = pltpu.CompilerParams(vmem_limit_bytes=24 * 1024 * 1024)

    slots = occ_order.reshape(pieces, cores).T.reshape(occ_total)
    pick = (jnp.arange(cabs_local, dtype=jnp.int32)[None, :] * occ_total + slots[:, None]).reshape(-1, 1)
    spread = (pick == jnp.arange(right_side.shape[1], dtype=jnp.int32)[None, :]).astype(jnp.float32)
    sent = lax.dot_general(spread, right_side, (((1,), (1,)), ((), ())), precision=HI, preferred_element_type=jnp.float32)
    sent = sent.reshape(occ_total, cabs_local, rows)

    def flat(block):
        return jnp.pad(block.reshape(per * ltiles, LANES), ((0, lpad - per * ltiles), (0, 0)))

    ltiles = span // LANES
    lpad = (per * ltiles + 7) // 8 * 8
    moved = lax.ppermute(factor[:, span : 2 * span], "y", [(3, 0)])
    flat_a = flat(jnp.where(plane == 0, moved, factor[:, :span]))
    flat_b = flat(lax.dynamic_slice_in_dim(factor, jnp.maximum(plane - 1, 0) * span, span, 1))
    flats = jnp.concatenate([flat_a, flat_b])

    swap = [(0, 1), (1, 0)]
    x_arg = lax.axis_index("x").reshape(1).astype(jnp.int32)
    smem = pl.BlockSpec(memory_space=pltpu.SMEM)
    here = pl.BlockSpec(memory_space=pltpu.VMEM)
    zs, xs = lax.axis_size("z"), lax.axis_size("x")
    diag = lax.dynamic_slice_in_dim(factor, plane * span, span, 1)
    low, high = diag[:, :rows], diag[:, rows:]
    half = rows // 2
    gap, short = jnp.zeros((per, 640 - rows), jnp.float32), jnp.zeros((per, 384 - half), jnp.float32)
    lent = lax.ppermute(low[:, half:], "core", [(1, 0)])
    diag = jnp.where(
        core == 0,
        jnp.concatenate([low, gap, lent, short], axis=1),
        jnp.concatenate([high, gap, low[:, :half], short], axis=1),
    )
    tiles = diag.shape[1] // LANES

    def spread(part):
        copies = jnp.broadcast_to(part[None], (zs, *part.shape))
        return lax.all_to_all(copies, "z", 0, 0, tiled=True).reshape(zs * part.shape[0], LANES)

    got = lax.all_to_all(sent, ("core", "x", "z"), 0, 0, tiled=True)
    piece = diag.reshape(per * tiles, LANES)
    whole = lax.all_gather(flats, ("x", "z"), axis=0, tiled=True)
    near = spread(piece)
    ahead = [(i, (i + 1) % xs) for i in range(xs)]
    behind = [(i, (i - 1) % xs) for i in range(xs)]

    left, right = lax.ppermute(near, "x", ahead), lax.ppermute(near, "x", behind)
    def far(left, right):
        middle = left.shape[0] // 2
        return lax.ppermute(left[:middle], "x", ahead), lax.ppermute(right[middle:], "x", behind)

    far0, far1 = far(left, right)
    far0, far1, got = lax.optimization_barrier((far0, far1, got))
    got = got.reshape(cores, cabs_total, rows)
    place = (jnp.arange(cabs_total, dtype=jnp.int32)[:, None] == cabs_order[None, :]).astype(jnp.float32)
    states = list(pl.pallas_call(
        place_kernel,
        out_shape=(jax.ShapeDtypeStruct((span, LANES), jnp.float32),) * (cabs_total // LANES),
        in_specs=[here, here],
        out_specs=(here,) * (cabs_total // LANES),
        compiler_params=small,
        cost_estimate=cheap,
        name="place",
    )(got, place))
    mine = pl.pallas_call(
        functools.partial(invert_kernel, rows, xs, zs, tiles),
        out_shape=jax.ShapeDtypeStruct((rows, tiles * LANES), jnp.float32),
        in_specs=[smem] + [here] * 5,
        out_specs=here,
        scratch_shapes=[pltpu.VMEM((tiles, 640, LANES), jnp.float32), pltpu.VMEM((5, LANES, LANES), jnp.float32)],
        compiler_params=pltpu.CompilerParams(vmem_limit_bytes=12 * 1024 * 1024),
        cost_estimate=cheap,
        name="invert",
    )(x_arg, near, left, far0, far1, right)
    theirs = lax.ppermute(mine, "core", swap)
    core_arg = core.reshape(1).astype(jnp.int32)
    plane_arg = plane.reshape(1).astype(jnp.int32)
    inverse = pl.pallas_call(
        pack_kernel,
        out_shape=jax.ShapeDtypeStruct((cores, 2, rows, tiles * LANES), jnp.bfloat16),
        in_specs=[smem, here, here],
        out_specs=here,
        compiler_params=small,
        cost_estimate=cheap,
        name="pack",
    )(core_arg, mine, theirs)

    def after(value, tokens):
        value, token = lax.optimization_barrier((value, sum(token[0, :1] for token in tokens)))
        return value, (token != token).astype(jnp.int32)

    def paired(own, zero):
        other = lax.ppermute(own, "core", swap)
        return pl.pallas_call(
            pack_kernel,
            out_shape=jax.ShapeDtypeStruct((cores, 2, *own.shape), jnp.bfloat16),
            in_specs=[smem, here, here],
            out_specs=here,
            compiler_params=small,
            cost_estimate=pl.CostEstimate(flops=1_000_000, bytes_accessed=8_000_000, transcendentals=0),
            name="pack",
        )(core_arg + zero, own, other)

    def ordered(whole):
        return pl.pallas_call(
            functools.partial(order_kernel, rows, pieces, lpad, ltiles),
            out_shape=(jax.ShapeDtypeStruct((rows, span), jnp.float32),) * 2,
            in_specs=[here],
            out_specs=(here, here),
            scratch_shapes=[pltpu.VMEM((rows, LANES), jnp.float32)],
            compiler_params=small,
            cost_estimate=pl.CostEstimate(flops=1_000_000, bytes_accessed=16_000_000, transcendentals=0),
            name="order",
        )(whole)

    block = jax.ShapeDtypeStruct((span, LANES), jnp.float32)

    def stage(number, *args):
        outs = 2 if number == 1 else 1
        return pl.pallas_call(
            functools.partial(stage_kernel, rows, number),
            out_shape=(block,) * outs,
            in_specs=[smem] + [here] * len(args),
            out_specs=(here,) * outs,
            scratch_shapes=[pltpu.VMEM((span + 64, LANES), jnp.float32), pltpu.VMEM((span, LANES), jnp.float32)],
            compiler_params=small,
            cost_estimate=pl.CostEstimate(flops=30_000_000_000, bytes_accessed=4_000_000, transcendentals=0),
            name=f"stage{number}",
        )(plane_arg, *args)

    def send(value, pairs):
        return lax.ppermute(value, "y", pairs)

    x0s, chunks = [], []
    for state in states:
        x0s += stage(0, inverse, state)
    firsts = [(send(x0, [(0, 1)]), send(x0, [(0, 3)])) for x0 in x0s[:1]] + [None]
    whole, *first, x0s[-1] = lax.optimization_barrier((whole, *firsts[0], x0s[-1]))
    firsts[0] = tuple(first)
    firsts[-1] = send(x0s[-1], [(0, 1)]), send(x0s[-1], [(0, 3)])
    own_a, own_b = ordered(whole)
    a_mat = paired(own_a, 0)
    x1s, nexts, tokens = [], [], []
    for index, (state, (to1, to3)) in enumerate(zip(list(states), firsts)):
        if index > 0:
            to1, to3, token = lax.optimization_barrier((to1, to3, x1s[-1][0][:1]))
            tokens.append(token)
        to2 = send(to3, [(3, 2)])
        states[index], x1 = stage(1, inverse, a_mat, state, to1, to3)
        near_x, to0 = send(x1, [(1, 2)]), send(x1, [(1, 0)])
        x1s.append((x1, to2))
        nexts.append((near_x, to0))
    _, zero = after(core_arg, [x1 for x1, _ in x1s] + tokens)
    b_mat = paired(own_b, zero)
    for state, x0, (x1, to2), (near_x, to0) in zip(states, x0s, x1s, nexts):
        state = pl.pallas_call(
            early_kernel,
            out_shape=block,
            in_specs=[smem, here, here, here],
            out_specs=here,
            compiler_params=small,
            cost_estimate=cheap,
            name="early",
        )(plane_arg, a_mat, state, to2)
        (x2,) = stage(2, inverse, a_mat, b_mat, state, to2, to0, near_x)
        part = send(x2, [(0, 3)])
        near_x = send(x2, [(2, 3)])
        (x3,) = stage(3, inverse, b_mat, state, part, near_x)
        chunks.append(jnp.where(plane == 0, x0, jnp.where(plane == 1, x1, jnp.where(plane == 2, x2, x3))))
    solved = jnp.concatenate([x.T for x in chunks], axis=0)
    keep = jnp.where(core == 0, solved[:, :rows], solved[:, rows:])
    give = jnp.where(core == 0, solved[:, rows:], solved[:, :rows])
    came = lax.ppermute(give, "core", [(0, 1), (1, 0)])
    return jnp.where(core == 0, jnp.stack([keep, came]), jnp.stack([came, keep]))


def solution(mesh):
    grid = Mesh(mesh.devices.reshape(4, 2, 4, 8), ("y", "core", "x", "z"))
    in_specs = (P(("y", "core", "x", "z"), None), P(("y", "core"), ("x", "z")), P(), P())
    out_specs = P(("x", "z"), None, ("y", "core"))
    return jax.shard_map(per_device, mesh=grid, in_specs=in_specs, out_specs=out_specs, check_vma=False)
```
